128 devices in a mesh: dp: 4 (over x), seq: 32 (over y, z, core).
Axes of the slice: x: 4, y: 4, z: 4, core: 2. Of those that a mesh axis runs over, the one named last changes fastest.
Arguments:
- hidden: bfloat16 [8, 6144, 3072], P('dp', 'seq'), may hold values from -6 to 6
- cotangent: bfloat16 [8, 6144, 1536], P('dp', 'seq'), may hold values from -6 to 6
- lengths: int32 [8], P('dp'), may hold values from 768 to 6144, as said below
- kernel: float32 [1536, 31], replicated, may hold values from -1 to 1
- conv_gain: float32 [1536], replicated, may hold values from 0.1 to 1.9
- w_out: bfloat16 [1536, 1536], replicated, may hold values from -0.15625 to 0.15625
Outputs:
- grad_hidden: bfloat16 [8, 6144, 3072], P('dp', 'seq')
- grad_w_out: float32 [1536, 1536], P(('dp', 'seq'))
- grad_kernel: float32 [1536, 31], P(('dp', 'seq'))
- grad_conv_gain: float32 [1536], P(('dp', 'seq'))
The draws below stay inside these ranges and needn't reach their ends.
Inputs may be any that keep to these rules, and one draw needn't show every extreme that they name: `lengths`: the first utterance of every group of 2 on one index of dp fills all 6144 frames.
All inputs are finite; a program needn't handle non-finite values.
Results may differ from the reference program's by a relative error of at most 0.0055.
Values may be sent and summed in bfloat16 or wider, within the bound.
No kernel may reach another device: no remote copies, remote signals or barrier semaphores. Data moves between devices by JAX's collectives and lax.ppermute only.
A program may use at most 128 MiB of HBM per device.

```python
import math
import jax
import jax.numpy as jnp
from jax import lax

D = 1536
KW = 31
UTT = 2
BATCH = 8
LEN = 6144


def draw_lengths(key, part):
    drawn = jax.random.randint(key, (BATCH,), LEN // 8, LEN + 1, dtype=jnp.int32)
    leading = jnp.arange(BATCH, dtype=jnp.int32) % UTT == 0
    return jnp.where(leading, jnp.int32(LEN), drawn).astype(jnp.int32)


def strengthened(values, rng, source, target, shards_of, factor):
    def block_of(dim):
        return (jnp.arange(values.shape[dim]) // (values.shape[dim] // shards_of)).reshape((-1,) + (1,) * (values.ndim - 1 - dim))

    first = jax.random.permutation(rng, shards_of)[block_of(target)]
    far = (block_of(target) + shards_of // 2) % shards_of
    return jnp.where((block_of(source) == first) | (block_of(source) == far), factor * values, values)


def steps_of(own_key, extent, cuts, least, largest):
    gain, own = 1.0, jax.random.fold_in(own_key, 6)
    for position, parts in cuts:
        draws = jnp.exp(jax.random.uniform(jax.random.fold_in(own, position), (parts,), jnp.float32, least / len(cuts), largest / len(cuts)))
        gain = gain * jnp.repeat(draws, extent[position] // parts).reshape([-1 if axis == position else 1 for axis in range(len(extent))])
    return gain


def noise(rng, shape, spread, limit, split=(), kind=jnp.bfloat16):
    loudness = steps_of(rng, shape, split, -0.22, 0.18) if split else 1.0
    values = jax.random.normal(rng, shape, jnp.float32) * spread * loudness
    return jnp.minimum(jnp.maximum(values, -limit), limit).astype(kind)


def gaussian_with(own_key, extent, deviation, reach, cuts, heavy, kind=jnp.bfloat16):
    result = deviation * jax.random.normal(own_key, extent, jnp.float32)
    if cuts:
        result = result * steps_of(own_key, extent, cuts, -0.22, 0.18)
    return jnp.clip(strengthened(result, jax.random.fold_in(own_key, 3), *heavy), -reach, reach).astype(kind)


def setup_inputs(seed: int = 0) -> dict:
    keys = jax.random.split(jax.random.key(seed), 7)
    hidden = gaussian_with(keys[0], (BATCH, LEN, 2 * D), 1.0, 6.0, ((0, 4), (1, 32)), (1, 2, 32, 2.75))
    cotangent = noise(keys[1], (BATCH, LEN, D), 1.0, 6.0, ((0, 4), (1, 32)))
    lengths = draw_lengths(jax.random.fold_in(keys[6], 71), 0)
    kernel = noise(keys[3], (D, KW), KW ** -0.5, 1.0, (), jnp.float32)
    conv_gain = jnp.clip(1.0 + 0.18 * jax.random.normal(keys[4], (D,), jnp.float32), 0.1, 1.9)
    w_out = noise(keys[5], (D, D), D ** -0.5, 0.15625)
    return {"hidden": hidden, "cotangent": cotangent, "lengths": lengths, "kernel": kernel, "conv_gain": conv_gain, "w_out": w_out}


EPSILON = 1e-05

def normalize(values):
    centered = values - lax.optimization_barrier(jnp.mean(values, axis=-1, keepdims=True))
    inverse = lax.rsqrt(lax.optimization_barrier(jnp.mean(centered * centered, axis=-1, keepdims=True)) + EPSILON)
    return (centered * inverse, inverse)

def norm_backward(grad_hat, normed, inverse):
    return inverse * (grad_hat - lax.optimization_barrier(jnp.mean(grad_hat, axis=-1, keepdims=True)) - normed * lax.optimization_barrier(jnp.mean(grad_hat * normed, axis=-1, keepdims=True)))

def reference(hidden, cotangent, lengths, kernel, conv_gain, w_out):
    half_width = KW // 2

    def one_utterance(totals, pieces):
        sample, upstream, length = pieces
        valid_rows = (jnp.arange(LEN, dtype=jnp.int32) < length).astype(jnp.float32)[:, None]
        hidden_float = sample.astype(jnp.float32)
        linear = hidden_float[:, :D]
        gate_open = jax.nn.sigmoid(hidden_float[:, D:])
        glu_out = (linear * gate_open * valid_rows).astype(jnp.bfloat16)
        padded = jnp.pad(glu_out.astype(jnp.float32), ((half_width, half_width), (0, 0)))
        conv_out = padded[0:LEN] * kernel[:, 0]
        for offset in range(1, KW):
            conv_out = conv_out + padded[offset:offset + LEN] * kernel[:, offset]
        conv_hat, conv_inverse = normalize(conv_out)
        pre_act = conv_hat * conv_gain
        act_gate = jax.nn.sigmoid(pre_act)
        swished = (pre_act * act_gate).astype(jnp.bfloat16)
        grad_out = upstream * valid_rows.astype(jnp.bfloat16)
        term_out = jnp.dot(swished.T, grad_out, preferred_element_type=jnp.float32)
        grad_swish = jnp.dot(grad_out, w_out.T, preferred_element_type=jnp.float32)
        grad_pre = grad_swish * act_gate * (1.0 + pre_act * (1.0 - act_gate))
        term_conv = lax.optimization_barrier(jnp.sum(grad_pre * conv_hat, axis=0))
        grad_rounded = lax.optimization_barrier(norm_backward(grad_pre * conv_gain, conv_hat, conv_inverse).astype(jnp.bfloat16))
        grad_conv = grad_rounded.astype(jnp.float32)
        grad_padded = jnp.pad(grad_conv, ((half_width, half_width), (0, 0)))
        last_tap = KW - 1
        grad_glu = grad_padded[last_tap:last_tap + LEN] * kernel[:, 0]
        for offset in range(1, KW):
            grad_glu = grad_glu + grad_padded[last_tap - offset:last_tap - offset + LEN] * kernel[:, offset]
        term_kernel = jnp.stack([lax.optimization_barrier(jnp.sum(grad_conv * padded[offset:offset + LEN], axis=0)) for offset in range(KW)], axis=1)
        grad_glu = grad_glu * valid_rows
        grad_sample = jnp.concatenate([grad_glu * gate_open, grad_glu * linear * gate_open * (1.0 - gate_open)], axis=1).astype(jnp.bfloat16)
        terms = (term_out, term_kernel, term_conv)
        return (tuple((old + new for old, new in zip(totals, terms))), grad_sample)
    start_totals = (jnp.zeros((D, D), jnp.float32), jnp.zeros((D, KW), jnp.float32), jnp.zeros((D,), jnp.float32))
    totals, grad_hidden = lax.scan(one_utterance, start_totals, (hidden, cotangent, lengths))
    factor = 1.0 / math.sqrt(BATCH * LEN)
    return (grad_hidden, totals[0] * factor, totals[1] * factor, totals[2] * factor)
```

```python
import math

import jax
import jax.numpy as jnp
from jax import lax
from jax.sharding import PartitionSpec as P

EPSILON = 1e-05
AXES = ("dp", "seq")


def inner_rows(left_side, right_side):
    return lax.dot_general(
        left_side, right_side, (((0,), (0,)), ((), ())), preferred_element_type=jnp.float32
    )


def outer_cols(left_side, right_side):
    return lax.dot_general(
        left_side, right_side, (((1,), (1,)), ((), ())), preferred_element_type=jnp.float32
    )


def extended(cells, width):
    count = lax.axis_size("seq")
    ends = count - 1
    frames = cells.shape[1]
    head = cells[:, :width]
    tail = cells[:, frames - width :]
    return jnp.concatenate(
        [
            lax.ppermute(tail, "seq", [(i, i + 1) for i in range(ends)]),
            cells,
            lax.ppermute(head, "seq", [(i + 1, i) for i in range(ends)]),
        ],
        axis=1,
    )


def normalize(values):
    centered = values - jnp.mean(values, axis=-1, keepdims=True)
    inverse = lax.rsqrt(jnp.mean(centered * centered, axis=-1, keepdims=True) + EPSILON)
    return (centered * inverse, inverse)


def norm_backward(grad_hat, normed, inverse):
    return inverse * (
        grad_hat
        - jnp.mean(grad_hat, axis=-1, keepdims=True)
        - normed * jnp.mean(grad_hat * normed, axis=-1, keepdims=True)
    )


def local(hidden, cotangent, lengths, kernel, conv_gain, w_out):
    groups, frames, double_width = hidden.shape
    width = double_width // 2
    half = width // 2
    taps = kernel.shape[1]
    reach = taps // 2
    seq_count = lax.axis_size("seq")
    devices = lax.axis_size("dp") * seq_count
    own = width // devices
    rows = groups * frames
    swap = [(i, i ^ 1) for i in range(seq_count)]
    core = lax.axis_index("seq") % 2

    positions = lax.axis_index("seq") * frames + jnp.arange(frames, dtype=jnp.int32)
    valid = (positions[None, :] < lengths[:, None]).astype(jnp.float32)
    valid_rows = valid.reshape(rows, 1)

    grad_out = (cotangent * valid.astype(jnp.bfloat16)[:, :, None]).reshape(rows, width)
    low, high = grad_out[:, :half], grad_out[:, half:]
    mine = jnp.where(core == 0, low, high)
    other = lax.ppermute(jnp.where(core == 0, high, low), "seq", swap)

    hidden_rows = hidden.reshape(rows, double_width).astype(jnp.float32)
    linear = hidden_rows[:, :width]
    gate_open = jax.nn.sigmoid(hidden_rows[:, width:])
    glu = (linear * gate_open * valid_rows).astype(jnp.bfloat16)
    padded = extended(glu.reshape(groups, frames, width), reach).astype(jnp.float32)
    conv_out = padded[:, 0:frames] * kernel[:, 0]
    for j in range(1, taps):
        conv_out = conv_out + padded[:, j : j + frames] * kernel[:, j]
    conv_hat, inverse = normalize(conv_out.reshape(rows, width))
    pre_act = conv_hat * conv_gain
    act_gate = jax.nn.sigmoid(pre_act)
    swished = (pre_act * act_gate).astype(jnp.bfloat16)

    far = lax.ppermute(swished, "seq", swap)
    term_out = inner_rows(
        jnp.concatenate([swished, far], axis=0), jnp.concatenate([mine, other], axis=0)
    )
    blocks = half // 128
    pieces = (
        term_out.astype(jnp.bfloat16)
        .reshape(devices, own, blocks, 128)
        .transpose(0, 2, 1, 3)
        .reshape(devices, blocks * own, 128)
    )
    got = lax.all_to_all(pieces, AXES, 0, 0, tiled=True)

    grad_swish = outer_cols(grad_out, w_out)
    grad_pre = grad_swish * act_gate * (1.0 + pre_act * (1.0 - act_gate))
    term_conv = jnp.sum(grad_pre * conv_hat, axis=0)
    grad_conv = norm_backward(grad_pre * conv_gain, conv_hat, inverse).astype(jnp.bfloat16)
    grad_block = grad_conv.reshape(groups, frames, width)
    grad_float = grad_block.astype(jnp.float32)
    terms = jnp.stack(
        [jnp.sum(grad_float * padded[:, j : j + frames], axis=(0, 1)) for j in range(taps)]
        + [term_conv]
    )
    small = terms.T.reshape(devices, own * (taps + 1) // 128, 128)
    got_small = lax.all_to_all(small, AXES, 0, 0, tiled=True)

    grad_padded = extended(grad_block, reach).astype(jnp.float32)
    last = taps - 1
    grad_glu = grad_padded[:, last : last + frames] * kernel[:, 0]
    for j in range(1, taps):
        grad_glu = grad_glu + grad_padded[:, last - j : last - j + frames] * kernel[:, j]
    grad_glu = grad_glu.reshape(rows, width) * valid_rows
    grad_hidden = jnp.concatenate(
        [grad_glu * gate_open, grad_glu * linear * gate_open * (1.0 - gate_open)], axis=1
    ).astype(jnp.bfloat16)

    factor = 1.0 / math.sqrt(groups * lax.axis_size("dp") * frames * seq_count)
    summed = jnp.sum(
        got.reshape(devices // 2, 2, blocks, own, 128).astype(jnp.float32), axis=0
    )
    grad_w = summed.transpose(2, 0, 1, 3).reshape(own, width) * factor
    summed_small = jnp.sum(got_small, axis=0).reshape(own, taps + 1) * factor
    return (
        grad_hidden.reshape(groups, frames, double_width),
        grad_w,
        summed_small[:, :taps],
        summed_small[:, taps],
    )


def solution(mesh):
    in_specs = (P("dp", "seq", None), P("dp", "seq", None), P("dp"), P(), P(), P())
    out_specs = (P("dp", "seq", None), P(AXES, None), P(AXES, None), P(AXES))
    return jax.shard_map(local, mesh=mesh, in_specs=in_specs, out_specs=out_specs, check_vma=False)
```

```python
import functools
import math

import jax
import jax.numpy as jnp
from jax import lax
from jax.experimental import pallas as pl
from jax.experimental.pallas import tpu as pltpu
from jax.sharding import PartitionSpec as P

EPSILON = 1e-05
AXES = ("dp", "seq")
LANES = 128
PAD = 16
F32, BF16 = jnp.float32, jnp.bfloat16


def sigmoid(x):
    return 0.5 * jnp.tanh(0.5 * x) + 0.5


def depthwise(slab, weight, start, rows, order):
    total = None
    for j, row in enumerate(order):
        term = slab[pl.ds(start + 1 + j, rows), :] * weight[row]
        total = term if total is None else total + term
    return total


def forward_kernel(limit, hidden, left, right, weights, gain, slab, hat, inverse, swished, conv):
    taps = weights.shape[0] - 1
    frames, double = hidden.shape[1:]
    width = double // 2
    blocks = width // LANES
    u = pl.program_id(0)
    rows = lax.broadcasted_iota(jnp.int32, (frames, LANES), 0)
    keep = rows < limit[u]

    def channel(cb, _):
        here = pl.ds(pl.multiple_of(cb * LANES, LANES), LANES)
        there = pl.ds(pl.multiple_of(width + cb * LANES, LANES), LANES)
        linear = hidden[0, :, here].astype(F32)
        gate = sigmoid(hidden[0, :, there].astype(F32))
        glu = jnp.where(keep, linear * gate, 0.0).astype(BF16).astype(F32)
        block = slab.at[0, cb]
        block[0:PAD, :] = left[0, :, here].astype(F32)
        block[PAD : PAD + frames, :] = glu
        block[PAD + frames :, :] = right[0, :, here].astype(F32)
        weight = [weights[j : j + 1, here] for j in range(taps)]
        for start in range(0, frames, 64):
            conv[start : start + 64, here] = depthwise(block, weight, start, 64, range(taps))
        return 0

    lax.fori_loop(0, blocks, channel, 0)

    def normalize(i, _):
        at = pl.ds(pl.multiple_of(i * 16, 16), 16)
        values = conv[at, :]
        centered = values - jnp.sum(values, axis=-1, keepdims=True) * (1.0 / width)
        spread = jnp.sum(centered * centered, axis=-1, keepdims=True) * (1.0 / width)
        inv = lax.rsqrt(spread + EPSILON)
        normed = centered * inv
        hat[0, at, :] = normed
        inverse[0, at, :] = jnp.broadcast_to(inv, (16, LANES))
        pre = normed * gain[...]
        out = pre * sigmoid(pre)
        row = i * 16 + lax.broadcasted_iota(jnp.int32, (16, width), 0)
        swished[0, at, :] = jnp.where(row < limit[u], out, 0.0).astype(BF16)
        return 0

    lax.fori_loop(0, frames // 16, normalize, 0)


def forward(limit, hidden, left, right, weights, gain):
    groups, frames, double = hidden.shape
    width = double // 2
    blocks = width // LANES
    length = frames + 2 * PAD
    per = lambda *shape: pl.BlockSpec((1, *shape), lambda u, *_: (u,) + (0,) * len(shape))
    whole = lambda *shape: pl.BlockSpec(shape, lambda u, *_: (0,) * len(shape))
    return pl.pallas_call(
        forward_kernel,
        grid_spec=pltpu.PrefetchScalarGridSpec(
            num_scalar_prefetch=1,
            grid=(groups,),
            in_specs=[
                per(frames, double),
                per(PAD, width),
                per(PAD, width),
                whole(*weights.shape),
                whole(1, width),
            ],
            out_specs=[
                per(blocks, length, LANES),
                per(frames, width),
                per(frames, LANES),
                per(frames, width),
            ],
            scratch_shapes=[pltpu.VMEM((frames, width), F32)],
        ),
        out_shape=[
            jax.ShapeDtypeStruct((groups, blocks, length, LANES), F32),
            jax.ShapeDtypeStruct((groups, frames, width), F32),
            jax.ShapeDtypeStruct((groups, frames, LANES), F32),
            jax.ShapeDtypeStruct((groups, frames, width), BF16),
        ],
        name="forward",
        cost_estimate=pl.CostEstimate(flops=2 * 31 * 600000, bytes_accessed=9 << 20, transcendentals=1200000),
        compiler_params=pltpu.CompilerParams(vmem_limit_bytes=24 << 20),
    )(limit, hidden, left, right, weights, gain)


def product_kernel(core, near, far, mine, other, out, scratch):
    contract = (((0,), (0,)), ((), ()))
    result = lax.dot_general(near[...], mine[...], contract, preferred_element_type=F32)
    result = result + lax.dot_general(far[...], other[...], contract, preferred_element_type=F32)
    pairs = scratch.shape[0]
    first = lax.broadcasted_iota(jnp.int32, (pairs, 8, LANES), 1) < 4
    pick = lambda a, b: jnp.where(first, a, b)
    roll = lambda a: pltpu.roll(a, 4, 1)

    def parts(k):
        cut = result[:, k * LANES : (k + 1) * LANES].reshape(pairs, 3, 8, LANES)
        return cut[:, 0], cut[:, 1], cut[:, 2]

    for q in range(result.shape[1] // LANES // 2):
        a, b, c = parts(2 * q)
        d, e, f = parts(2 * q + 1)
        rb, rc, rd = roll(b), roll(c), roll(d)
        even = (a, pick(b, rd), pick(rd, roll(e)))
        odd = (pick(rb, rc), pick(rc, e), f)
        for side, tiles in enumerate((even, odd)):
            for i, tile in enumerate(tiles):
                scratch[:, side, 24 * q + 8 * i : 24 * q + 8 * i + 8, :] = tile
    out[...] = scratch[...].astype(BF16)


def product(core, near, far, cotangent, other, devices):
    rows, width = near.shape
    half = width // 2
    own = width // devices
    step = 32 * own
    pairs = 16
    deep = own * half // LANES
    return pl.pallas_call(
        product_kernel,
        grid_spec=pltpu.PrefetchScalarGridSpec(
            num_scalar_prefetch=1,
            grid=(width // step,),
            in_specs=[
                pl.BlockSpec((rows, step), lambda i, c: (0, i)),
                pl.BlockSpec((rows, step), lambda i, c: (0, i)),
                pl.BlockSpec((rows, half), lambda i, c: (0, c[0])),
                pl.BlockSpec((rows, half), lambda i, c: (0, 0)),
            ],
            out_specs=pl.BlockSpec((pairs, 2, deep, LANES), lambda i, c: (i, 0, 0, 0)),
            scratch_shapes=[pltpu.VMEM((pairs, 2, deep, LANES), F32)],
        ),
        out_shape=jax.ShapeDtypeStruct((devices // 2, 2, deep, LANES), BF16),
        name="product",
        cost_estimate=pl.CostEstimate(flops=4 * rows * width * half, bytes_accessed=6 << 20, transcendentals=0),
        compiler_params=pltpu.CompilerParams(vmem_limit_bytes=20 << 20),
    )(core, near, far, cotangent, other)


def backward_kernel(limit, cotangent, w_out, hat, inverse, gain, grad_conv, term, grad, sums):
    frames, width = hat.shape[1:]
    u = pl.program_id(0)
    grad[...] = lax.dot_general(
        cotangent[0], w_out[...], (((1,), (1,)), ((), ())), preferred_element_type=F32
    )

    @pl.when(u == 0)
    def _():
        sums[...] = jnp.zeros_like(sums)

    def norm(i, _):
        at = pl.ds(pl.multiple_of(i * 16, 16), 16)
        row = i * 16 + lax.broadcasted_iota(jnp.int32, (16, width), 0)
        swish = jnp.where(row < limit[u], grad[at, :], 0.0)
        normed = hat[0, at, :]
        pre = normed * gain[...]
        gate = sigmoid(pre)
        grad_pre = swish * gate * (1.0 + pre * (1.0 - gate))
        product = grad_pre * normed
        sums[...] += product[0:8] + product[8:16]
        scaled = grad_pre * gain[...]
        mean = jnp.sum(scaled, axis=-1, keepdims=True) * (1.0 / width)
        slope = jnp.sum(scaled * normed, axis=-1, keepdims=True) * (1.0 / width)
        inv = inverse[0, at, 0:1]
        grad_conv[0, at, :] = (inv * (scaled - mean - normed * slope)).astype(BF16)
        return 0

    lax.fori_loop(0, frames // 16, norm, 0)

    @pl.when(u == pl.num_programs(0) - 1)
    def _():
        term[...] = jnp.sum(sums[...], axis=0, keepdims=True)


def backward(limit, cotangent, w_out, hat, inverse, gain):
    groups, frames, width = hat.shape
    per = lambda *shape: pl.BlockSpec((1, *shape), lambda u, *_: (u,) + (0,) * len(shape))
    whole = lambda *shape: pl.BlockSpec(shape, lambda u, *_: (0,) * len(shape))
    return pl.pallas_call(
        backward_kernel,
        grid_spec=pltpu.PrefetchScalarGridSpec(
            num_scalar_prefetch=1,
            grid=(groups,),
            in_specs=[
                per(frames, width),
                whole(width, width),
                per(frames, width),
                per(frames, LANES),
                whole(1, width),
            ],
            out_specs=[per(frames, width), whole(1, width)],
            scratch_shapes=[pltpu.VMEM((frames, width), F32), pltpu.VMEM((8, width), F32)],
        ),
        out_shape=[
            jax.ShapeDtypeStruct((groups, frames, width), BF16),
            jax.ShapeDtypeStruct((1, width), F32),
        ],
        name="backward",
        cost_estimate=pl.CostEstimate(
            flops=2 * groups * frames * width * width, bytes_accessed=10 << 20, transcendentals=600000
        ),
        compiler_params=pltpu.CompilerParams(vmem_limit_bytes=30 << 20),
    )(limit, cotangent, w_out, hat, inverse, gain)


def terms_kernel(grad_conv, slab, term, out, grad):
    groups, frames = grad_conv.shape[:2]
    taps = out.shape[0] - 1
    grad[...] = grad_conv[...].astype(F32)
    for r in range(8):
        chosen = [j for j in range(r, taps, 8)]
        totals = [None] * len(chosen)
        for u in range(groups):
            for i in range(frames // 8):
                left = grad[u, 8 * i : 8 * i + 8, :]
                for n, j in enumerate(chosen):
                    value = left * slab[u, 0, pl.ds(8 * i + 1 + j, 8), :]
                    totals[n] = value if totals[n] is None else totals[n] + value
        for n, j in enumerate(chosen):
            out[j : j + 1, :] = jnp.sum(totals[n], axis=0, keepdims=True)
    out[taps : taps + 1, :] = term[...]


def kernel_terms(grad_conv, slab, term, taps):
    groups, frames, width = grad_conv.shape
    blocks, length = slab.shape[1:3]
    return pl.pallas_call(
        terms_kernel,
        grid=(blocks,),
        in_specs=[
            pl.BlockSpec((groups, frames, LANES), lambda c: (0, 0, c)),
            pl.BlockSpec((groups, 1, length, LANES), lambda c: (0, c, 0, 0)),
            pl.BlockSpec((1, LANES), lambda c: (0, c)),
        ],
        out_specs=pl.BlockSpec((taps + 1, LANES), lambda c: (0, c)),
        out_shape=jax.ShapeDtypeStruct((taps + 1, width), F32),
        scratch_shapes=[pltpu.VMEM((groups, frames, LANES), F32)],
        name="kernel_terms",
        cost_estimate=pl.CostEstimate(flops=2 * 31 * 600000, bytes_accessed=4 << 20, transcendentals=0),
        compiler_params=pltpu.CompilerParams(vmem_limit_bytes=16 << 20),
    )(grad_conv, slab, term)


def input_kernel(limit, grad_conv, left, right, hidden, weights, out, block):
    taps = weights.shape[0] - 1
    frames, width = grad_conv.shape[1:]
    blocks = width // LANES
    u = pl.program_id(0)

    def channel(cb, _):
        here = pl.ds(pl.multiple_of(cb * LANES, LANES), LANES)
        there = pl.ds(pl.multiple_of(width + cb * LANES, LANES), LANES)
        block[0:PAD, :] = left[0, :, here].astype(F32)
        block[PAD : PAD + frames, :] = grad_conv[0, :, here].astype(F32)
        block[PAD + frames :, :] = right[0, :, here].astype(F32)
        weight = [weights[j : j + 1, here] for j in range(taps)]
        for start in range(0, frames, 64):
            at = slice(start, start + 64)
            grad = depthwise(block, weight, start, 64, range(taps - 1, -1, -1))
            row = start + lax.broadcasted_iota(jnp.int32, (64, LANES), 0)
            grad = jnp.where(row < limit[u], grad, 0.0)
            linear = hidden[0, at, here].astype(F32)
            gate = sigmoid(hidden[0, at, there].astype(F32))
            opened = grad * gate
            out[0, at, here] = opened.astype(BF16)
            out[0, at, there] = (opened * linear * (1.0 - gate)).astype(BF16)
        return 0

    lax.fori_loop(0, blocks, channel, 0)


def input_gradient(limit, grad_conv, left, right, hidden, weights):
    groups, frames, double = hidden.shape
    width = double // 2
    per = lambda *shape: pl.BlockSpec((1, *shape), lambda u, *_: (u,) + (0,) * len(shape))
    whole = lambda *shape: pl.BlockSpec(shape, lambda u, *_: (0,) * len(shape))
    return pl.pallas_call(
        input_kernel,
        grid_spec=pltpu.PrefetchScalarGridSpec(
            num_scalar_prefetch=1,
            grid=(groups,),
            in_specs=[
                per(frames, width),
                per(PAD, width),
                per(PAD, width),
                per(frames, double),
                whole(*weights.shape),
            ],
            out_specs=per(frames, double),
            scratch_shapes=[pltpu.VMEM((frames + 2 * PAD, LANES), F32)],
        ),
        out_shape=jax.ShapeDtypeStruct((groups, frames, double), BF16),
        name="input_gradient",
        cost_estimate=pl.CostEstimate(flops=2 * 31 * 600000, bytes_accessed=6 << 20, transcendentals=600000),
        compiler_params=pltpu.CompilerParams(vmem_limit_bytes=20 << 20),
    )(limit, grad_conv, left, right, hidden, weights)


def sum_kernel(factor, got, out, total):
    i = pl.program_id(0)
    own = out.shape[0]

    @pl.when(i == 0)
    def _():
        total[...] = jnp.zeros_like(total)

    total[...] += jnp.sum(got[...].astype(F32), axis=0)

    @pl.when(i == pl.num_programs(0) - 1)
    def _():
        blocks = total.shape[1] // own
        for side in range(2):
            for k in range(blocks):
                lane = (side * blocks + k) * LANES
                out[:, lane : lane + LANES] = total[side, own * k : own * (k + 1), :] * factor


def sum_pieces(got, factor, own, width):
    pairs, sides, deep, _ = got.shape
    step = 8
    return pl.pallas_call(
        functools.partial(sum_kernel, factor),
        grid=(pairs // step,),
        in_specs=[pl.BlockSpec((step, sides, deep, LANES), lambda i: (i, 0, 0, 0))],
        out_specs=pl.BlockSpec((own, width), lambda i: (0, 0)),
        out_shape=jax.ShapeDtypeStruct((own, width), F32),
        scratch_shapes=[pltpu.VMEM((sides, deep, LANES), F32)],
        name="sum_pieces",
        compiler_params=pltpu.CompilerParams(vmem_limit_bytes=8 << 20),
    )(got)


def neighbours(tail, head):
    ends = lax.axis_size("seq") - 1
    left = lax.ppermute(tail, "seq", [(i, i + 1) for i in range(ends)])
    right = lax.ppermute(head, "seq", [(i + 1, i) for i in range(ends)])
    return left, right


def local(hidden, cotangent, lengths, kernel, conv_gain, w_out):
    groups, frames, double = hidden.shape
    width = double // 2
    half = width // 2
    taps = kernel.shape[1]
    seq_count = lax.axis_size("seq")
    devices = lax.axis_size("dp") * seq_count
    own = width // devices
    rows = groups * frames
    swap = [(i, i ^ 1) for i in range(seq_count)]
    place = lax.axis_index("seq")
    core = place % 2
    limit = lengths - place * frames
    weights = jnp.concatenate([kernel, jnp.zeros((width, 1), F32)], axis=1).T
    gain = conv_gain.reshape(1, width)

    def gated(start):
        cells = hidden[:, start : start + PAD].astype(F32)
        spots = start + jnp.arange(PAD, dtype=jnp.int32)
        keep = spots[None, :, None] < limit[:, None, None]
        return jnp.where(keep, cells[..., :width] * sigmoid(cells[..., width:]), 0.0).astype(BF16)

    left, right = neighbours(gated(frames - PAD), gated(0))
    flat = cotangent.reshape(rows, width)
    sent = jnp.where(core == 0, flat[:, half:], flat[:, :half])
    other = lax.ppermute(sent, "seq", swap)

    slab, hat, inverse, swished = forward(limit, hidden, left, right, weights, gain)
    near = swished.reshape(rows, width)
    far = lax.ppermute(near, "seq", swap)
    pieces = product(core.reshape(1), near, far, flat, other, devices)
    got = lax.all_to_all(
        pieces.reshape(devices, own * half // LANES, LANES), AXES, 0, 0, tiled=True
    )

    hat, pieces = lax.optimization_barrier((hat, pieces))
    grad_conv, term_conv = backward(limit, cotangent, w_out, hat, inverse, gain)
    grad_left, grad_right = neighbours(grad_conv[:, frames - PAD :], grad_conv[:, :PAD])
    terms = kernel_terms(grad_conv, slab, term_conv, taps)
    small = terms.T.reshape(devices, own * (taps + 1) // LANES, LANES)
    got_small = lax.all_to_all(small, AXES, 0, 0, tiled=True)
    grad_hidden = input_gradient(limit, grad_conv, grad_left, grad_right, hidden, weights)

    factor = 1.0 / math.sqrt(groups * lax.axis_size("dp") * frames * seq_count)
    grad_w = sum_pieces(got.reshape(devices // 2, 2, -1, LANES), factor, own, width)
    summed = jnp.sum(got_small, axis=0).reshape(own, taps + 1) * factor
    return grad_hidden, grad_w, summed[:, :taps], summed[:, taps]


def solution(mesh):
    in_specs = (P("dp", "seq", None), P("dp", "seq", None), P("dp"), P(), P(), P())
    out_specs = (P("dp", "seq", None), P(AXES, None), P(AXES, None), P(AXES))
    return jax.shard_map(local, mesh=mesh, in_specs=in_specs, out_specs=out_specs, check_vma=False)
```

```python
import functools
import math

import jax
import jax.numpy as jnp
from jax import lax
from jax.experimental import pallas as pl
from jax.experimental.pallas import tpu as pltpu
from jax.sharding import PartitionSpec as P

EPSILON = 1e-05
AXES = ("dp", "seq")
LANES = 128
HALF_PAD = 16
PAD = 32
TILE = 16
F32, BF16 = jnp.float32, jnp.bfloat16
VMEM = pl.BlockSpec(memory_space=pltpu.VMEM)
SMEM = pl.BlockSpec(memory_space=pltpu.SMEM)


def sigmoid(x):
    return 0.5 * jnp.tanh(0.5 * x) + 0.5


def lane(block):
    return pl.ds(pl.multiple_of(block * LANES, LANES), LANES)


def call(kernel, in_specs, out_shape, scratch, flops, limit, aliases=None):
    return pl.pallas_call(
        kernel,
        in_specs=in_specs,
        out_specs=jax.tree.map(lambda _: VMEM, out_shape),
        out_shape=out_shape,
        scratch_shapes=scratch,
        input_output_aliases=aliases or {},
        cost_estimate=pl.CostEstimate(flops=flops, bytes_accessed=8 << 20, transcendentals=0),
        compiler_params=pltpu.CompilerParams(vmem_limit_bytes=limit << 20),
    )


def shape(dims, dtype):
    return jax.ShapeDtypeStruct(dims, dtype)


def depthwise(slab, weight, start, rows, order):
    total = None
    for j, row in enumerate(order):
        term = slab[pl.ds(start + 1 + j, rows), :] * weight[row]
        total = term if total is None else total + term
    return total


def edges_kernel(limit, hidden, cotangent, tail, head):
    groups, frames, double = hidden.shape
    width = double // 2
    for u in range(groups):
        for out, start, near in ((tail, frames - PAD, frames - HALF_PAD), (head, 0, 0)):
            for cb in range(width // LANES):
                here = slice(cb * LANES, (cb + 1) * LANES)
                there = slice(width + cb * LANES, width + (cb + 1) * LANES)
                row = start + lax.broadcasted_iota(jnp.int32, (PAD, LANES), 0)
                linear = hidden[u, start : start + PAD, here].astype(F32)
                gate = sigmoid(hidden[u, start : start + PAD, there].astype(F32))
                glu = jnp.where(row < limit[u], linear * gate, 0.0)
                out[u, 0:PAD, here] = glu.astype(BF16)
            out[u, PAD:, :] = cotangent[u, near : near + HALF_PAD, :]


def gate_kernel(limit, hidden, slab):
    groups, frames, double = hidden.shape
    width = double // 2
    blocks = width // LANES
    for u in range(groups):

        def channel(cb, _):
            row = lax.broadcasted_iota(jnp.int32, (frames, LANES), 0)
            linear = hidden[u, :, lane(cb)].astype(F32)
            gate = sigmoid(hidden[u, :, lane(blocks + cb)].astype(F32))
            glu = jnp.where(row < limit[u], linear * gate, 0.0)
            slab[u, cb, PAD : PAD + frames, :] = glu.astype(BF16).astype(F32)
            return 0

        lax.fori_loop(0, blocks, channel, 0)


def forward_kernel(limit, gated, left, right, weights, gain, slab, hat, inverse, swished):
    groups, blocks, length = slab.shape[:3]
    taps = weights.shape[0] - 1
    width = blocks * LANES
    frames = length - 2 * PAD
    span = frames + 2 * HALF_PAD
    chunk = span // 4
    for u in range(groups):

        def channel(cb, _):
            block = slab.at[u, cb]
            block[0:PAD, :] = left[u, 0:PAD, lane(cb)].astype(F32)
            block[PAD + frames :, :] = right[u, 0:PAD, lane(cb)].astype(F32)
            weight = [weights[j : j + 1, lane(cb)] for j in range(taps)]
            for start in range(0, span, chunk):
                at = slice(u * span + start, u * span + start + chunk)
                hat[at, lane(cb)] = depthwise(block, weight, start, chunk, range(taps))
            return 0

        lax.fori_loop(0, blocks, channel, 0)

        def normalize(i, _):
            at = pl.ds(pl.multiple_of(u * span + i * TILE, TILE), TILE)
            values = hat[at, :]
            centered = values - jnp.sum(values, axis=-1, keepdims=True) * (1.0 / width)
            spread = jnp.sum(centered * centered, axis=-1, keepdims=True) * (1.0 / width)
            inv = lax.rsqrt(spread + EPSILON)
            normed = centered * inv
            hat[at, :] = normed
            inverse[at, :] = jnp.broadcast_to(inv, (TILE, LANES))

            @pl.when((i >= 1) & (i <= frames // TILE))
            def _():
                pre = normed * gain[...]
                out = pre * sigmoid(pre)
                row = (i - 1) * TILE + lax.broadcasted_iota(jnp.int32, (TILE, width), 0)
                to = pl.ds(pl.multiple_of(u * frames + (i - 1) * TILE, TILE), TILE)
                swished[to, :] = jnp.where(row < limit[u], out, 0.0).astype(BF16)

            return 0

        lax.fori_loop(0, span // TILE, normalize, 0)


CONTRACT_ROWS = (((0,), (0,)), ((), ()))


def product_kernel(core, near, cotangent, far, other, packed, out, scratch):
    width = near.shape[1]
    half = width // 2
    pairs = scratch.shape[0]
    step = 24 * pairs
    deep = out.shape[2] - 8
    first = lax.broadcasted_iota(jnp.int32, (pairs, 8, LANES), 1) < 4
    pick = lambda a, b: jnp.where(first, a, b)
    roll = lambda a: pltpu.roll(a, 4, 1)
    mine = pl.ds(pl.multiple_of(core[0] * half, LANES), half)

    def rows(s, _):
        at = pl.ds(pl.multiple_of(s * step, step), step)
        result = lax.dot_general(
            near[:, at], cotangent[:, mine], CONTRACT_ROWS, preferred_element_type=F32
        ) + lax.dot_general(far[:, at], other[...], CONTRACT_ROWS, preferred_element_type=F32)

        def parts(k):
            cut = result[:, k * LANES : (k + 1) * LANES].reshape(pairs, 3, 8, LANES)
            return cut[:, 0], cut[:, 1], cut[:, 2]

        for q in range(half // LANES // 2):
            a, b, c = parts(2 * q)
            d, e, f = parts(2 * q + 1)
            rb, rc, rd = roll(b), roll(c), roll(d)
            even = (a, pick(b, rd), pick(rd, roll(e)))
            odd = (pick(rb, rc), pick(rc, e), f)
            for side, tiles in enumerate((even, odd)):
                for i, tile in enumerate(tiles):
                    scratch[:, side, 24 * q + 8 * i : 24 * q + 8 * i + 8, :] = tile
        small = packed[pl.ds(s * pairs, pairs)]
        scratch[:, :, deep:, :] = small
        out[pl.ds(s * pairs, pairs)] = scratch[...].astype(BF16)
        return 0

    lax.fori_loop(0, width // step, rows, 0)


def backward_kernel(limit, cotangent, left, right, w_out, hat, inverse, gain, slab, term, held, grad, sums):
    groups, frames, width = cotangent.shape
    span = frames + 2 * HALF_PAD
    blocks = width // LANES
    for u in range(groups):
        base = u * span
        held[base : base + HALF_PAD, :] = left[u, PAD:, :]
        held[base + HALF_PAD : base + HALF_PAD + frames, :] = cotangent[u]
        held[base + HALF_PAD + frames : base + span, :] = right[u, PAD:, :]
    step = 2 * LANES

    def columns(n, _):
        at = pl.ds(pl.multiple_of(n * step, step), step)
        grad[:, at] = lax.dot_general(
            held[...], w_out[at, :], (((1,), (1,)), ((), ())), preferred_element_type=F32
        )
        return 0

    lax.fori_loop(0, width // step, columns, 0)
    sums[...] = jnp.zeros_like(sums)
    for u in range(groups):

        def norm(i, _):
            at = pl.ds(pl.multiple_of(u * span + i * TILE, TILE), TILE)
            row = i * TILE - HALF_PAD + lax.broadcasted_iota(jnp.int32, (TILE, width), 0)
            swish = jnp.where(row < limit[u], grad[at, :], 0.0)
            normed = hat[at, :]
            pre = normed * gain[...]
            gate = sigmoid(pre)
            grad_pre = swish * gate * (1.0 + pre * (1.0 - gate))

            @pl.when((i >= 1) & (i <= frames // TILE))
            def _():
                product = grad_pre * normed
                sums[...] += product[0:8] + product[8:16]

            scaled = grad_pre * gain[...]
            mean = jnp.sum(scaled, axis=-1, keepdims=True) * (1.0 / width)
            slope = jnp.sum(scaled * normed, axis=-1, keepdims=True) * (1.0 / width)
            inv = inverse[at, 0:1]
            result = (inv * (scaled - mean - normed * slope)).astype(BF16).astype(F32)
            to = pl.ds(pl.multiple_of(i * TILE, TILE), TILE)
            for cb in range(blocks):
                slab[u, cb, to, :] = result[:, cb * LANES : (cb + 1) * LANES]
            return 0

        lax.fori_loop(0, span // TILE, norm, 0)
    term[...] = jnp.sum(sums[...], axis=0, keepdims=True)


def terms_kernel(grad, slab, term, packed, square, columns, rounded, rest):
    groups, blocks, span = grad.shape[:3]
    frames = span - 2 * HALF_PAD
    taps = 31
    square[...] = jnp.zeros_like(square)

    def channel(cb, _):
        for r in range(8):
            chosen = [j for j in range(r, taps, 8)]
            totals = [None] * len(chosen)
            for u in range(groups):
                for i in range(frames // 8):
                    value = grad[u, cb, HALF_PAD + 8 * i : HALF_PAD + 8 * i + 8, :]
                    for n, j in enumerate(chosen):
                        place = PAD - taps // 2 + 8 * i + j
                        part = value * slab[u, cb, pl.ds(place, 8), :]
                        totals[n] = part if totals[n] is None else totals[n] + part
            for n, j in enumerate(chosen):
                square[j : j + 1, :] = jnp.sum(totals[n], axis=0, keepdims=True)
        square[taps : taps + 1, :] = term[:, lane(cb)]
        columns[lane(cb), :] = square[...].T
        return 0

    lax.fori_loop(0, blocks, channel, 0)
    quarter = columns.shape[0] // 4
    total = columns[pl.ds(0, quarter, stride=4), :]
    for m in range(1, 4):
        total = total + pltpu.roll(columns[pl.ds(m, quarter, stride=4), :], 32 * m, 1)
    high = total.astype(BF16).astype(F32)
    rounded[0:quarter, :] = high
    rest[8 : 8 + quarter, :] = total - high
    row = lax.broadcasted_iota(jnp.int32, (8, LANES), 0)
    pairs, sides = packed.shape[:2]
    for d in range(pairs * sides):
        upper = rounded[3 * d : 3 * d + 8, :]
        lower = rest[3 * d + 5 : 3 * d + 13, :]
        tile = jnp.where(row < 3, upper, jnp.where(row < 6, lower, 0.0))
        packed[d // 2, d % 2] = tile


def input_kernel(limit, grad, hidden, weights, out):
    groups, frames, _ = hidden.shape
    blocks = grad.shape[1]
    taps = weights.shape[0] - 1
    chunk = 64
    for u in range(groups):

        def channel(cb, _):
            block = grad.at[u, cb]
            weight = [weights[j : j + 1, lane(cb)] for j in range(taps)]
            for start in range(0, frames, chunk):
                at = slice(start, start + chunk)
                total = depthwise(block, weight, start, chunk, range(taps - 1, -1, -1))
                row = start + lax.broadcasted_iota(jnp.int32, (chunk, LANES), 0)
                total = jnp.where(row < limit[u], total, 0.0)
                linear = hidden[u, at, lane(cb)].astype(F32)
                gate = sigmoid(hidden[u, at, lane(blocks + cb)].astype(F32))
                opened = total * gate
                out[u, at, lane(cb)] = opened.astype(BF16)
                out[u, at, lane(blocks + cb)] = (opened * linear * (1.0 - gate)).astype(BF16)
            return 0

        lax.fori_loop(0, blocks, channel, 0)


def sum_kernel(factor, got, out, taps_out, gain_out, total):
    own = out.shape[0]
    pairs, _, tall, _ = got.shape
    step = 4
    total[...] = jnp.zeros_like(total)

    def add(i, _):
        total[...] += jnp.sum(got[pl.ds(i * step, step)].astype(F32), axis=0)
        return 0

    lax.fori_loop(0, pairs // step, add, 0)
    deep = tall - 8
    blocks = deep // own
    for side in range(2):
        for k in range(blocks):
            at = (side * blocks + k) * LANES
            out[:, at : at + LANES] = total[side, own * k : own * (k + 1), :] * factor
    both = total[0, deep:, :] + total[1, deep:, :]
    small = (both[0:3] + both[3:6]) * factor
    taps = taps_out.shape[1]
    spot = lax.broadcasted_iota(jnp.int32, (1, LANES), 1)
    gains = jnp.zeros((1, LANES), F32)
    for r in range(3):
        for m in range(4):
            c = 4 * r + m
            turned = pltpu.roll(small[r : r + 1, :], (LANES - 32 * m) % LANES, 1)
            taps_out[c : c + 1, :] = turned[:, :taps]
            gains = jnp.where(spot == c, pltpu.roll(turned, (c - taps) % LANES, 1), gains)
    gain_out[...] = gains[:, :own]


def local(hidden, cotangent, lengths, kernel, conv_gain, w_out):
    groups, frames, double = hidden.shape
    width = double // 2
    half = width // 2
    blocks = width // LANES
    taps = kernel.shape[1]
    seq_count = lax.axis_size("seq")
    devices = lax.axis_size("dp") * seq_count
    own = width // devices
    rows = groups * frames
    span = frames + 2 * HALF_PAD
    length = frames + 2 * PAD
    deep = own * half // LANES
    ends = seq_count - 1
    swap = [(i, i ^ 1) for i in range(seq_count)]
    place = lax.axis_index("seq")
    core = place & 1
    conv_flops = 2 * taps * rows * width

    limit = lengths - place * frames
    flat = cotangent.reshape(rows, width)
    tail, head = call(
        edges_kernel,
        [SMEM, VMEM, VMEM],
        [shape((groups, PAD + HALF_PAD, width), BF16)] * 2,
        [],
        1 << 20,
        4,
    )(limit, hidden, cotangent)
    left = lax.ppermute(tail, "seq", [(i, i + 1) for i in range(ends)])
    right = lax.ppermute(head, "seq", [(i + 1, i) for i in range(ends)])
    sent = jnp.where(core == 0, flat[:, half:], flat[:, :half])
    other = lax.ppermute(sent, "seq", swap)
    gated = call(
        gate_kernel, [SMEM, VMEM], shape((groups, blocks, length, LANES), F32), [], 8 << 20, 4
    )(limit, hidden)
    weights = jnp.concatenate([kernel, jnp.zeros((width, 1), F32)], axis=1).T
    gain = conv_gain.reshape(1, width)
    slab, hat, inverse, swished = call(
        forward_kernel,
        [SMEM] + [VMEM] * 5,
        [
            shape((groups, blocks, length, LANES), F32),
            shape((groups * span, width), F32),
            shape((groups * span, LANES), F32),
            shape((rows, width), BF16),
        ],
        [],
        conv_flops,
        4,
        {1: 0},
    )(limit, gated, left, right, weights, gain)
    far = lax.ppermute(swished, "seq", swap)
    grad, term_conv = call(
        backward_kernel,
        [SMEM] + [VMEM] * 7,
        [shape((groups, blocks, span, LANES), F32), shape((1, width), F32)],
        [
            pltpu.VMEM((groups * span, width), BF16),
            pltpu.VMEM((groups * span, width), F32),
            pltpu.VMEM((8, width), F32),
        ],
        2 * rows * width * width,
        10,
    )(limit, cotangent, left, right, w_out, hat, inverse, gain)
    packed = call(
        terms_kernel,
        [VMEM] * 3,
        shape((devices // 2, 2, 8, LANES), F32),
        [
            pltpu.VMEM((LANES, LANES), F32),
            pltpu.VMEM((width, LANES), F32),
            pltpu.VMEM((width // 4 + 8, LANES), F32),
            pltpu.VMEM((width // 4 + 16, LANES), F32),
        ],
        conv_flops,
        6,
    )(grad, slab, term_conv)
    pieces = call(
        product_kernel,
        [SMEM] + [VMEM] * 5,
        shape((devices // 2, 2, deep + 8, LANES), BF16),
        [pltpu.VMEM((16, 2, deep + 8, LANES), F32)],
        4 * rows * width * half,
        8,
    )(core.reshape(1), swished, flat, far, other, packed)
    got = lax.all_to_all(pieces.reshape(devices, deep + 8, LANES), AXES, 0, 0, tiled=True)
    grad_hidden = call(
        input_kernel, [SMEM] + [VMEM] * 3, shape((groups, frames, double), BF16), [], conv_flops, 4
    )(limit, grad, hidden, weights)

    factor = 1.0 / math.sqrt(groups * lax.axis_size("dp") * frames * seq_count)
    grad_w, grad_kernel, grad_gain = call(
        functools.partial(sum_kernel, factor),
        [VMEM],
        [shape((own, width), F32), shape((own, taps), F32), shape((1, own), F32)],
        [pltpu.VMEM((2, deep + 8, LANES), F32)],
        1 << 20,
        4,
    )(got.reshape(devices // 2, 2, deep + 8, LANES))
    return grad_hidden, grad_w, grad_kernel, grad_gain.reshape(own)


def solution(mesh):
    in_specs = (P("dp", "seq", None), P("dp", "seq", None), P("dp"), P(), P(), P())
    out_specs = (P("dp", "seq", None), P(AXES, None), P(AXES, None), P(AXES))
    return jax.shard_map(local, mesh=mesh, in_specs=in_specs, out_specs=out_specs, check_vma=False)
```

```python
import functools
import math

import jax
import jax.numpy as jnp
from jax import lax
from jax.experimental import pallas as pl
from jax.experimental.pallas import tpu as pltpu
from jax.sharding import PartitionSpec as P

EPSILON = 1e-05
AXES = ("dp", "seq")
LANES = 128
HALF_PAD = 16
PAD = 32
TILE = 16
F32, BF16 = jnp.float32, jnp.bfloat16
VMEM = pl.BlockSpec(memory_space=pltpu.VMEM)
SMEM = pl.BlockSpec(memory_space=pltpu.SMEM)
HBM = pl.BlockSpec(memory_space=pltpu.HBM)


def sigmoid(x):
    return 0.5 * jnp.tanh(0.5 * x) + 0.5


def left_of(lengths, place, u, frames):
    return lengths[u] - place[0] * frames


def lane(block):
    return pl.ds(pl.multiple_of(block * LANES, LANES), LANES)


def call(kernel, in_specs, out_shape, scratch, flops, limit, aliases=None, out_specs=None):
    return pl.pallas_call(
        kernel,
        in_specs=in_specs,
        out_specs=out_specs or jax.tree.map(lambda _: VMEM, out_shape),
        out_shape=out_shape,
        scratch_shapes=scratch,
        input_output_aliases=aliases or {},
        cost_estimate=pl.CostEstimate(flops=flops, bytes_accessed=8 << 20, transcendentals=0),
        compiler_params=pltpu.CompilerParams(vmem_limit_bytes=limit << 20),
    )


def shape(dims, dtype):
    return jax.ShapeDtypeStruct(dims, dtype)


def far_memory(array):
    return pltpu.with_memory_space_constraint(array, pltpu.HBM)


def depthwise(slab, weight, start, rows, order):
    total = None
    for j, row in enumerate(order):
        term = slab[pl.ds(start + 1 + j, rows), :] * weight[row]
        total = term if total is None else total + term
    return total


def edges_kernel(lengths, place, hidden, cotangent, tail, head, cells, upstream, arrived):
    groups, frames, double = hidden.shape
    width = double // 2
    copies = []
    for side, (start, near) in enumerate(((frames - PAD, frames - HALF_PAD), (0, 0))):
        for u in range(groups):
            copies.append(
                (
                    pltpu.make_async_copy(
                        hidden.at[u, start : start + PAD], cells.at[side, u], arrived.at[0, side, u]
                    ),
                    pltpu.make_async_copy(
                        cotangent.at[u, near : near + HALF_PAD],
                        upstream.at[side, u],
                        arrived.at[1, side, u],
                    ),
                )
            )
    for first, second in copies:
        first.start()
        second.start()
    n = 0
    for side, (out, start) in enumerate(((tail, frames - PAD), (head, 0))):
        for u in range(groups):
            limit = left_of(lengths, place, u, frames)
            copies[n][0].wait()
            row = start + lax.broadcasted_iota(jnp.int32, (PAD, LANES), 0)
            for cb in range(width // LANES):
                here = slice(cb * LANES, (cb + 1) * LANES)
                there = slice(width + cb * LANES, width + (cb + 1) * LANES)
                linear = cells[side, u, :, here].astype(F32)
                gate = sigmoid(cells[side, u, :, there].astype(F32))
                glu = jnp.where(row < limit, linear * gate, 0.0)
                out[u, 0:PAD, here] = glu.astype(BF16)
            copies[n][1].wait()
            out[u, PAD:, :] = upstream[side, u]
            n += 1


def gate_kernel(lengths, place, hidden, slab):
    groups, frames, double = hidden.shape
    width = double // 2
    blocks = width // LANES
    for u in range(groups):
        limit = left_of(lengths, place, u, frames)

        def channel(cb, _):
            row = lax.broadcasted_iota(jnp.int32, (frames, LANES), 0)
            linear = hidden[u, :, lane(cb)].astype(F32)
            gate = sigmoid(hidden[u, :, lane(blocks + cb)].astype(F32))
            glu = jnp.where(row < limit, linear * gate, 0.0)
            slab[u, cb, PAD : PAD + frames, :] = glu.astype(BF16).astype(F32)
            return 0

        lax.fori_loop(0, blocks, channel, 0)


def row_mean(values, width):
    mean = jnp.sum(values, axis=-1, keepdims=True) * (1.0 / width)
    return jnp.broadcast_to(mean, values.shape)


def forward_kernel(
    lengths, place, gated, left, right, weights, gain, cotangent, slab, hat, inverse, message, mean
):
    groups, blocks, length = slab.shape[:3]
    taps = weights.shape[0] - 1
    width = blocks * LANES
    half = width // 2
    frames = length - 2 * PAD
    span = frames + 2 * HALF_PAD
    chunk = span // 4
    theirs = pl.ds(pl.multiple_of((1 - (place[0] & 1)) * half, LANES), half)
    message[:, width:] = cotangent[:, theirs]
    for u in range(groups):
        limit = left_of(lengths, place, u, frames)
        base = u * span

        def channel(cb, _):
            block = slab.at[u, cb]
            block[0:PAD, :] = left[u, 0:PAD, lane(cb)].astype(F32)
            block[PAD + frames :, :] = right[u, 0:PAD, lane(cb)].astype(F32)
            weight = [weights[j : j + 1, lane(cb)] for j in range(taps)]
            for start in range(0, span, chunk):
                at = slice(base + start, base + start + chunk)
                hat[at, lane(cb)] = depthwise(block, weight, start, chunk, range(taps))
            return 0

        lax.fori_loop(0, blocks, channel, 0)
        rows = slice(base, base + span)
        total = hat[rows, 0:LANES]
        for cb in range(1, blocks):
            total = total + hat[rows, cb * LANES : (cb + 1) * LANES]
        mean[...] = row_mean(total, width)
        total = None
        for cb in range(blocks):
            centered = hat[rows, cb * LANES : (cb + 1) * LANES] - mean[...]
            total = centered * centered if total is None else total + centered * centered
        inverse[rows, :] = lax.rsqrt(row_mean(total, width) + EPSILON)

        def normalize(cb, _):
            normed = (hat[rows, lane(cb)] - mean[...]) * inverse[rows, :]
            hat[rows, lane(cb)] = normed
            pre = normed[HALF_PAD : HALF_PAD + frames] * (0.5 * gain[:, lane(cb)])
            out = pre * jnp.tanh(pre) + pre
            row = lax.broadcasted_iota(jnp.int32, (frames, LANES), 0)
            out = jnp.where(row < limit, out, 0.0).astype(BF16)
            message[u * frames : (u + 1) * frames, lane(cb)] = out
            return 0

        lax.fori_loop(0, blocks, normalize, 0)


CONTRACT_ROWS = (((0,), (0,)), ((), ()))


def product_kernel(place, near, cotangent, far, packed, out, scratch, held, sent):
    half = cotangent.shape[1] // 2
    width = 2 * half
    pairs = scratch.shape[0]
    step = 24 * pairs
    deep = scratch.shape[2] - 8
    first = lax.broadcasted_iota(jnp.int32, (pairs, 8, LANES), 1) < 4
    pick = lambda a, b: jnp.where(first, a, b)
    roll = lambda a: pltpu.roll(a, 4, 1)
    mine = pl.ds(pl.multiple_of((place[0] & 1) * half, LANES), half)

    def copy(s):
        return pltpu.make_async_copy(held.at[s], out.at[pl.ds(s * pairs, pairs)], sent.at[s])

    def rows(s, _):
        at = pl.ds(pl.multiple_of(s * step, step), step)
        result = lax.dot_general(
            near[:, at], cotangent[:, mine], CONTRACT_ROWS, preferred_element_type=F32
        ) + lax.dot_general(far[:, at], far[:, width:], CONTRACT_ROWS, preferred_element_type=F32)

        def parts(k):
            cut = result[:, k * LANES : (k + 1) * LANES].reshape(pairs, 3, 8, LANES)
            return cut[:, 0], cut[:, 1], cut[:, 2]

        for q in range(half // LANES // 2):
            a, b, c = parts(2 * q)
            d, e, f = parts(2 * q + 1)
            rb, rc, rd = roll(b), roll(c), roll(d)
            even = (a, pick(b, rd), pick(rd, roll(e)))
            odd = (pick(rb, rc), pick(rc, e), f)
            for side, tiles in enumerate((even, odd)):
                for i, tile in enumerate(tiles):
                    scratch[:, side, 24 * q + 8 * i : 24 * q + 8 * i + 8, :] = tile
        scratch[:, :, deep:, :] = packed[pl.ds(s * pairs, pairs)]
        held[s] = scratch[...].astype(BF16)
        copy(s).start()
        return 0

    lax.fori_loop(0, width // step, rows, 0)
    for s in range(width // step):
        copy(s).wait()


def backward_kernel(
    lengths, place, cotangent, left, right, w_out, hat, inverse, gain, slab, term, held, grad, sums
):
    groups, frames, width = cotangent.shape
    span = frames + 2 * HALF_PAD
    blocks = width // LANES
    for u in range(groups):
        base = u * span
        held[base : base + HALF_PAD, :] = left[u, PAD:, :]
        held[base + HALF_PAD : base + HALF_PAD + frames, :] = cotangent[u]
        held[base + HALF_PAD + frames : base + span, :] = right[u, PAD:, :]
    step = 2 * LANES

    def columns(n, _):
        at = pl.ds(pl.multiple_of(n * step, step), step)
        grad[:, at] = lax.dot_general(
            held[...], w_out[at, :], (((1,), (1,)), ((), ())), preferred_element_type=F32
        )
        return 0

    lax.fori_loop(0, width // step, columns, 0)
    sums[...] = jnp.zeros_like(sums)
    part = span // 2

    def norm(n, _):
        u, start = n // 2, (n % 2) * part
        at = pl.ds(pl.multiple_of(n * part, TILE), part)
        limit = left_of(lengths, place, u, frames)
        row = start - HALF_PAD + lax.broadcasted_iota(jnp.int32, (part, LANES), 0)
        keep = row < limit
        inside = (row >= 0) & (row < frames)
        first = second = None
        for cb in range(blocks):
            here = slice(cb * LANES, (cb + 1) * LANES)
            normed = hat[at, here]
            halved = normed * (0.5 * gain[:, here])
            turn = jnp.tanh(halved)
            gate = 0.5 * turn + 0.5
            grad_pre = jnp.where(keep, grad[at, here], 0.0) * (gate * (1.0 + halved * (1.0 - turn)))
            term_part = jnp.where(inside, grad_pre * normed, 0.0)
            sums[:, here] += jnp.sum(term_part.reshape(part // 8, 8, LANES), axis=0)
            scaled = grad_pre * gain[:, here]
            grad[at, here] = scaled
            first = scaled if first is None else first + scaled
            second = scaled * normed if second is None else second + scaled * normed
        mean = row_mean(first, width)
        slope = row_mean(second, width)
        inv = inverse[at, :]
        for cb in range(blocks):
            here = slice(cb * LANES, (cb + 1) * LANES)
            result = inv * (grad[at, here] - mean - hat[at, here] * slope)
            to = pl.ds(pl.multiple_of(start, TILE), part)
            slab[u, cb, to, :] = result.astype(BF16).astype(F32)
        return 0

    lax.fori_loop(0, 2 * groups, norm, 0)
    term[...] = jnp.sum(sums[...], axis=0, keepdims=True)


def terms_kernel(grad, slab, term, packed, square, columns, rounded, rest):
    groups, blocks, span = grad.shape[:3]
    frames = span - 2 * HALF_PAD
    taps = 31
    square[...] = jnp.zeros_like(square)

    def channel(cb, _):
        for r in range(8):
            chosen = [j for j in range(r, taps, 8)]
            totals = [None] * len(chosen)
            for u in range(groups):
                for i in range(frames // 8):
                    value = grad[u, cb, HALF_PAD + 8 * i : HALF_PAD + 8 * i + 8, :]
                    for n, j in enumerate(chosen):
                        place = PAD - taps // 2 + 8 * i + j
                        part = value * slab[u, cb, pl.ds(place, 8), :]
                        totals[n] = part if totals[n] is None else totals[n] + part
            for n, j in enumerate(chosen):
                square[j : j + 1, :] = jnp.sum(totals[n], axis=0, keepdims=True)
        square[taps : taps + 1, :] = term[:, lane(cb)]
        columns[lane(cb), :] = square[...].T
        return 0

    lax.fori_loop(0, blocks, channel, 0)
    quarter = columns.shape[0] // 4
    total = columns[pl.ds(0, quarter, stride=4), :]
    for m in range(1, 4):
        total = total + pltpu.roll(columns[pl.ds(m, quarter, stride=4), :], 32 * m, 1)
    high = total.astype(BF16).astype(F32)
    rounded[0:quarter, :] = high
    rest[8 : 8 + quarter, :] = total - high
    row = lax.broadcasted_iota(jnp.int32, (8, LANES), 0)
    pairs, sides = packed.shape[:2]
    for d in range(pairs * sides):
        upper = rounded[3 * d : 3 * d + 8, :]
        lower = rest[3 * d + 5 : 3 * d + 13, :]
        tile = jnp.where(row < 3, upper, jnp.where(row < 6, lower, 0.0))
        packed[d // 2, d % 2] = tile


def input_kernel(lengths, place, grad, hidden, weights, out):
    groups, frames, _ = hidden.shape
    blocks = grad.shape[1]
    taps = weights.shape[0] - 1
    chunk = 64
    for u in range(groups):
        limit = left_of(lengths, place, u, frames)

        def channel(cb, _):
            block = grad.at[u, cb]
            weight = [weights[j : j + 1, lane(cb)] for j in range(taps)]
            for start in range(0, frames, chunk):
                at = slice(start, start + chunk)
                total = depthwise(block, weight, start, chunk, range(taps - 1, -1, -1))
                row = start + lax.broadcasted_iota(jnp.int32, (chunk, LANES), 0)
                total = jnp.where(row < limit, total, 0.0)
                linear = hidden[u, at, lane(cb)].astype(F32)
                gate = sigmoid(hidden[u, at, lane(blocks + cb)].astype(F32))
                opened = total * gate
                out[u, at, lane(cb)] = opened.astype(BF16)
                out[u, at, lane(blocks + cb)] = (opened * linear * (1.0 - gate)).astype(BF16)
            return 0

        lax.fori_loop(0, blocks, channel, 0)


def sum_kernel(factor, got, out, taps_out, gain_out, total, held, arrived):
    own = out.shape[0]
    slots, step, _, tall, _ = held.shape

    def copy(i):
        return pltpu.make_async_copy(got.at[pl.ds(i * step, step)], held.at[i], arrived.at[i])

    for i in range(slots):
        copy(i).start()
    total[...] = jnp.zeros_like(total)

    def add(i, _):
        copy(i).wait()
        for k in range(0, step, 4):
            total[...] += jnp.sum(held[i, k : k + 4].astype(F32), axis=0)
        return 0

    lax.fori_loop(0, slots, add, 0)
    deep = tall - 8
    blocks = deep // own
    for side in range(2):
        for k in range(blocks):
            at = (side * blocks + k) * LANES
            out[:, at : at + LANES] = total[side, own * k : own * (k + 1), :] * factor
    both = total[0, deep:, :] + total[1, deep:, :]
    small = (both[0:3] + both[3:6]) * factor
    taps = taps_out.shape[1]
    spot = lax.broadcasted_iota(jnp.int32, (1, LANES), 1)
    gains = jnp.zeros((1, LANES), F32)
    for r in range(3):
        for m in range(4):
            c = 4 * r + m
            turned = pltpu.roll(small[r : r + 1, :], (LANES - 32 * m) % LANES, 1)
            taps_out[c : c + 1, :] = turned[:, :taps]
            gains = jnp.where(spot == c, pltpu.roll(turned, (c - taps) % LANES, 1), gains)
    gain_out[...] = gains[:, :own]


def local(hidden, cotangent, lengths, kernel, conv_gain, w_out):
    groups, frames, double = hidden.shape
    width = double // 2
    half = width // 2
    blocks = width // LANES
    taps = kernel.shape[1]
    seq_count = lax.axis_size("seq")
    devices = lax.axis_size("dp") * seq_count
    own = width // devices
    rows = groups * frames
    span = frames + 2 * HALF_PAD
    length = frames + 2 * PAD
    deep = own * half // LANES
    ends = seq_count - 1
    swap = [(i, i ^ 1) for i in range(seq_count)]
    place = lax.axis_index("seq")
    conv_flops = 2 * taps * rows * width

    spot = place.reshape(1)
    flat = cotangent.reshape(rows, width)
    tail, head = call(
        edges_kernel,
        [SMEM, SMEM, HBM, HBM],
        [shape((groups, PAD + HALF_PAD, width), BF16)] * 2,
        [
            pltpu.VMEM((2, groups, PAD, double), BF16),
            pltpu.VMEM((2, groups, HALF_PAD, width), BF16),
            pltpu.SemaphoreType.DMA((2, 2, groups)),
        ],
        1 << 20,
        4,
    )(lengths, spot, far_memory(hidden), far_memory(cotangent))
    left = lax.ppermute(tail, "seq", [(i, i + 1) for i in range(ends)])
    right = lax.ppermute(head, "seq", [(i + 1, i) for i in range(ends)])
    gated = call(
        gate_kernel, [SMEM, SMEM, VMEM], shape((groups, blocks, length, LANES), F32), [], 8 << 20, 4
    )(lengths, spot, hidden)
    weights = jnp.concatenate([kernel, jnp.zeros((width, 1), F32)], axis=1).T
    gain = conv_gain.reshape(1, width)
    slab, hat, inverse, message = call(
        forward_kernel,
        [SMEM, SMEM] + [VMEM] * 6,
        [
            shape((groups, blocks, length, LANES), F32),
            shape((groups * span, width), F32),
            shape((groups * span, LANES), F32),
            shape((rows, width + half), BF16),
        ],
        [pltpu.VMEM((span, LANES), F32)],
        conv_flops,
        4,
        {2: 0},
    )(lengths, spot, gated, left, right, weights, gain, flat)
    far = lax.ppermute(message, "seq", swap)
    grad, term_conv = call(
        backward_kernel,
        [SMEM, SMEM] + [VMEM] * 7,
        [shape((groups, blocks, span, LANES), F32), shape((1, width), F32)],
        [
            pltpu.VMEM((groups * span, width), BF16),
            pltpu.VMEM((groups * span, width), F32),
            pltpu.VMEM((8, width), F32),
        ],
        2 * rows * width * width,
        10,
    )(lengths, spot, cotangent, left, right, w_out, hat, inverse, gain)
    packed = call(
        terms_kernel,
        [VMEM] * 3,
        shape((devices // 2, 2, 8, LANES), F32),
        [
            pltpu.VMEM((LANES, LANES), F32),
            pltpu.VMEM((width, LANES), F32),
            pltpu.VMEM((width // 4 + 8, LANES), F32),
            pltpu.VMEM((width // 4 + 16, LANES), F32),
        ],
        conv_flops,
        6,
    )(grad, slab, term_conv)
    steps = devices // 32
    pieces = call(
        product_kernel,
        [SMEM] + [VMEM] * 4,
        pltpu.HBM((devices // 2, 2, deep + 8, LANES), BF16),
        [
            pltpu.VMEM((16, 2, deep + 8, LANES), F32),
            pltpu.VMEM((steps, 16, 2, deep + 8, LANES), BF16),
            pltpu.SemaphoreType.DMA((steps,)),
        ],
        4 * rows * width * half,
        10,
        out_specs=HBM,
    )(spot, message, flat, far, packed)
    got = lax.all_to_all(pieces.reshape(devices, deep + 8, LANES), AXES, 0, 0, tiled=True)
    grad_hidden = call(
        input_kernel,
        [SMEM, SMEM] + [VMEM] * 3,
        shape((groups, frames, double), BF16),
        [],
        conv_flops,
        4,
    )(lengths, spot, grad, hidden, weights)

    factor = 1.0 / math.sqrt(groups * lax.axis_size("dp") * frames * seq_count)
    slots = 4
    grad_w, grad_kernel, grad_gain = call(
        functools.partial(sum_kernel, factor),
        [HBM],
        [shape((own, width), F32), shape((own, taps), F32), shape((1, own), F32)],
        [
            pltpu.VMEM((2, deep + 8, LANES), F32),
            pltpu.VMEM((slots, devices // 2 // slots, 2, deep + 8, LANES), BF16),
            pltpu.SemaphoreType.DMA((slots,)),
        ],
        1 << 20,
        6,
    )(far_memory(got.reshape(devices // 2, 2, deep + 8, LANES)))
    return grad_hidden, grad_w, grad_kernel, grad_gain.reshape(own)


def solution(mesh):
    in_specs = (P("dp", "seq", None), P("dp", "seq", None), P("dp"), P(), P(), P())
    out_specs = (P("dp", "seq", None), P(AXES, None), P(AXES, None), P(AXES))
    return jax.shard_map(local, mesh=mesh, in_specs=in_specs, out_specs=out_specs, check_vma=False)
```

```python
import functools
import math

import jax
import jax.numpy as jnp
from jax import lax
from jax.experimental import pallas as pl
from jax.experimental.pallas import tpu as pltpu
from jax.sharding import PartitionSpec as P

EPSILON = 1e-05
AXES = ("dp", "seq")
LANES = 128
HALF_PAD = 16
PAD = 32
TILE = 16
F32, BF16 = jnp.float32, jnp.bfloat16
VMEM = pl.BlockSpec(memory_space=pltpu.VMEM)
SMEM = pl.BlockSpec(memory_space=pltpu.SMEM)
HBM = pl.BlockSpec(memory_space=pltpu.HBM)


def sigmoid(x):
    return 0.5 * jnp.tanh(0.5 * x) + 0.5


def left_of(lengths, place, u, frames):
    return lengths[u] - place[0] * frames


def lane(block):
    return pl.ds(pl.multiple_of(block * LANES, LANES), LANES)


def call(kernel, in_specs, out_shape, scratch, flops, limit, aliases=None, out_specs=None):
    return pl.pallas_call(
        kernel,
        in_specs=in_specs,
        out_specs=out_specs or jax.tree.map(lambda _: VMEM, out_shape),
        out_shape=out_shape,
        scratch_shapes=scratch,
        input_output_aliases=aliases or {},
        cost_estimate=pl.CostEstimate(flops=flops, bytes_accessed=8 << 20, transcendentals=0),
        compiler_params=pltpu.CompilerParams(vmem_limit_bytes=limit << 20),
    )


def shape(dims, dtype):
    return jax.ShapeDtypeStruct(dims, dtype)


def far_memory(array):
    return pltpu.with_memory_space_constraint(array, pltpu.HBM)


def depthwise(slab, weight, start, rows, order):
    total = None
    for j, row in enumerate(order):
        term = slab[pl.ds(start + 1 + j, rows), :] * weight[row]
        total = term if total is None else total + term
    return total


def edges_kernel(hidden, cotangent, tail, head, cells, upstream, arrived):
    groups, frames, double = hidden.shape
    width = double // 2
    copies = []
    for side, (start, near) in enumerate(((frames - PAD, frames - HALF_PAD), (0, 0))):
        for u in range(groups):
            copies.append(
                (
                    pltpu.make_async_copy(
                        hidden.at[u, start : start + PAD], cells.at[side, u], arrived.at[0, side, u]
                    ),
                    pltpu.make_async_copy(
                        cotangent.at[u, near : near + HALF_PAD],
                        upstream.at[side, u],
                        arrived.at[1, side, u],
                    ),
                )
            )
    for first, second in copies:
        first.start()
        second.start()
    n = 0
    for side, out in enumerate((tail, head)):
        for u in range(groups):
            copies[n][0].wait()
            for cb in range(width // LANES):
                here = slice(cb * LANES, (cb + 1) * LANES)
                there = slice(width + cb * LANES, width + (cb + 1) * LANES)
                linear = cells[side, u, :, here].astype(F32)
                gate = sigmoid(cells[side, u, :, there].astype(F32))
                out[u, 0:PAD, here] = (linear * gate).astype(BF16)
            copies[n][1].wait()
            out[u, PAD:, :] = upstream[side, u]
            n += 1


CONTRACT_COLUMNS = (((1,), (1,)), ((), ()))


def gate_kernel(
    lengths, place, hidden, weights, cotangent, source, slab, hat, grad, w_out, arrived
):
    groups, frames, double = hidden.shape
    taps = weights.shape[0] - 1
    width = double // 2
    blocks = width // LANES
    span = frames + 2 * HALF_PAD
    chunk = (span - 2 * PAD) // 2

    def copy(n):
        at = pl.ds(pl.multiple_of(n * 2 * LANES, 2 * LANES), 2 * LANES)
        return pltpu.make_async_copy(source.at[at], w_out.at[at], arrived.at[n])

    for n in range(blocks // 2):
        copy(n).start()

    def pair(n, _):
        at = pl.ds(pl.multiple_of(n * 2 * LANES, 2 * LANES), 2 * LANES)
        copy(n).wait()
        swish = lax.dot_general(
            cotangent[...], w_out[at, :], CONTRACT_COLUMNS, preferred_element_type=F32
        )
        for u in range(groups):
            limit = left_of(lengths, place, u, frames)
            base = u * span
            for cb in (2 * n, 2 * n + 1):
                row = lax.broadcasted_iota(jnp.int32, (frames, LANES), 0)
                linear = hidden[u, :, lane(cb)].astype(F32)
                gate = sigmoid(hidden[u, :, lane(blocks + cb)].astype(F32))
                glu = jnp.where(row < limit, linear * gate, 0.0)
                block = slab.at[u, cb]
                block[PAD : PAD + frames, :] = glu.astype(BF16).astype(F32)
                weight = [weights[j : j + 1, lane(cb)] for j in range(taps)]
                for start in range(PAD, span - PAD, chunk):
                    to = slice(base + start, base + start + chunk)
                    hat[to, lane(cb)] = depthwise(block, weight, start, chunk, range(taps))
        for u in range(groups):
            to = u * span + HALF_PAD
            grad[to : to + frames, at] = swish[u * frames : (u + 1) * frames]
        return 0

    lax.fori_loop(0, blocks // 2, pair, 0)


def row_mean(values, width):
    mean = jnp.sum(values, axis=-1, keepdims=True) * (1.0 / width)
    return jnp.broadcast_to(mean, values.shape)


def forward_kernel(
    lengths,
    place,
    gated,
    inner,
    swish,
    left,
    right,
    weights,
    gain,
    cotangent,
    w_out,
    slab,
    hat,
    grad,
    inverse,
    message,
    mean,
    held,
):
    groups, blocks, length = slab.shape[:3]
    taps = weights.shape[0] - 1
    width = blocks * LANES
    half = width // 2
    frames = length - 2 * PAD
    span = frames + 2 * HALF_PAD
    theirs = pl.ds(pl.multiple_of((1 - (place[0] & 1)) * half, LANES), half)
    message[:, width:] = cotangent[:, theirs]
    for u in range(groups):
        held[2 * u * HALF_PAD : (2 * u + 1) * HALF_PAD, :] = left[u, PAD:, :]
        held[(2 * u + 1) * HALF_PAD : (2 * u + 2) * HALF_PAD, :] = right[u, PAD:, :]

    def pair(n, _):
        at = pl.ds(pl.multiple_of(n * 2 * LANES, 2 * LANES), 2 * LANES)
        result = lax.dot_general(
            held[...], w_out[at, :], CONTRACT_COLUMNS, preferred_element_type=F32
        )
        row = lax.broadcasted_iota(jnp.int32, (PAD, LANES), 0)
        for u in range(groups):
            limit = left_of(lengths, place, u, frames)
            base = u * span
            for cb in (2 * n, 2 * n + 1):
                block = slab.at[u, cb]
                before = left[u, 0:PAD, lane(cb)].astype(F32)
                after = right[u, 0:PAD, lane(cb)].astype(F32)
                block[0:PAD, :] = jnp.where(row - PAD < limit, before, 0.0)
                block[PAD + frames :, :] = jnp.where(row + frames < limit, after, 0.0)
                weight = [weights[j : j + 1, lane(cb)] for j in range(taps)]
                for start in (0, span - PAD):
                    to = slice(base + start, base + start + PAD)
                    hat[to, lane(cb)] = depthwise(block, weight, start, PAD, range(taps))
        for u in range(groups):
            base = u * span
            near = 2 * u * HALF_PAD
            grad[base : base + HALF_PAD, at] = result[near : near + HALF_PAD]
            grad[base + span - HALF_PAD : base + span, at] = result[
                near + HALF_PAD : near + 2 * HALF_PAD
            ]
        return 0

    lax.fori_loop(0, blocks // 2, pair, 0)
    for u in range(groups):
        limit = left_of(lengths, place, u, frames)
        base = u * span
        rows = slice(base, base + span)
        total = hat[rows, 0:LANES]
        for cb in range(1, blocks):
            total = total + hat[rows, cb * LANES : (cb + 1) * LANES]
        mean[...] = row_mean(total, width)
        total = None
        for cb in range(blocks):
            centered = hat[rows, cb * LANES : (cb + 1) * LANES] - mean[...]
            total = centered * centered if total is None else total + centered * centered
        inverse[rows, :] = lax.rsqrt(row_mean(total, width) + EPSILON)

        def normalize(cb, _):
            normed = (hat[rows, lane(cb)] - mean[...]) * inverse[rows, :]
            hat[rows, lane(cb)] = normed
            pre = normed[HALF_PAD : HALF_PAD + frames] * (0.5 * gain[:, lane(cb)])
            out = pre * jnp.tanh(pre) + pre
            row = lax.broadcasted_iota(jnp.int32, (frames, LANES), 0)
            out = jnp.where(row < limit, out, 0.0).astype(BF16)
            message[u * frames : (u + 1) * frames, lane(cb)] = out
            return 0

        lax.fori_loop(0, blocks, normalize, 0)


CONTRACT_ROWS = (((0,), (0,)), ((), ()))


def product_kernel(place, near, cotangent, far, packed, out, scratch, held, sent):
    half = cotangent.shape[1] // 2
    width = 2 * half
    pairs = scratch.shape[0]
    step = 24 * pairs
    deep = scratch.shape[2] - 8
    first = lax.broadcasted_iota(jnp.int32, (pairs, 8, LANES), 1) < 4
    pick = lambda a, b: jnp.where(first, a, b)
    roll = lambda a: pltpu.roll(a, 4, 1)
    mine = pl.ds(pl.multiple_of((place[0] & 1) * half, LANES), half)

    def copy(s):
        return pltpu.make_async_copy(held.at[s], out.at[pl.ds(s * pairs, pairs)], sent.at[s])

    def rows(s, _):
        at = pl.ds(pl.multiple_of(s * step, step), step)
        result = lax.dot_general(
            near[:, at], cotangent[:, mine], CONTRACT_ROWS, preferred_element_type=F32
        ) + lax.dot_general(far[:, at], far[:, width:], CONTRACT_ROWS, preferred_element_type=F32)

        def parts(k):
            cut = result[:, k * LANES : (k + 1) * LANES].reshape(pairs, 3, 8, LANES)
            return cut[:, 0], cut[:, 1], cut[:, 2]

        for q in range(half // LANES // 2):
            a, b, c = parts(2 * q)
            d, e, f = parts(2 * q + 1)
            rb, rc, rd = roll(b), roll(c), roll(d)
            even = (a, pick(b, rd), pick(rd, roll(e)))
            odd = (pick(rb, rc), pick(rc, e), f)
            for side, tiles in enumerate((even, odd)):
                for i, tile in enumerate(tiles):
                    scratch[:, side, 24 * q + 8 * i : 24 * q + 8 * i + 8, :] = tile
        scratch[:, :, deep:, :] = packed[pl.ds(s * pairs, pairs)]
        held[s] = scratch[...].astype(BF16)
        copy(s).start()
        return 0

    lax.fori_loop(0, width // step, rows, 0)
    for s in range(width // step):
        copy(s).wait()


def backward_kernel(lengths, place, grad, hat, inverse, gain, slab, term, work, sums):
    groups, blocks, span = slab.shape[:3]
    width = blocks * LANES
    frames = span - 2 * HALF_PAD
    sums[...] = jnp.zeros_like(sums)
    part = span // 2

    def norm(n, _):
        u, start = n // 2, (n % 2) * part
        at = pl.ds(pl.multiple_of(n * part, TILE), part)
        limit = left_of(lengths, place, u, frames)
        row = start - HALF_PAD + lax.broadcasted_iota(jnp.int32, (part, LANES), 0)
        keep = row < limit
        inside = (row >= 0) & (row < frames)
        first = second = None
        for cb in range(blocks):
            here = slice(cb * LANES, (cb + 1) * LANES)
            normed = hat[at, here]
            halved = normed * (0.5 * gain[:, here])
            turn = jnp.tanh(halved)
            gate = 0.5 * turn + 0.5
            grad_pre = jnp.where(keep, grad[at, here], 0.0) * (gate * (1.0 + halved * (1.0 - turn)))
            term_part = jnp.where(inside, grad_pre * normed, 0.0)
            sums[:, here] += jnp.sum(term_part.reshape(part // 8, 8, LANES), axis=0)
            scaled = grad_pre * gain[:, here]
            work[at, here] = scaled
            first = scaled if first is None else first + scaled
            second = scaled * normed if second is None else second + scaled * normed
        mean = row_mean(first, width)
        slope = row_mean(second, width)
        inv = inverse[at, :]
        for cb in range(blocks):
            here = slice(cb * LANES, (cb + 1) * LANES)
            result = inv * (work[at, here] - mean - hat[at, here] * slope)
            to = pl.ds(pl.multiple_of(start, TILE), part)
            slab[u, cb, to, :] = result.astype(BF16).astype(F32)
        return 0

    lax.fori_loop(0, 2 * groups, norm, 0)
    term[...] = jnp.sum(sums[...], axis=0, keepdims=True)


def terms_kernel(grad, slab, term, packed, square, columns, rounded, rest):
    groups, blocks, span = grad.shape[:3]
    frames = span - 2 * HALF_PAD
    taps = 31
    square[...] = jnp.zeros_like(square)

    def channel(cb, _):
        for r in range(8):
            chosen = [j for j in range(r, taps, 8)]
            totals = [None] * len(chosen)
            for u in range(groups):
                for i in range(frames // 8):
                    value = grad[u, cb, HALF_PAD + 8 * i : HALF_PAD + 8 * i + 8, :]
                    for n, j in enumerate(chosen):
                        place = PAD - taps // 2 + 8 * i + j
                        part = value * slab[u, cb, pl.ds(place, 8), :]
                        totals[n] = part if totals[n] is None else totals[n] + part
            for n, j in enumerate(chosen):
                square[j : j + 1, :] = jnp.sum(totals[n], axis=0, keepdims=True)
        square[taps : taps + 1, :] = term[:, lane(cb)]
        columns[lane(cb), :] = square[...].T
        return 0

    lax.fori_loop(0, blocks, channel, 0)
    quarter = columns.shape[0] // 4
    total = columns[pl.ds(0, quarter, stride=4), :]
    for m in range(1, 4):
        total = total + pltpu.roll(columns[pl.ds(m, quarter, stride=4), :], 32 * m, 1)
    high = total.astype(BF16).astype(F32)
    rounded[0:quarter, :] = high
    rest[8 : 8 + quarter, :] = total - high
    row = lax.broadcasted_iota(jnp.int32, (8, LANES), 0)
    pairs, sides = packed.shape[:2]
    for d in range(pairs * sides):
        upper = rounded[3 * d : 3 * d + 8, :]
        lower = rest[3 * d + 5 : 3 * d + 13, :]
        tile = jnp.where(row < 3, upper, jnp.where(row < 6, lower, 0.0))
        packed[d // 2, d % 2] = tile


def input_kernel(lengths, place, grad, hidden, weights, out):
    groups, frames, _ = hidden.shape
    blocks = grad.shape[1]
    taps = weights.shape[0] - 1
    chunk = 64
    for u in range(groups):
        limit = left_of(lengths, place, u, frames)

        def channel(cb, _):
            block = grad.at[u, cb]
            weight = [weights[j : j + 1, lane(cb)] for j in range(taps)]
            for start in range(0, frames, chunk):
                at = slice(start, start + chunk)
                total = depthwise(block, weight, start, chunk, range(taps - 1, -1, -1))
                row = start + lax.broadcasted_iota(jnp.int32, (chunk, LANES), 0)
                total = jnp.where(row < limit, total, 0.0)
                linear = hidden[u, at, lane(cb)].astype(F32)
                gate = sigmoid(hidden[u, at, lane(blocks + cb)].astype(F32))
                opened = total * gate
                out[u, at, lane(cb)] = opened.astype(BF16)
                out[u, at, lane(blocks + cb)] = (opened * linear * (1.0 - gate)).astype(BF16)
            return 0

        lax.fori_loop(0, blocks, channel, 0)


def sum_kernel(factor, got, out, taps_out, gain_out, total, held, arrived):
    own = out.shape[0]
    slots, step, _, tall, _ = held.shape

    def copy(i):
        return pltpu.make_async_copy(got.at[pl.ds(i * step, step)], held.at[i], arrived.at[i])

    for i in range(slots):
        copy(i).start()
    total[...] = jnp.zeros_like(total)

    def add(i, _):
        copy(i).wait()
        for k in range(0, step, 4):
            total[...] += jnp.sum(held[i, k : k + 4].astype(F32), axis=0)
        return 0

    lax.fori_loop(0, slots, add, 0)
    deep = tall - 8
    blocks = deep // own
    for side in range(2):
        for k in range(blocks):
            at = (side * blocks + k) * LANES
            out[:, at : at + LANES] = total[side, own * k : own * (k + 1), :] * factor
    both = total[0, deep:, :] + total[1, deep:, :]
    small = (both[0:3] + both[3:6]) * factor
    taps = taps_out.shape[1]
    spot = lax.broadcasted_iota(jnp.int32, (1, LANES), 1)
    gains = jnp.zeros((1, LANES), F32)
    for r in range(3):
        for m in range(4):
            c = 4 * r + m
            turned = pltpu.roll(small[r : r + 1, :], (LANES - 32 * m) % LANES, 1)
            taps_out[c : c + 1, :] = turned[:, :taps]
            gains = jnp.where(spot == c, pltpu.roll(turned, (c - taps) % LANES, 1), gains)
    gain_out[...] = gains[:, :own]


def local(hidden, cotangent, lengths, kernel, conv_gain, w_out):
    groups, frames, double = hidden.shape
    width = double // 2
    half = width // 2
    blocks = width // LANES
    taps = kernel.shape[1]
    seq_count = lax.axis_size("seq")
    devices = lax.axis_size("dp") * seq_count
    own = width // devices
    rows = groups * frames
    span = frames + 2 * HALF_PAD
    length = frames + 2 * PAD
    deep = own * half // LANES
    ends = seq_count - 1
    swap = [(i, i ^ 1) for i in range(seq_count)]
    place = lax.axis_index("seq")
    conv_flops = 2 * taps * rows * width

    spot = place.reshape(1)
    flat = cotangent.reshape(rows, width)
    tail, head = call(
        edges_kernel,
        [HBM, HBM],
        [shape((groups, PAD + HALF_PAD, width), BF16)] * 2,
        [
            pltpu.VMEM((2, groups, PAD, double), BF16),
            pltpu.VMEM((2, groups, HALF_PAD, width), BF16),
            pltpu.SemaphoreType.DMA((2, 2, groups)),
        ],
        1 << 20,
        4,
    )(far_memory(hidden), far_memory(cotangent))
    left = lax.ppermute(tail, "seq", [(i, i + 1) for i in range(ends)])
    right = lax.ppermute(head, "seq", [(i + 1, i) for i in range(ends)])
    weights = jnp.concatenate([kernel, jnp.zeros((width, 1), F32)], axis=1).T
    gain = conv_gain.reshape(1, width)
    slab_shape = shape((groups, blocks, length, LANES), F32)
    wide_shape = shape((groups * span, width), F32)
    gated, inner, swish, w_near = call(
        gate_kernel,
        [SMEM, SMEM] + [VMEM] * 3 + [HBM],
        [slab_shape, wide_shape, wide_shape, shape((width, width), BF16)],
        [pltpu.SemaphoreType.DMA((blocks // 2,))],
        conv_flops,
        4,
    )(lengths, spot, hidden, weights, flat, far_memory(w_out))
    slab, hat, grad_swish, inverse, message = call(
        forward_kernel,
        [SMEM, SMEM] + [VMEM] * 9,
        [
            slab_shape,
            wide_shape,
            wide_shape,
            shape((groups * span, LANES), F32),
            shape((rows, width + half), BF16),
        ],
        [pltpu.VMEM((span, LANES), F32), pltpu.VMEM((2 * groups * HALF_PAD, width), BF16)],
        conv_flops,
        4,
        {2: 0, 3: 1, 4: 2},
    )(lengths, spot, gated, inner, swish, left, right, weights, gain, flat, w_near)
    far = lax.ppermute(message, "seq", swap)
    grad, term_conv = call(
        backward_kernel,
        [SMEM, SMEM] + [VMEM] * 4,
        [shape((groups, blocks, span, LANES), F32), shape((1, width), F32)],
        [pltpu.VMEM((groups * span, width), F32), pltpu.VMEM((8, width), F32)],
        20 * rows * width,
        6,
    )(lengths, spot, grad_swish, hat, inverse, gain)
    packed = call(
        terms_kernel,
        [VMEM] * 3,
        shape((devices // 2, 2, 8, LANES), F32),
        [
            pltpu.VMEM((LANES, LANES), F32),
            pltpu.VMEM((width, LANES), F32),
            pltpu.VMEM((width // 4 + 8, LANES), F32),
            pltpu.VMEM((width // 4 + 16, LANES), F32),
        ],
        conv_flops,
        6,
    )(grad, slab, term_conv)
    steps = devices // 32
    pieces = call(
        product_kernel,
        [SMEM] + [VMEM] * 4,
        pltpu.HBM((devices // 2, 2, deep + 8, LANES), BF16),
        [
            pltpu.VMEM((16, 2, deep + 8, LANES), F32),
            pltpu.VMEM((steps, 16, 2, deep + 8, LANES), BF16),
            pltpu.SemaphoreType.DMA((steps,)),
        ],
        4 * rows * width * half,
        10,
        out_specs=HBM,
    )(spot, message, flat, far, packed)
    got = lax.all_to_all(pieces.reshape(devices, deep + 8, LANES), AXES, 0, 0, tiled=True)
    grad_hidden = call(
        input_kernel,
        [SMEM, SMEM] + [VMEM] * 3,
        shape((groups, frames, double), BF16),
        [],
        conv_flops,
        4,
    )(lengths, spot, grad, hidden, weights)

    factor = 1.0 / math.sqrt(groups * lax.axis_size("dp") * frames * seq_count)
    slots = 4
    grad_w, grad_kernel, grad_gain = call(
        functools.partial(sum_kernel, factor),
        [HBM],
        [shape((own, width), F32), shape((own, taps), F32), shape((1, own), F32)],
        [
            pltpu.VMEM((2, deep + 8, LANES), F32),
            pltpu.VMEM((slots, devices // 2 // slots, 2, deep + 8, LANES), BF16),
            pltpu.SemaphoreType.DMA((slots,)),
        ],
        1 << 20,
        6,
    )(far_memory(got.reshape(devices // 2, 2, deep + 8, LANES)))
    return grad_hidden, grad_w, grad_kernel, grad_gain.reshape(own)


def solution(mesh):
    in_specs = (P("dp", "seq", None), P("dp", "seq", None), P("dp"), P(), P(), P())
    out_specs = (P("dp", "seq", None), P(AXES, None), P(AXES, None), P(AXES))
    return jax.shard_map(local, mesh=mesh, in_specs=in_specs, out_specs=out_specs, check_vma=False)
```

```python
import functools
import math

import jax
import jax.numpy as jnp
from jax import lax
from jax.experimental import pallas as pl
from jax.experimental.pallas import tpu as pltpu
from jax.sharding import PartitionSpec as P

EPSILON = 1e-05
AXES = ("dp", "seq")
LANES = 128
HALF_PAD = 16
PAD = 32
TILE = 16
F32, BF16 = jnp.float32, jnp.bfloat16
VMEM = pl.BlockSpec(memory_space=pltpu.VMEM)
SMEM = pl.BlockSpec(memory_space=pltpu.SMEM)
HBM = pl.BlockSpec(memory_space=pltpu.HBM)


def sigmoid(x):
    return 0.5 * jnp.tanh(0.5 * x) + 0.5


def left_of(lengths, place, u, frames):
    return lengths[u] - place[0] * frames


def lane(block):
    return pl.ds(pl.multiple_of(block * LANES, LANES), LANES)


def call(kernel, in_specs, out_shape, scratch, flops, limit, aliases=None, out_specs=None):
    return pl.pallas_call(
        kernel,
        in_specs=in_specs,
        out_specs=out_specs or jax.tree.map(lambda _: VMEM, out_shape),
        out_shape=out_shape,
        scratch_shapes=scratch,
        input_output_aliases=aliases or {},
        cost_estimate=pl.CostEstimate(flops=flops, bytes_accessed=8 << 20, transcendentals=0),
        compiler_params=pltpu.CompilerParams(vmem_limit_bytes=limit << 20),
    )


def shape(dims, dtype):
    return jax.ShapeDtypeStruct(dims, dtype)


def far_memory(array):
    return pltpu.with_memory_space_constraint(array, pltpu.HBM)


def depthwise(slab, weight, start, rows, order):
    total = None
    for j, row in enumerate(order):
        term = slab[pl.ds(start + 1 + j, rows), :] * weight[row]
        total = term if total is None else total + term
    return total


def edges_kernel(
    place, hidden, cotangent, source, inside, across, weights, cells, upstream, arrived, loaded
):
    groups, frames, double = hidden.shape
    width = double // 2
    core = place[0] & 1
    copies = []
    for side, last in enumerate((core, 1 - core)):
        start = pl.multiple_of(last * (frames - PAD), TILE)
        near = pl.multiple_of(last * (frames - HALF_PAD), TILE)
        for u in range(groups):
            copies.append(
                (
                    pltpu.make_async_copy(
                        hidden.at[u, pl.ds(start, PAD)], cells.at[side, u], arrived.at[0, side, u]
                    ),
                    pltpu.make_async_copy(
                        cotangent.at[u, pl.ds(near, HALF_PAD)],
                        upstream.at[side, u],
                        arrived.at[1, side, u],
                    ),
                )
            )
    for first, second in copies:
        first.start()
        second.start()
    taps = pltpu.make_async_copy(source, weights, loaded)
    taps.start()
    n = 0
    for side, out in enumerate((across, inside)):
        for u in range(groups):
            copies[n][0].wait()
            for cb in range(width // LANES):
                here = slice(cb * LANES, (cb + 1) * LANES)
                there = slice(width + cb * LANES, width + (cb + 1) * LANES)
                linear = cells[side, u, :, here].astype(F32)
                gate = sigmoid(cells[side, u, :, there].astype(F32))
                out[u, 0:PAD, here] = (linear * gate).astype(BF16)
            copies[n][1].wait()
            out[u, PAD:, :] = upstream[side, u]
            n += 1
    taps.wait()


CONTRACT_COLUMNS = (((1,), (1,)), ((), ()))


def gate_kernel(
    lengths, place, hidden, weights, cotangent, source, slab, hat, grad, w_out, arrived
):
    groups, frames, double = hidden.shape
    taps = weights.shape[0]
    width = double // 2
    blocks = width // LANES
    span = frames + 2 * HALF_PAD
    chunk = (span - 2 * PAD) // 2

    def copy(n):
        at = pl.ds(pl.multiple_of(n * 2 * LANES, 2 * LANES), 2 * LANES)
        return pltpu.make_async_copy(source.at[at], w_out.at[at], arrived.at[n])

    for n in range(blocks // 2):
        copy(n).start()

    def pair(n, _):
        at = pl.ds(pl.multiple_of(n * 2 * LANES, 2 * LANES), 2 * LANES)
        copy(n).wait()
        swish = lax.dot_general(
            cotangent[...], w_out[at, :], CONTRACT_COLUMNS, preferred_element_type=F32
        )
        for u in range(groups):
            limit = left_of(lengths, place, u, frames)
            base = u * span
            for cb in (2 * n, 2 * n + 1):
                row = lax.broadcasted_iota(jnp.int32, (frames, LANES), 0)
                linear = hidden[u, :, lane(cb)].astype(F32)
                gate = sigmoid(hidden[u, :, lane(blocks + cb)].astype(F32))
                glu = jnp.where(row < limit, linear * gate, 0.0)
                block = slab.at[u, cb]
                block[PAD : PAD + frames, :] = glu.astype(BF16).astype(F32)
                weight = [weights[j : j + 1, lane(cb)] for j in range(taps)]
                for start in range(PAD, span - PAD, chunk):
                    to = slice(base + start, base + start + chunk)
                    hat[to, lane(cb)] = depthwise(block, weight, start, chunk, range(taps))
        for u in range(groups):
            to = u * span + HALF_PAD
            grad[to : to + frames, at] = swish[u * frames : (u + 1) * frames]
        return 0

    lax.fori_loop(0, blocks // 2, pair, 0)


def row_mean(values, width):
    mean = jnp.sum(values, axis=-1, keepdims=True) * (1.0 / width)
    return jnp.broadcast_to(mean, values.shape)


def forward_kernel(
    lengths,
    place,
    gated,
    inner,
    swish,
    inside,
    across,
    weights,
    gain,
    cotangent,
    w_out,
    slab,
    hat,
    grad,
    inverse,
    message,
    mean,
    held,
):
    groups, blocks, length = slab.shape[:3]
    taps = weights.shape[0]
    width = blocks * LANES
    half = width // 2
    frames = length - 2 * PAD
    span = frames + 2 * HALF_PAD
    theirs = pl.ds(pl.multiple_of((1 - (place[0] & 1)) * half, LANES), half)
    message[:, width:] = cotangent[:, theirs]
    first = (place[0] & 1) == 0

    def sides(u, rows, lanes):
        one, two = inside[u, rows, lanes].astype(F32), across[u, rows, lanes].astype(F32)
        return jnp.where(first, two, one), jnp.where(first, one, two)

    for u in range(groups):
        left, right = sides(u, slice(PAD, PAD + HALF_PAD), slice(0, width))
        held[2 * u * HALF_PAD : (2 * u + 1) * HALF_PAD, :] = left.astype(BF16)
        held[(2 * u + 1) * HALF_PAD : (2 * u + 2) * HALF_PAD, :] = right.astype(BF16)

    def pair(n, _):
        at = pl.ds(pl.multiple_of(n * 2 * LANES, 2 * LANES), 2 * LANES)
        result = lax.dot_general(
            held[...], w_out[at, :], CONTRACT_COLUMNS, preferred_element_type=F32
        )
        row = lax.broadcasted_iota(jnp.int32, (PAD, LANES), 0)
        for u in range(groups):
            limit = left_of(lengths, place, u, frames)
            base = u * span
            for cb in (2 * n, 2 * n + 1):
                block = slab.at[u, cb]
                before, after = sides(u, slice(0, PAD), lane(cb))
                block[0:PAD, :] = jnp.where(row - PAD < limit, before, 0.0)
                block[PAD + frames :, :] = jnp.where(row + frames < limit, after, 0.0)
                weight = [weights[j : j + 1, lane(cb)] for j in range(taps)]
                for start in (0, span - PAD):
                    to = slice(base + start, base + start + PAD)
                    hat[to, lane(cb)] = depthwise(block, weight, start, PAD, range(taps))
        for u in range(groups):
            base = u * span
            near = 2 * u * HALF_PAD
            grad[base : base + HALF_PAD, at] = result[near : near + HALF_PAD]
            grad[base + span - HALF_PAD : base + span, at] = result[
                near + HALF_PAD : near + 2 * HALF_PAD
            ]
        return 0

    lax.fori_loop(0, blocks // 2, pair, 0)
    for u in range(groups):
        limit = left_of(lengths, place, u, frames)
        base = u * span
        rows = slice(base, base + span)
        total = hat[rows, 0:LANES]
        for cb in range(1, blocks):
            total = total + hat[rows, cb * LANES : (cb + 1) * LANES]
        mean[...] = row_mean(total, width)
        total = None
        for cb in range(blocks):
            centered = hat[rows, cb * LANES : (cb + 1) * LANES] - mean[...]
            total = centered * centered if total is None else total + centered * centered
        inverse[rows, :] = lax.rsqrt(row_mean(total, width) + EPSILON)

        def normalize(cb, _):
            normed = (hat[rows, lane(cb)] - mean[...]) * inverse[rows, :]
            hat[rows, lane(cb)] = normed
            pre = normed[HALF_PAD : HALF_PAD + frames] * (0.5 * gain[:, lane(cb)])
            out = pre * jnp.tanh(pre) + pre
            row = lax.broadcasted_iota(jnp.int32, (frames, LANES), 0)
            out = jnp.where(row < limit, out, 0.0).astype(BF16)
            message[u * frames : (u + 1) * frames, lane(cb)] = out
            return 0

        lax.fori_loop(0, blocks, normalize, 0)


CONTRACT_ROWS = (((0,), (0,)), ((), ()))


CONTRACT_ROWS = (((0,), (0,)), ((), ()))


def product_kernel(place, near, cotangent, far, packed, out, scratch, held, sent):
    half = cotangent.shape[1] // 2
    width = 2 * half
    pairs = scratch.shape[0]
    step = 24 * pairs
    deep = scratch.shape[2] - 8
    first = lax.broadcasted_iota(jnp.int32, (pairs, 8, LANES), 1) < 4
    pick = lambda a, b: jnp.where(first, a, b)
    roll = lambda a: pltpu.roll(a, 4, 1)
    mine = pl.ds(pl.multiple_of((place[0] & 1) * half, LANES), half)

    def copy(s):
        return pltpu.make_async_copy(held.at[s], out.at[pl.ds(s * pairs, pairs)], sent.at[s])

    def rows(s, _):
        at = pl.ds(pl.multiple_of(s * step, step), step)
        result = lax.dot_general(
            near[:, at], cotangent[:, mine], CONTRACT_ROWS, preferred_element_type=F32
        ) + lax.dot_general(far[:, at], far[:, width:], CONTRACT_ROWS, preferred_element_type=F32)

        def parts(k):
            cut = result[:, k * LANES : (k + 1) * LANES].reshape(pairs, 3, 8, LANES)
            return cut[:, 0], cut[:, 1], cut[:, 2]

        for q in range(half // LANES // 2):
            a, b, c = parts(2 * q)
            d, e, f = parts(2 * q + 1)
            rb, rc, rd = roll(b), roll(c), roll(d)
            even = (a, pick(b, rd), pick(rd, roll(e)))
            odd = (pick(rb, rc), pick(rc, e), f)
            for side, tiles in enumerate((even, odd)):
                for i, tile in enumerate(tiles):
                    scratch[:, side, 24 * q + 8 * i : 24 * q + 8 * i + 8, :] = tile
        scratch[:, :, deep:, :] = packed[pl.ds(s * pairs, pairs)]
        held[s] = scratch[...].astype(BF16)
        copy(s).start()
        return 0

    lax.fori_loop(0, width // step, rows, 0)
    for s in range(width // step):
        copy(s).wait()


def backward_kernel(lengths, place, grad, hat, inverse, gain, slab, term, work, sums):
    groups, blocks, span = slab.shape[:3]
    width = blocks * LANES
    frames = span - 2 * HALF_PAD
    sums[...] = jnp.zeros_like(sums)
    part = span // 2

    def norm(n, _):
        u, start = n // 2, (n % 2) * part
        at = pl.ds(pl.multiple_of(n * part, TILE), part)
        limit = left_of(lengths, place, u, frames)
        row = start - HALF_PAD + lax.broadcasted_iota(jnp.int32, (part, LANES), 0)
        keep = row < limit
        inside = (row >= 0) & (row < frames)
        first = second = None
        for cb in range(blocks):
            here = slice(cb * LANES, (cb + 1) * LANES)
            normed = hat[at, here]
            halved = normed * (0.5 * gain[:, here])
            turn = jnp.tanh(halved)
            gate = 0.5 * turn + 0.5
            grad_pre = jnp.where(keep, grad[at, here], 0.0) * (gate * (1.0 + halved * (1.0 - turn)))
            term_part = jnp.where(inside, grad_pre * normed, 0.0)
            sums[:, here] += jnp.sum(term_part.reshape(part // 8, 8, LANES), axis=0)
            scaled = grad_pre * gain[:, here]
            work[at, here] = scaled
            first = scaled if first is None else first + scaled
            second = scaled * normed if second is None else second + scaled * normed
        mean = row_mean(first, width)
        slope = row_mean(second, width)
        inv = inverse[at, :]
        for cb in range(blocks):
            here = slice(cb * LANES, (cb + 1) * LANES)
            result = inv * (work[at, here] - mean - hat[at, here] * slope)
            to = pl.ds(pl.multiple_of(start, TILE), part)
            slab[u, cb, to, :] = result.astype(BF16).astype(F32)
        return 0

    lax.fori_loop(0, 2 * groups, norm, 0)
    term[...] = jnp.sum(sums[...], axis=0, keepdims=True)


def terms_kernel(grad, slab, term, packed, square, columns, rounded, rest):
    groups, blocks, span = grad.shape[:3]
    frames = span - 2 * HALF_PAD
    taps = 31
    square[...] = jnp.zeros_like(square)

    def channel(cb, _):
        for r in range(8):
            chosen = [j for j in range(r, taps, 8)]
            totals = [None] * len(chosen)
            for u in range(groups):
                for i in range(frames // 8):
                    value = grad[u, cb, HALF_PAD + 8 * i : HALF_PAD + 8 * i + 8, :]
                    for n, j in enumerate(chosen):
                        place = PAD - taps // 2 + 8 * i + j
                        part = value * slab[u, cb, pl.ds(place, 8), :]
                        totals[n] = part if totals[n] is None else totals[n] + part
            for n, j in enumerate(chosen):
                square[j : j + 1, :] = jnp.sum(totals[n], axis=0, keepdims=True)
        square[taps : taps + 1, :] = term[:, lane(cb)]
        columns[lane(cb), :] = square[...].T
        return 0

    lax.fori_loop(0, blocks, channel, 0)
    quarter = columns.shape[0] // 4
    total = columns[pl.ds(0, quarter, stride=4), :]
    for m in range(1, 4):
        total = total + pltpu.roll(columns[pl.ds(m, quarter, stride=4), :], 32 * m, 1)
    high = total.astype(BF16).astype(F32)
    rounded[0:quarter, :] = high
    rest[8 : 8 + quarter, :] = total - high
    row = lax.broadcasted_iota(jnp.int32, (8, LANES), 0)
    pairs, sides = packed.shape[:2]
    for d in range(pairs * sides):
        upper = rounded[3 * d : 3 * d + 8, :]
        lower = rest[3 * d + 5 : 3 * d + 13, :]
        tile = jnp.where(row < 3, upper, jnp.where(row < 6, lower, 0.0))
        packed[d // 2, d % 2] = tile


def input_kernel(lengths, place, grad, hidden, weights, out):
    groups, frames, _ = hidden.shape
    blocks = grad.shape[1]
    taps = weights.shape[0]
    chunk = 64
    for u in range(groups):
        limit = left_of(lengths, place, u, frames)

        def channel(cb, _):
            block = grad.at[u, cb]
            weight = [weights[j : j + 1, lane(cb)] for j in range(taps)]
            for start in range(0, frames, chunk):
                at = slice(start, start + chunk)
                total = depthwise(block, weight, start, chunk, range(taps - 1, -1, -1))
                row = start + lax.broadcasted_iota(jnp.int32, (chunk, LANES), 0)
                total = jnp.where(row < limit, total, 0.0)
                linear = hidden[u, at, lane(cb)].astype(F32)
                gate = sigmoid(hidden[u, at, lane(blocks + cb)].astype(F32))
                opened = total * gate
                out[u, at, lane(cb)] = opened.astype(BF16)
                out[u, at, lane(blocks + cb)] = (opened * linear * (1.0 - gate)).astype(BF16)
            return 0

        lax.fori_loop(0, blocks, channel, 0)


def sum_kernel(factor, got, out, taps_out, gain_out, total, held, arrived):
    own = out.shape[0]
    slots, step, _, tall, _ = held.shape

    def copy(i):
        return pltpu.make_async_copy(got.at[pl.ds(i * step, step)], held.at[i], arrived.at[i])

    for i in range(slots):
        copy(i).start()
    total[...] = jnp.zeros_like(total)

    def add(i, _):
        copy(i).wait()
        for k in range(0, step, 4):
            total[...] += jnp.sum(held[i, k : k + 4].astype(F32), axis=0)
        return 0

    lax.fori_loop(0, slots, add, 0)
    deep = tall - 8
    blocks = deep // own
    for side in range(2):
        for k in range(blocks):
            at = (side * blocks + k) * LANES
            out[:, at : at + LANES] = total[side, own * k : own * (k + 1), :] * factor
    both = total[0, deep:, :] + total[1, deep:, :]
    small = (both[0:3] + both[3:6]) * factor
    taps = taps_out.shape[1]
    spot = lax.broadcasted_iota(jnp.int32, (1, LANES), 1)
    gains = jnp.zeros((1, LANES), F32)
    for r in range(3):
        for m in range(4):
            c = 4 * r + m
            turned = pltpu.roll(small[r : r + 1, :], (LANES - 32 * m) % LANES, 1)
            taps_out[c : c + 1, :] = turned[:, :taps]
            gains = jnp.where(spot == c, pltpu.roll(turned, (c - taps) % LANES, 1), gains)
    gain_out[...] = gains[:, :own]


def local(hidden, cotangent, lengths, kernel, conv_gain, w_out):
    groups, frames, double = hidden.shape
    width = double // 2
    half = width // 2
    blocks = width // LANES
    taps = kernel.shape[1]
    seq_count = lax.axis_size("seq")
    devices = lax.axis_size("dp") * seq_count
    own = width // devices
    rows = groups * frames
    span = frames + 2 * HALF_PAD
    length = frames + 2 * PAD
    deep = own * half // LANES
    ends = seq_count - 1
    swap = [(i, i ^ 1) for i in range(seq_count)]
    place = lax.axis_index("seq")
    conv_flops = 2 * taps * rows * width

    spot = place.reshape(1)
    flat = cotangent.reshape(rows, width)
    inner_edge, outer_edge, weights = call(
        edges_kernel,
        [SMEM, HBM, HBM, HBM],
        [shape((groups, PAD + HALF_PAD, width), BF16)] * 2 + [shape((taps, width), F32)],
        [
            pltpu.VMEM((2, groups, PAD, double), BF16),
            pltpu.VMEM((2, groups, HALF_PAD, width), BF16),
            pltpu.SemaphoreType.DMA((2, 2, groups)),
            pltpu.SemaphoreType.DMA,
        ],
        1 << 20,
        4,
    )(spot, far_memory(hidden), far_memory(cotangent), far_memory(kernel.T))
    bridge = [(i, i + 1) for i in range(1, ends, 2)]
    across = lax.ppermute(outer_edge, "seq", bridge + [(j, i) for i, j in bridge])
    inside = lax.ppermute(inner_edge, "seq", swap)
    gain = conv_gain.reshape(1, width)
    slab_shape = shape((groups, blocks, length, LANES), F32)
    wide_shape = shape((groups * span, width), F32)
    gated, inner, swish, w_near = call(
        gate_kernel,
        [SMEM, SMEM] + [VMEM] * 3 + [HBM],
        [slab_shape, wide_shape, wide_shape, shape((width, width), BF16)],
        [pltpu.SemaphoreType.DMA((blocks // 2,))],
        conv_flops,
        4,
    )(lengths, spot, hidden, weights, flat, far_memory(w_out))
    slab, hat, grad_swish, inverse, message = call(
        forward_kernel,
        [SMEM, SMEM] + [VMEM] * 9,
        [
            slab_shape,
            wide_shape,
            wide_shape,
            shape((groups * span, LANES), F32),
            shape((rows, width + half), BF16),
        ],
        [pltpu.VMEM((span, LANES), F32), pltpu.VMEM((2 * groups * HALF_PAD, width), BF16)],
        conv_flops,
        4,
        {2: 0, 3: 1, 4: 2},
    )(lengths, spot, gated, inner, swish, inside, across, weights, gain, flat, w_near)
    far = lax.ppermute(message, "seq", swap)
    grad, term_conv = call(
        backward_kernel,
        [SMEM, SMEM] + [VMEM] * 4,
        [shape((groups, blocks, span, LANES), F32), shape((1, width), F32)],
        [pltpu.VMEM((groups * span, width), F32), pltpu.VMEM((8, width), F32)],
        20 * rows * width,
        6,
    )(lengths, spot, grad_swish, hat, inverse, gain)
    packed = call(
        terms_kernel,
        [VMEM] * 3,
        shape((devices // 2, 2, 8, LANES), F32),
        [
            pltpu.VMEM((LANES, LANES), F32),
            pltpu.VMEM((width, LANES), F32),
            pltpu.VMEM((width // 4 + 8, LANES), F32),
            pltpu.VMEM((width // 4 + 16, LANES), F32),
        ],
        conv_flops,
        6,
    )(grad, slab, term_conv)
    steps = devices // 32
    pieces = call(
        product_kernel,
        [SMEM] + [VMEM] * 4,
        pltpu.HBM((devices // 2, 2, deep + 8, LANES), BF16),
        [
            pltpu.VMEM((16, 2, deep + 8, LANES), F32),
            pltpu.VMEM((steps, 16, 2, deep + 8, LANES), BF16),
            pltpu.SemaphoreType.DMA((steps,)),
        ],
        4 * rows * width * half,
        10,
        out_specs=HBM,
    )(spot, message, flat, far, packed)
    got = lax.all_to_all(pieces.reshape(devices, deep + 8, LANES), AXES, 0, 0, tiled=True)
    grad_hidden = call(
        input_kernel,
        [SMEM, SMEM] + [VMEM] * 3,
        shape((groups, frames, double), BF16),
        [],
        conv_flops,
        4,
    )(lengths, spot, grad, hidden, weights)

    factor = 1.0 / math.sqrt(groups * lax.axis_size("dp") * frames * seq_count)
    slots = 4
    grad_w, grad_kernel, grad_gain = call(
        functools.partial(sum_kernel, factor),
        [HBM],
        [shape((own, width), F32), shape((own, taps), F32), shape((1, own), F32)],
        [
            pltpu.VMEM((2, deep + 8, LANES), F32),
            pltpu.VMEM((slots, devices // 2 // slots, 2, deep + 8, LANES), BF16),
            pltpu.SemaphoreType.DMA((slots,)),
        ],
        1 << 20,
        6,
    )(far_memory(got.reshape(devices // 2, 2, deep + 8, LANES)))
    return grad_hidden, grad_w, grad_kernel, grad_gain.reshape(own)


def solution(mesh):
    in_specs = (P("dp", "seq", None), P("dp", "seq", None), P("dp"), P(), P(), P())
    out_specs = (P("dp", "seq", None), P(AXES, None), P(AXES, None), P(AXES))
    return jax.shard_map(local, mesh=mesh, in_specs=in_specs, out_specs=out_specs, check_vma=False)
```

```python
import functools
import math

import jax
import jax.numpy as jnp
from jax import lax
from jax.experimental import pallas as pl
from jax.experimental.pallas import tpu as pltpu
from jax.sharding import PartitionSpec as P

EPSILON = 1e-05
AXES = ("dp", "seq")
LANES = 128
HALF_PAD = 16
PAD = 32
TILE = 16
F32, BF16 = jnp.float32, jnp.bfloat16
VMEM = pl.BlockSpec(memory_space=pltpu.VMEM)
SMEM = pl.BlockSpec(memory_space=pltpu.SMEM)
HBM = pl.BlockSpec(memory_space=pltpu.HBM)


def sigmoid(x):
    return 0.5 * jnp.tanh(0.5 * x) + 0.5


def left_of(lengths, place, u, frames):
    return lengths[u] - place[0] * frames


def lane(block):
    return pl.ds(pl.multiple_of(block * LANES, LANES), LANES)


def call(kernel, in_specs, out_shape, scratch, flops, limit, aliases=None, out_specs=None):
    return pl.pallas_call(
        kernel,
        in_specs=in_specs,
        out_specs=out_specs or jax.tree.map(lambda _: VMEM, out_shape),
        out_shape=out_shape,
        scratch_shapes=scratch,
        input_output_aliases=aliases or {},
        cost_estimate=pl.CostEstimate(flops=flops, bytes_accessed=8 << 20, transcendentals=0),
        compiler_params=pltpu.CompilerParams(vmem_limit_bytes=limit << 20),
    )


def shape(dims, dtype):
    return jax.ShapeDtypeStruct(dims, dtype)


def far_memory(array):
    return pltpu.with_memory_space_constraint(array, pltpu.HBM)


def depthwise(slab, weight, start, rows, order):
    total = None
    for j, row in enumerate(order):
        term = slab[pl.ds(start + 1 + j, rows), :] * weight[row]
        total = term if total is None else total + term
    return total


def edges_kernel(
    place, hidden, cotangent, source, inside, across, weights, cells, upstream, arrived, loaded
):
    groups, frames, double = hidden.shape
    width = double // 2
    core = place[0] & 1
    copies = []
    for side, last in enumerate((core, 1 - core)):
        start = pl.multiple_of(last * (frames - PAD), TILE)
        near = pl.multiple_of(last * (frames - HALF_PAD), TILE)
        for u in range(groups):
            copies.append(
                (
                    pltpu.make_async_copy(
                        hidden.at[u, pl.ds(start, PAD)], cells.at[side, u], arrived.at[0, side, u]
                    ),
                    pltpu.make_async_copy(
                        cotangent.at[u, pl.ds(near, HALF_PAD)],
                        upstream.at[side, u],
                        arrived.at[1, side, u],
                    ),
                )
            )
    for first, second in copies:
        first.start()
        second.start()
    taps = pltpu.make_async_copy(source, weights, loaded)
    taps.start()
    n = 0
    for side, out in enumerate((across, inside)):
        for u in range(groups):
            copies[n][0].wait()
            for cb in range(width // LANES):
                here = slice(cb * LANES, (cb + 1) * LANES)
                there = slice(width + cb * LANES, width + (cb + 1) * LANES)
                linear = cells[side, u, :, here].astype(F32)
                gate = sigmoid(cells[side, u, :, there].astype(F32))
                out[u, 0:PAD, here] = (linear * gate).astype(BF16)
            copies[n][1].wait()
            out[u, PAD:, :] = upstream[side, u]
            n += 1
    taps.wait()


CONTRACT_COLUMNS = (((1,), (1,)), ((), ()))


def gate_kernel(
    lengths, place, hidden, weights, cotangent, source, slab, hat, grad, w_out, arrived
):
    groups, frames, double = hidden.shape
    taps = weights.shape[0]
    width = double // 2
    blocks = width // LANES
    span = frames + 2 * HALF_PAD
    chunk = (span - 2 * PAD) // 2

    def copy(n):
        at = pl.ds(pl.multiple_of(n * 2 * LANES, 2 * LANES), 2 * LANES)
        return pltpu.make_async_copy(source.at[at], w_out.at[at], arrived.at[n])

    for n in range(blocks // 2):
        copy(n).start()

    def pair(n, _):
        at = pl.ds(pl.multiple_of(n * 2 * LANES, 2 * LANES), 2 * LANES)
        copy(n).wait()
        swish = lax.dot_general(
            cotangent[...], w_out[at, :], CONTRACT_COLUMNS, preferred_element_type=F32
        )
        for u in range(groups):
            limit = left_of(lengths, place, u, frames)
            base = u * span
            for cb in (2 * n, 2 * n + 1):
                row = lax.broadcasted_iota(jnp.int32, (frames, LANES), 0)
                linear = hidden[u, :, lane(cb)].astype(F32)
                gate = sigmoid(hidden[u, :, lane(blocks + cb)].astype(F32))
                glu = jnp.where(row < limit, linear * gate, 0.0)
                block = slab.at[u, cb]
                block[PAD : PAD + frames, :] = glu.astype(BF16).astype(F32)
                weight = [weights[j : j + 1, lane(cb)] for j in range(taps)]
                for start in range(PAD, span - PAD, chunk):
                    to = slice(base + start, base + start + chunk)
                    hat[to, lane(cb)] = depthwise(block, weight, start, chunk, range(taps))
        for u in range(groups):
            to = u * span + HALF_PAD
            grad[to : to + frames, at] = swish[u * frames : (u + 1) * frames]
        return 0

    lax.fori_loop(0, blocks // 2, pair, 0)


def row_mean(values, width):
    mean = jnp.sum(values, axis=-1, keepdims=True) * (1.0 / width)
    return jnp.broadcast_to(mean, values.shape)


def forward_kernel(
    lengths,
    place,
    gated,
    inner,
    swish,
    inside,
    across,
    weights,
    gain,
    cotangent,
    w_out,
    slab,
    hat,
    grad,
    inverse,
    message,
    mean,
    held,
):
    groups, blocks, length = slab.shape[:3]
    taps = weights.shape[0]
    width = blocks * LANES
    half = width // 2
    frames = length - 2 * PAD
    span = frames + 2 * HALF_PAD
    rows = groups * frames
    for side in range(half // rows):
        theirs = (1 - (place[0] & 1)) * half + side * rows
        part = cotangent[:, pl.ds(pl.multiple_of(theirs, LANES), rows)]
        message[width + side * rows : width + (side + 1) * rows, :] = part
    first = (place[0] & 1) == 0

    def sides(u, rows, lanes):
        one, two = inside[u, rows, lanes].astype(F32), across[u, rows, lanes].astype(F32)
        return jnp.where(first, two, one), jnp.where(first, one, two)

    for u in range(groups):
        left, right = sides(u, slice(PAD, PAD + HALF_PAD), slice(0, width))
        held[2 * u * HALF_PAD : (2 * u + 1) * HALF_PAD, :] = left.astype(BF16)
        held[(2 * u + 1) * HALF_PAD : (2 * u + 2) * HALF_PAD, :] = right.astype(BF16)

    def pair(n, _):
        at = pl.ds(pl.multiple_of(n * 2 * LANES, 2 * LANES), 2 * LANES)
        result = lax.dot_general(
            held[...], w_out[at, :], CONTRACT_COLUMNS, preferred_element_type=F32
        )
        row = lax.broadcasted_iota(jnp.int32, (PAD, LANES), 0)
        for u in range(groups):
            limit = left_of(lengths, place, u, frames)
            base = u * span
            for cb in (2 * n, 2 * n + 1):
                block = slab.at[u, cb]
                before, after = sides(u, slice(0, PAD), lane(cb))
                block[0:PAD, :] = jnp.where(row - PAD < limit, before, 0.0)
                block[PAD + frames :, :] = jnp.where(row + frames < limit, after, 0.0)
                weight = [weights[j : j + 1, lane(cb)] for j in range(taps)]
                for start in (0, span - PAD):
                    to = slice(base + start, base + start + PAD)
                    hat[to, lane(cb)] = depthwise(block, weight, start, PAD, range(taps))
        for u in range(groups):
            base = u * span
            near = 2 * u * HALF_PAD
            grad[base : base + HALF_PAD, at] = result[near : near + HALF_PAD]
            grad[base + span - HALF_PAD : base + span, at] = result[
                near + HALF_PAD : near + 2 * HALF_PAD
            ]
        return 0

    lax.fori_loop(0, blocks // 2, pair, 0)
    for u in range(groups):
        rows = slice(u * span, (u + 1) * span)
        total = hat[rows, 0:LANES]
        for cb in range(1, blocks):
            total = total + hat[rows, cb * LANES : (cb + 1) * LANES]
        mean[rows, :] = row_mean(total, width)
        total = None
        for cb in range(blocks):
            centered = hat[rows, cb * LANES : (cb + 1) * LANES] - mean[rows, :]
            total = centered * centered if total is None else total + centered * centered
        inverse[rows, :] = lax.rsqrt(row_mean(total, width) + EPSILON)

    def normalize(cb, _):
        outs = []
        for u in range(groups):
            limit = left_of(lengths, place, u, frames)
            rows = slice(u * span, (u + 1) * span)
            normed = (hat[rows, lane(cb)] - mean[rows, :]) * inverse[rows, :]
            hat[rows, lane(cb)] = normed
            pre = normed[HALF_PAD : HALF_PAD + frames] * (0.5 * gain[:, lane(cb)])
            out = pre * jnp.tanh(pre) + pre
            row = lax.broadcasted_iota(jnp.int32, (frames, LANES), 0)
            outs.append(jnp.where(row < limit, out, 0.0).astype(BF16))
        message[lane(cb), :] = jnp.concatenate(outs, axis=0).T
        return 0

    lax.fori_loop(0, blocks, normalize, 0)


def product_kernel(place, near, cotangent, far, packed, out, scratch, held, sent):
    rows, width = cotangent.shape
    half = width // 2
    pairs = scratch.shape[0]
    step = 24 * pairs
    deep = scratch.shape[2] - 8
    wide = 2 * LANES
    first = lax.broadcasted_iota(jnp.int32, (pairs, 8, LANES), 1) < 4
    pick = lambda a, b: jnp.where(first, a, b)
    roll = lambda a: pltpu.roll(a, 4, 1)
    mine = pl.ds(pl.multiple_of((place[0] & 1) * half, LANES), half)

    def copy(s):
        return pltpu.make_async_copy(held.at[s], out.at[pl.ds(s * pairs, pairs)], sent.at[s])

    def chunk(s, _):
        at = pl.ds(pl.multiple_of(s * step, step), step)
        theirs = [far[width + n * rows : width + (n + 1) * rows, :] for n in range(half // rows)]
        left = jnp.concatenate([near[at, :], far[at, :]], axis=1)
        right = jnp.concatenate([cotangent[:, mine], jnp.concatenate(theirs, axis=1)], axis=0)
        for q in range(half // wide):
            result = jnp.dot(
                left, right[:, q * wide : (q + 1) * wide], preferred_element_type=F32
            )

            def parts(k):
                cut = result[:, k * LANES : (k + 1) * LANES].reshape(pairs, 3, 8, LANES)
                return cut[:, 0], cut[:, 1], cut[:, 2]

            a, b, c = parts(0)
            d, e, f = parts(1)
            rb, rc, rd = roll(b), roll(c), roll(d)
            even = (a, pick(b, rd), pick(rd, roll(e)))
            odd = (pick(rb, rc), pick(rc, e), f)
            for side, tiles in enumerate((even, odd)):
                for i, tile in enumerate(tiles):
                    scratch[:, side, 24 * q + 8 * i : 24 * q + 8 * i + 8, :] = tile
        scratch[:, :, deep:, :] = packed[pl.ds(s * pairs, pairs)]
        held[s] = scratch[...].astype(BF16)
        copy(s).start()
        return 0

    lax.fori_loop(0, width // step, chunk, 0)
    for s in range(width // step):
        copy(s).wait()


def backward_kernel(lengths, place, grad, hat, inverse, gain, slab, term, work, sums):
    groups, blocks, span = slab.shape[:3]
    width = blocks * LANES
    frames = span - 2 * HALF_PAD
    sums[...] = jnp.zeros_like(sums)
    part = span // 2

    def norm(n, _):
        u, start = n // 2, (n % 2) * part
        at = pl.ds(pl.multiple_of(n * part, TILE), part)
        limit = left_of(lengths, place, u, frames)
        row = start - HALF_PAD + lax.broadcasted_iota(jnp.int32, (part, LANES), 0)
        keep = row < limit
        inside = (row >= 0) & (row < frames)
        first = second = None
        for cb in range(blocks):
            here = slice(cb * LANES, (cb + 1) * LANES)
            normed = hat[at, here]
            halved = normed * (0.5 * gain[:, here])
            turn = jnp.tanh(halved)
            gate = 0.5 * turn + 0.5
            grad_pre = jnp.where(keep, grad[at, here], 0.0) * (gate * (1.0 + halved * (1.0 - turn)))
            term_part = jnp.where(inside, grad_pre * normed, 0.0)
            sums[:, here] += jnp.sum(term_part.reshape(part // 8, 8, LANES), axis=0)
            scaled = grad_pre * gain[:, here]
            work[at, here] = scaled
            first = scaled if first is None else first + scaled
            second = scaled * normed if second is None else second + scaled * normed
        mean = row_mean(first, width)
        slope = row_mean(second, width)
        inv = inverse[at, :]
        for cb in range(blocks):
            here = slice(cb * LANES, (cb + 1) * LANES)
            result = inv * (work[at, here] - mean - hat[at, here] * slope)
            to = pl.ds(pl.multiple_of(start, TILE), part)
            slab[u, cb, to, :] = result.astype(BF16).astype(F32)
        return 0

    lax.fori_loop(0, 2 * groups, norm, 0)
    term[...] = jnp.sum(sums[...], axis=0, keepdims=True)


def terms_kernel(
    grad, slab, term, packed, square, columns, rounded, rest, values, cells, taken
):
    groups, blocks, span = grad.shape[:3]
    frames = span - 2 * HALF_PAD
    taps = 31
    some = frames // 2
    reach = cells.shape[2]
    start = PAD - taps // 2
    square[...] = jnp.zeros_like(square)
    taken[...] = jnp.zeros_like(taken)

    def channel(cb, _):
        for u in range(groups):
            even = grad[u, cb, pl.ds(HALF_PAD, some, stride=2), :]
            odd = grad[u, cb, pl.ds(HALF_PAD + 1, some, stride=2), :]
            values[0, u], values[1, u], values[2, u] = even, odd, even + odd
            here = slab[u, cb, pl.ds(start, reach, stride=2), :]
            there = slab[u, cb, pl.ds(start + 1, reach, stride=2), :]
            after = slab[u, cb, pl.ds(start + 2, reach, stride=2), :]
            cells[0, u], cells[1, u], cells[2, u] = here, there, there + after
        for kind, lags in enumerate((taps // 2 + 1, taps // 2 + 1, taps // 2)):
            for r in range(8):
                chosen = [i for i in range(r, lags, 8)]
                totals = [None] * len(chosen)
                for u in range(groups):
                    for m in range(0, some, 8):
                        value = values[kind, u, m : m + 8, :]
                        for n, i in enumerate(chosen):
                            part = value * cells[kind, u, pl.ds(m + i, 8), :]
                            totals[n] = part if totals[n] is None else totals[n] + part
                for n, i in enumerate(chosen):
                    taken[kind, i : i + 1, :] = jnp.sum(totals[n], axis=0, keepdims=True)
        evens = taken[0] + taken[1]
        odds = taken[2] - pltpu.roll(taken[0], 15, 0) - taken[1]
        square[pl.ds(0, 16, stride=2), :] = evens
        square[pl.ds(1, 16, stride=2), :] = odds
        square[taps : taps + 1, :] = term[:, lane(cb)]
        columns[lane(cb), :] = square[...].T
        return 0

    lax.fori_loop(0, blocks, channel, 0)
    quarter = columns.shape[0] // 4
    total = columns[pl.ds(0, quarter, stride=4), :]
    for m in range(1, 4):
        total = total + pltpu.roll(columns[pl.ds(m, quarter, stride=4), :], 32 * m, 1)
    high = total.astype(BF16).astype(F32)
    rounded[0:quarter, :] = high
    rest[8 : 8 + quarter, :] = total - high
    row = lax.broadcasted_iota(jnp.int32, (8, LANES), 0)
    pairs, sides = packed.shape[:2]
    for d in range(pairs * sides):
        upper = rounded[3 * d : 3 * d + 8, :]
        lower = rest[3 * d + 5 : 3 * d + 13, :]
        tile = jnp.where(row < 3, upper, jnp.where(row < 6, lower, 0.0))
        packed[d // 2, d % 2] = tile


def input_kernel(lengths, place, grad, hidden, weights, out):
    groups, frames, _ = hidden.shape
    blocks = grad.shape[1]
    taps = weights.shape[0]
    chunk = 64
    for u in range(groups):
        limit = left_of(lengths, place, u, frames)

        def channel(cb, _):
            block = grad.at[u, cb]
            weight = [weights[j : j + 1, lane(cb)] for j in range(taps)]
            for start in range(0, frames, chunk):
                at = slice(start, start + chunk)
                total = depthwise(block, weight, start, chunk, range(taps - 1, -1, -1))
                row = start + lax.broadcasted_iota(jnp.int32, (chunk, LANES), 0)
                total = jnp.where(row < limit, total, 0.0)
                linear = hidden[u, at, lane(cb)].astype(F32)
                gate = sigmoid(hidden[u, at, lane(blocks + cb)].astype(F32))
                opened = total * gate
                out[u, at, lane(cb)] = opened.astype(BF16)
                out[u, at, lane(blocks + cb)] = (opened * linear * (1.0 - gate)).astype(BF16)
            return 0

        lax.fori_loop(0, blocks, channel, 0)


def sum_kernel(factor, got, out, taps_out, gain_out, total, held, arrived):
    own = out.shape[0]
    slots, step, _, tall, _ = held.shape

    def copy(i):
        return pltpu.make_async_copy(got.at[pl.ds(i * step, step)], held.at[i], arrived.at[i])

    for i in range(slots):
        copy(i).start()
    total[...] = jnp.zeros_like(total)

    def add(i, _):
        copy(i).wait()
        for k in range(0, step, 4):
            total[...] += jnp.sum(held[i, k : k + 4].astype(F32), axis=0)
        return 0

    lax.fori_loop(0, slots, add, 0)
    deep = tall - 8
    blocks = deep // own
    for side in range(2):
        for k in range(blocks):
            at = (side * blocks + k) * LANES
            out[:, at : at + LANES] = total[side, own * k : own * (k + 1), :] * factor
    both = total[0, deep:, :] + total[1, deep:, :]
    small = (both[0:3] + both[3:6]) * factor
    taps = taps_out.shape[1]
    spot = lax.broadcasted_iota(jnp.int32, (1, LANES), 1)
    gains = jnp.zeros((1, LANES), F32)
    for r in range(3):
        for m in range(4):
            c = 4 * r + m
            turned = pltpu.roll(small[r : r + 1, :], (LANES - 32 * m) % LANES, 1)
            taps_out[c : c + 1, :] = turned[:, :taps]
            gains = jnp.where(spot == c, pltpu.roll(turned, (c - taps) % LANES, 1), gains)
    gain_out[...] = gains[:, :own]


def local(hidden, cotangent, lengths, kernel, conv_gain, w_out):
    groups, frames, double = hidden.shape
    width = double // 2
    half = width // 2
    blocks = width // LANES
    taps = kernel.shape[1]
    seq_count = lax.axis_size("seq")
    devices = lax.axis_size("dp") * seq_count
    own = width // devices
    rows = groups * frames
    span = frames + 2 * HALF_PAD
    length = frames + 2 * PAD
    deep = own * half // LANES
    ends = seq_count - 1
    swap = [(i, i ^ 1) for i in range(seq_count)]
    place = lax.axis_index("seq")
    conv_flops = 2 * taps * rows * width

    spot = place.reshape(1)
    flat = cotangent.reshape(rows, width)
    inner_edge, outer_edge, weights = call(
        edges_kernel,
        [SMEM, HBM, HBM, HBM],
        [shape((groups, PAD + HALF_PAD, width), BF16)] * 2 + [shape((taps, width), F32)],
        [
            pltpu.VMEM((2, groups, PAD, double), BF16),
            pltpu.VMEM((2, groups, HALF_PAD, width), BF16),
            pltpu.SemaphoreType.DMA((2, 2, groups)),
            pltpu.SemaphoreType.DMA,
        ],
        1 << 20,
        4,
    )(spot, far_memory(hidden), far_memory(cotangent), far_memory(kernel.T))
    bridge = [(i, i + 1) for i in range(1, ends, 2)]
    across = lax.ppermute(outer_edge, "seq", bridge + [(j, i) for i, j in bridge])
    inside = lax.ppermute(inner_edge, "seq", swap)
    gain = conv_gain.reshape(1, width)
    slab_shape = shape((groups, blocks, length, LANES), F32)
    wide_shape = shape((groups * span, width), F32)
    gated, inner, swish, w_near = call(
        gate_kernel,
        [SMEM, SMEM] + [VMEM] * 3 + [HBM],
        [slab_shape, wide_shape, wide_shape, shape((width, width), BF16)],
        [pltpu.SemaphoreType.DMA((blocks // 2,))],
        conv_flops,
        4,
    )(lengths, spot, hidden, weights, flat, far_memory(w_out))
    slab, hat, grad_swish, inverse, message = call(
        forward_kernel,
        [SMEM, SMEM] + [VMEM] * 9,
        [
            slab_shape,
            wide_shape,
            wide_shape,
            shape((groups * span, LANES), F32),
            shape((width + half, rows), BF16),
        ],
        [pltpu.VMEM((groups * span, LANES), F32), pltpu.VMEM((2 * groups * HALF_PAD, width), BF16)],
        conv_flops,
        4,
        {2: 0, 3: 1, 4: 2},
    )(lengths, spot, gated, inner, swish, inside, across, weights, gain, flat, w_near)
    far = lax.ppermute(message, "seq", swap)
    grad, term_conv = call(
        backward_kernel,
        [SMEM, SMEM] + [VMEM] * 4,
        [shape((groups, blocks, span, LANES), F32), shape((1, width), F32)],
        [pltpu.VMEM((groups * span, width), F32), pltpu.VMEM((8, width), F32)],
        20 * rows * width,
        6,
    )(lengths, spot, grad_swish, hat, inverse, gain)
    packed = call(
        terms_kernel,
        [VMEM] * 3,
        shape((devices // 2, 2, 8, LANES), F32),
        [
            pltpu.VMEM((LANES, LANES), F32),
            pltpu.VMEM((width, LANES), F32),
            pltpu.VMEM((width // 4 + 8, LANES), F32),
            pltpu.VMEM((width // 4 + 16, LANES), F32),
            pltpu.VMEM((3, groups, frames // 2, LANES), F32),
            pltpu.VMEM((3, groups, frames // 2 + 16, LANES), F32),
            pltpu.VMEM((3, 16, LANES), F32),
        ],
        conv_flops,
        6,
    )(grad, slab, term_conv)
    pairs = 32
    steps = devices // (2 * pairs)
    pieces = call(
        product_kernel,
        [SMEM] + [VMEM] * 4,
        pltpu.HBM((devices // 2, 2, deep + 8, LANES), BF16),
        [
            pltpu.VMEM((pairs, 2, deep + 8, LANES), F32),
            pltpu.VMEM((steps, pairs, 2, deep + 8, LANES), BF16),
            pltpu.SemaphoreType.DMA((steps,)),
        ],
        4 * rows * width * half,
        10,
        out_specs=HBM,
    )(spot, message, flat, far, packed)
    got = lax.all_to_all(pieces.reshape(devices, deep + 8, LANES), AXES, 0, 0, tiled=True)
    grad_hidden = call(
        input_kernel,
        [SMEM, SMEM] + [VMEM] * 3,
        shape((groups, frames, double), BF16),
        [],
        conv_flops,
        4,
    )(lengths, spot, grad, hidden, weights)

    factor = 1.0 / math.sqrt(groups * lax.axis_size("dp") * frames * seq_count)
    slots = 4
    grad_w, grad_kernel, grad_gain = call(
        functools.partial(sum_kernel, factor),
        [HBM],
        [shape((own, width), F32), shape((own, taps), F32), shape((1, own), F32)],
        [
            pltpu.VMEM((2, deep + 8, LANES), F32),
            pltpu.VMEM((slots, devices // 2 // slots, 2, deep + 8, LANES), BF16),
            pltpu.SemaphoreType.DMA((slots,)),
        ],
        1 << 20,
        6,
    )(far_memory(got.reshape(devices // 2, 2, deep + 8, LANES)))
    return grad_hidden, grad_w, grad_kernel, grad_gain.reshape(own)


def solution(mesh):
    in_specs = (P("dp", "seq", None), P("dp", "seq", None), P("dp"), P(), P(), P())
    out_specs = (P("dp", "seq", None), P(AXES, None), P(AXES, None), P(AXES))
    return jax.shard_map(local, mesh=mesh, in_specs=in_specs, out_specs=out_specs, check_vma=False)
```

```python
import functools
import math

import jax
import jax.numpy as jnp
from jax import lax
from jax.experimental import pallas as pl
from jax.experimental.pallas import tpu as pltpu
from jax.sharding import PartitionSpec as P

EPSILON = 1e-05
AXES = ("dp", "seq")
LANES = 128
HALF_PAD = 16
PAD = 32
TILE = 16
F32, BF16 = jnp.float32, jnp.bfloat16
VMEM = pl.BlockSpec(memory_space=pltpu.VMEM)
SMEM = pl.BlockSpec(memory_space=pltpu.SMEM)
HBM = pl.BlockSpec(memory_space=pltpu.HBM)


def sigmoid(x):
    return 0.5 * jnp.tanh(0.5 * x) + 0.5


def left_of(lengths, place, u, frames):
    return lengths[u] - place[0] * frames


def lane(block):
    return pl.ds(pl.multiple_of(block * LANES, LANES), LANES)


def call(kernel, in_specs, out_shape, scratch, flops, limit, aliases=None, out_specs=None):
    return pl.pallas_call(
        kernel,
        in_specs=in_specs,
        out_specs=out_specs or jax.tree.map(lambda _: VMEM, out_shape),
        out_shape=out_shape,
        scratch_shapes=scratch,
        input_output_aliases=aliases or {},
        cost_estimate=pl.CostEstimate(flops=flops, bytes_accessed=8 << 20, transcendentals=0),
        compiler_params=pltpu.CompilerParams(vmem_limit_bytes=limit << 20),
    )


def shape(dims, dtype):
    return jax.ShapeDtypeStruct(dims, dtype)


def far_memory(array):
    return pltpu.with_memory_space_constraint(array, pltpu.HBM)


def depthwise(slab, weight, start, rows, order):
    total = None
    for j, row in enumerate(order):
        term = slab[pl.ds(start + 1 + j, rows), :] * weight[row]
        total = term if total is None else total + term
    return total


def edges_kernel(
    place, hidden, cotangent, source, inside, across, weights, cells, upstream, arrived, loaded
):
    groups, frames, double = hidden.shape
    width = double // 2
    core = place[0] & 1
    copies = []
    for side, last in enumerate((core, 1 - core)):
        start = pl.multiple_of(last * (frames - PAD), TILE)
        near = pl.multiple_of(last * (frames - HALF_PAD), TILE)
        for u in range(groups):
            copies.append(
                (
                    pltpu.make_async_copy(
                        hidden.at[u, pl.ds(start, PAD)], cells.at[side, u], arrived.at[0, side, u]
                    ),
                    pltpu.make_async_copy(
                        cotangent.at[u, pl.ds(near, HALF_PAD)],
                        upstream.at[side, u],
                        arrived.at[1, side, u],
                    ),
                )
            )
    for first, second in copies:
        first.start()
        second.start()
    taps = pltpu.make_async_copy(source, weights, loaded)
    taps.start()
    n = 0
    for side, out in enumerate((across, inside)):
        for u in range(groups):
            copies[n][0].wait()
            for cb in range(width // LANES):
                here = slice(cb * LANES, (cb + 1) * LANES)
                there = slice(width + cb * LANES, width + (cb + 1) * LANES)
                linear = cells[side, u, :, here].astype(F32)
                gate = sigmoid(cells[side, u, :, there].astype(F32))
                out[u, 0:PAD, here] = (linear * gate).astype(BF16)
            copies[n][1].wait()
            out[u, PAD:, :] = upstream[side, u]
            n += 1
    taps.wait()


CONTRACT_COLUMNS = (((1,), (1,)), ((), ()))


def inner_rows(block, weights, cb, cells, evens, mixed, some, taps):
    reach = cells.shape[1]
    here = block[pl.ds(PAD + 1, reach, stride=2), :]
    there = block[pl.ds(PAD + 2, reach, stride=2), :]
    after = block[pl.ds(PAD + 3, reach, stride=2), :]
    cells[0], cells[1], cells[2] = here, there, there + after
    weight = [weights[j : j + 1, lane(cb)] for j in range(taps)]
    paired = [weight[j] + weight[j + 1] for j in range(0, taps - 1, 2)] + [weight[taps - 1]]

    def run(kind, rows, chosen):
        total = None
        for i, factor in enumerate(chosen):
            part = cells[kind, pl.ds(i, rows), :] * factor
            total = part if total is None else total + part
        return total

    evens[...] = run(0, some + 8, weight[0::2])
    odd = run(1, some, weight[1::2])
    mixed[pl.ds(0, some, stride=2), :] = evens[0:some, :] + odd
    both = run(2, some, paired)
    mixed[pl.ds(1, some, stride=2), :] = both - evens[1 : some + 1, :] - odd


def gate_kernel(
    lengths, place, hidden, weights, cotangent, source, slab, hat, grad, w_out, arrived, cells, evens, mixed
):
    groups, frames, double = hidden.shape
    taps = weights.shape[0]
    width = double // 2
    blocks = width // LANES
    span = frames + 2 * HALF_PAD
    some = (span - 2 * PAD) // 2

    def copy(n):
        at = pl.ds(pl.multiple_of(n * 2 * LANES, 2 * LANES), 2 * LANES)
        return pltpu.make_async_copy(source.at[at], w_out.at[at], arrived.at[n])

    for n in range(blocks // 2):
        copy(n).start()

    def pair(n, _):
        at = pl.ds(pl.multiple_of(n * 2 * LANES, 2 * LANES), 2 * LANES)
        copy(n).wait()
        swish = lax.dot_general(
            cotangent[...], w_out[at, :], CONTRACT_COLUMNS, preferred_element_type=F32
        )
        for u in range(groups):
            limit = left_of(lengths, place, u, frames)
            base = u * span
            for cb in (2 * n, 2 * n + 1):
                row = lax.broadcasted_iota(jnp.int32, (frames, LANES), 0)
                linear = hidden[u, :, lane(cb)].astype(F32)
                gate = sigmoid(hidden[u, :, lane(blocks + cb)].astype(F32))
                glu = jnp.where(row < limit, linear * gate, 0.0)
                block = slab.at[u, cb]
                block[PAD : PAD + frames, :] = glu.astype(BF16).astype(F32)
                inner_rows(
                    block, weights, cb, cells.at[u], evens.at[u], mixed.at[u], some, taps
                )
                to = slice(base + PAD, base + span - PAD)
                hat[to, lane(cb)] = mixed[u]
        for u in range(groups):
            to = u * span + HALF_PAD
            grad[to : to + frames, at] = swish[u * frames : (u + 1) * frames]
        return 0

    lax.fori_loop(0, blocks // 2, pair, 0)


def row_mean(values, width):
    mean = jnp.sum(values, axis=-1, keepdims=True) * (1.0 / width)
    return jnp.broadcast_to(mean, values.shape)


def forward_kernel(
    lengths,
    place,
    gated,
    inner,
    swish,
    inside,
    across,
    weights,
    gain,
    cotangent,
    w_out,
    slab,
    hat,
    grad,
    inverse,
    message,
    mean,
    held,
):
    groups, blocks, length = slab.shape[:3]
    taps = weights.shape[0]
    width = blocks * LANES
    half = width // 2
    frames = length - 2 * PAD
    span = frames + 2 * HALF_PAD
    rows = groups * frames
    for side in range(half // rows):
        theirs = (1 - (place[0] & 1)) * half + side * rows
        part = cotangent[:, pl.ds(pl.multiple_of(theirs, LANES), rows)]
        message[width + side * rows : width + (side + 1) * rows, :] = part
    first = (place[0] & 1) == 0

    def sides(u, rows, lanes):
        one, two = inside[u, rows, lanes].astype(F32), across[u, rows, lanes].astype(F32)
        return jnp.where(first, two, one), jnp.where(first, one, two)

    for u in range(groups):
        left, right = sides(u, slice(PAD, PAD + HALF_PAD), slice(0, width))
        held[2 * u * HALF_PAD : (2 * u + 1) * HALF_PAD, :] = left.astype(BF16)
        held[(2 * u + 1) * HALF_PAD : (2 * u + 2) * HALF_PAD, :] = right.astype(BF16)

    def pair(n, _):
        at = pl.ds(pl.multiple_of(n * 2 * LANES, 2 * LANES), 2 * LANES)
        result = lax.dot_general(
            held[...], w_out[at, :], CONTRACT_COLUMNS, preferred_element_type=F32
        )
        row = lax.broadcasted_iota(jnp.int32, (PAD, LANES), 0)
        for u in range(groups):
            limit = left_of(lengths, place, u, frames)
            base = u * span
            for cb in (2 * n, 2 * n + 1):
                block = slab.at[u, cb]
                before, after = sides(u, slice(0, PAD), lane(cb))
                block[0:PAD, :] = jnp.where(row - PAD < limit, before, 0.0)
                block[PAD + frames :, :] = jnp.where(row + frames < limit, after, 0.0)
                weight = [weights[j : j + 1, lane(cb)] for j in range(taps)]
                for start in (0, span - PAD):
                    to = slice(base + start, base + start + PAD)
                    hat[to, lane(cb)] = depthwise(block, weight, start, PAD, range(taps))
        for u in range(groups):
            base = u * span
            near = 2 * u * HALF_PAD
            grad[base : base + HALF_PAD, at] = result[near : near + HALF_PAD]
            grad[base + span - HALF_PAD : base + span, at] = result[
                near + HALF_PAD : near + 2 * HALF_PAD
            ]
        return 0

    lax.fori_loop(0, blocks // 2, pair, 0)
    for u in range(groups):
        rows = slice(u * span, (u + 1) * span)
        total = hat[rows, 0:LANES]
        for cb in range(1, blocks):
            total = total + hat[rows, cb * LANES : (cb + 1) * LANES]
        mean[rows, :] = row_mean(total, width)
        total = None
        for cb in range(blocks):
            centered = hat[rows, cb * LANES : (cb + 1) * LANES] - mean[rows, :]
            total = centered * centered if total is None else total + centered * centered
        inverse[rows, :] = lax.rsqrt(row_mean(total, width) + EPSILON)

    def normalize(cb, _):
        outs = []
        for u in range(groups):
            limit = left_of(lengths, place, u, frames)
            rows = slice(u * span, (u + 1) * span)
            normed = (hat[rows, lane(cb)] - mean[rows, :]) * inverse[rows, :]
            hat[rows, lane(cb)] = normed
            pre = normed[HALF_PAD : HALF_PAD + frames] * (0.5 * gain[:, lane(cb)])
            out = pre * jnp.tanh(pre) + pre
            row = lax.broadcasted_iota(jnp.int32, (frames, LANES), 0)
            outs.append(jnp.where(row < limit, out, 0.0).astype(BF16))
        message[lane(cb), :] = jnp.concatenate(outs, axis=0).T
        return 0

    lax.fori_loop(0, blocks, normalize, 0)


def product_kernel(place, near, cotangent, far, packed, out, scratch, held, sent):
    rows, width = cotangent.shape
    half = width // 2
    pairs = scratch.shape[0]
    step = 24 * pairs
    deep = scratch.shape[2] - 8
    wide = 2 * LANES
    first = lax.broadcasted_iota(jnp.int32, (pairs, 8, LANES), 1) < 4
    pick = lambda a, b: jnp.where(first, a, b)
    roll = lambda a: pltpu.roll(a, 4, 1)
    mine = pl.ds(pl.multiple_of((place[0] & 1) * half, LANES), half)

    def copy(s):
        return pltpu.make_async_copy(held.at[s], out.at[pl.ds(s * pairs, pairs)], sent.at[s])

    def chunk(s, _):
        at = pl.ds(pl.multiple_of(s * step, step), step)
        theirs = [far[width + n * rows : width + (n + 1) * rows, :] for n in range(half // rows)]
        left = jnp.concatenate([near[at, :], far[at, :]], axis=1)
        right = jnp.concatenate([cotangent[:, mine], jnp.concatenate(theirs, axis=1)], axis=0)
        for q in range(half // wide):
            result = jnp.dot(
                left, right[:, q * wide : (q + 1) * wide], preferred_element_type=F32
            )

            def parts(k):
                cut = result[:, k * LANES : (k + 1) * LANES].reshape(pairs, 3, 8, LANES)
                return cut[:, 0], cut[:, 1], cut[:, 2]

            a, b, c = parts(0)
            d, e, f = parts(1)
            rb, rc, rd = roll(b), roll(c), roll(d)
            even = (a, pick(b, rd), pick(rd, roll(e)))
            odd = (pick(rb, rc), pick(rc, e), f)
            for side, tiles in enumerate((even, odd)):
                for i, tile in enumerate(tiles):
                    scratch[:, side, 24 * q + 8 * i : 24 * q + 8 * i + 8, :] = tile
        scratch[:, :, deep:, :] = packed[pl.ds(s * pairs, pairs)]
        held[s] = scratch[...].astype(BF16)
        copy(s).start()
        return 0

    lax.fori_loop(0, width // step, chunk, 0)
    for s in range(width // step):
        copy(s).wait()


def backward_kernel(lengths, place, grad, hat, inverse, gain, slab, term, work, sums):
    groups, blocks, span = slab.shape[:3]
    width = blocks * LANES
    frames = span - 2 * HALF_PAD
    sums[...] = jnp.zeros_like(sums)
    part = span // 2

    def norm(n, _):
        u, start = n // 2, (n % 2) * part
        at = pl.ds(pl.multiple_of(n * part, TILE), part)
        limit = left_of(lengths, place, u, frames)
        row = start - HALF_PAD + lax.broadcasted_iota(jnp.int32, (part, LANES), 0)
        keep = row < limit
        inside = (row >= 0) & (row < frames)
        first = second = None
        for cb in range(blocks):
            here = slice(cb * LANES, (cb + 1) * LANES)
            normed = hat[at, here]
            halved = normed * (0.5 * gain[:, here])
            turn = jnp.tanh(halved)
            gate = 0.5 * turn + 0.5
            grad_pre = jnp.where(keep, grad[at, here], 0.0) * (gate * (1.0 + halved * (1.0 - turn)))
            term_part = jnp.where(inside, grad_pre * normed, 0.0)
            sums[:, here] += jnp.sum(term_part.reshape(part // 8, 8, LANES), axis=0)
            scaled = grad_pre * gain[:, here]
            work[at, here] = scaled
            first = scaled if first is None else first + scaled
            second = scaled * normed if second is None else second + scaled * normed
        mean = row_mean(first, width)
        slope = row_mean(second, width)
        inv = inverse[at, :]
        for cb in range(blocks):
            here = slice(cb * LANES, (cb + 1) * LANES)
            result = inv * (work[at, here] - mean - hat[at, here] * slope)
            to = pl.ds(pl.multiple_of(start, TILE), part)
            slab[u, cb, to, :] = result.astype(BF16).astype(F32)
        return 0

    lax.fori_loop(0, 2 * groups, norm, 0)
    term[...] = jnp.sum(sums[...], axis=0, keepdims=True)


def terms_kernel(
    grad, slab, term, packed, square, columns, rounded, rest, values, cells, taken
):
    groups, blocks, span = grad.shape[:3]
    frames = span - 2 * HALF_PAD
    taps = 31
    some = frames // 2
    reach = cells.shape[2]
    start = PAD - taps // 2
    taken[...] = jnp.zeros_like(taken)

    def channel(cb, _):
        for u in range(groups):
            even = grad[u, cb, pl.ds(HALF_PAD, some, stride=2), :]
            odd = grad[u, cb, pl.ds(HALF_PAD + 1, some, stride=2), :]
            values[0, u], values[1, u], values[2, u] = even, odd, even + odd
            here = slab[u, cb, pl.ds(start, reach, stride=2), :]
            there = slab[u, cb, pl.ds(start + 1, reach, stride=2), :]
            after = slab[u, cb, pl.ds(start + 2, reach, stride=2), :]
            cells[0, u], cells[1, u], cells[2, u] = here, there, there + after
        for kind, lags in enumerate((taps // 2 + 1, taps // 2 + 1, taps // 2)):
            for r in range(8):
                chosen = [i for i in range(r, lags, 8)]
                totals = [None] * len(chosen)
                for u in range(groups):
                    for m in range(0, some, 8):
                        value = values[kind, u, m : m + 8, :]
                        for n, i in enumerate(chosen):
                            part = value * cells[kind, u, pl.ds(m + i, 8), :]
                            totals[n] = part if totals[n] is None else totals[n] + part
                for n, i in enumerate(chosen):
                    taken[kind, 8 * i : 8 * i + 8, :] = totals[n]
        sums = []
        for kind in range(3):
            line = taken[kind, pl.ds(0, 16, stride=8), :]
            for k in range(1, 8):
                line = line + taken[kind, pl.ds(k, 16, stride=8), :]
            sums.append(line)
        evens = sums[0] + sums[1]
        odds = sums[2] - pltpu.roll(sums[0], 15, 0) - sums[1]
        square[cb, pl.ds(0, 16, stride=2), :] = evens
        square[cb, pl.ds(1, 16, stride=2), :] = odds
        square[cb, taps : taps + 1, :] = term[:, lane(cb)]
        return 0

    lax.fori_loop(0, blocks, channel, 0)
    quarter = blocks * LANES // 4
    spot = lax.broadcasted_iota(jnp.int32, (32, LANES), 1) // 32
    lines = []
    for g in range(blocks // 4):
        columns[g] = square[4 * g : 4 * g + 4].reshape(LANES, LANES).T
        for b in range(4):
            line = jnp.zeros((32, LANES), F32)
            for m in range(4):
                taken_rows = columns[g, pl.ds(m, 32, stride=4), :]
                line = jnp.where(spot == m, pltpu.roll(taken_rows, 32 * ((m - b) % 4), 1), line)
            lines.append(line)
    total = jnp.concatenate(lines, axis=0)
    high = total.astype(BF16).astype(F32)
    rounded[0:quarter, :] = high
    rest[8 : 8 + quarter, :] = total - high
    row = lax.broadcasted_iota(jnp.int32, (8, LANES), 0)
    pairs, sides = packed.shape[:2]
    for d in range(pairs * sides):
        upper = rounded[3 * d : 3 * d + 8, :]
        lower = rest[3 * d + 5 : 3 * d + 13, :]
        tile = jnp.where(row < 3, upper, jnp.where(row < 6, lower, 0.0))
        packed[d // 2, d % 2] = tile


def input_kernel(lengths, place, grad, hidden, weights, out):
    groups, frames, _ = hidden.shape
    blocks = grad.shape[1]
    taps = weights.shape[0]
    chunk = 64
    for u in range(groups):
        limit = left_of(lengths, place, u, frames)

        def channel(cb, _):
            block = grad.at[u, cb]
            weight = [weights[j : j + 1, lane(cb)] for j in range(taps)]
            for start in range(0, frames, chunk):
                at = slice(start, start + chunk)
                total = depthwise(block, weight, start, chunk, range(taps - 1, -1, -1))
                row = start + lax.broadcasted_iota(jnp.int32, (chunk, LANES), 0)
                total = jnp.where(row < limit, total, 0.0)
                linear = hidden[u, at, lane(cb)].astype(F32)
                gate = sigmoid(hidden[u, at, lane(blocks + cb)].astype(F32))
                opened = total * gate
                out[u, at, lane(cb)] = opened.astype(BF16)
                out[u, at, lane(blocks + cb)] = (opened * linear * (1.0 - gate)).astype(BF16)
            return 0

        lax.fori_loop(0, blocks, channel, 0)


def sum_kernel(factor, got, out, taps_out, gain_out, total, held, arrived):
    own = out.shape[0]
    slots, step, _, tall, _ = held.shape

    def copy(i):
        return pltpu.make_async_copy(got.at[pl.ds(i * step, step)], held.at[i], arrived.at[i])

    for i in range(slots):
        copy(i).start()
    total[...] = jnp.zeros_like(total)

    def add(i, _):
        copy(i).wait()
        for k in range(0, step, 4):
            total[...] += jnp.sum(held[i, k : k + 4].astype(F32), axis=0)
        return 0

    lax.fori_loop(0, slots, add, 0)
    deep = tall - 8
    blocks = deep // own
    for side in range(2):
        for k in range(blocks):
            at = (side * blocks + k) * LANES
            out[:, at : at + LANES] = total[side, own * k : own * (k + 1), :] * factor
    both = total[0, deep:, :] + total[1, deep:, :]
    small = (both[0:3] + both[3:6]) * factor
    taps = taps_out.shape[1]
    spot = lax.broadcasted_iota(jnp.int32, (1, LANES), 1)
    gains = jnp.zeros((1, LANES), F32)
    for r in range(3):
        for m in range(4):
            c = 4 * r + m
            turned = pltpu.roll(small[r : r + 1, :], (LANES - 32 * m) % LANES, 1)
            taps_out[c : c + 1, :] = turned[:, :taps]
            gains = jnp.where(spot == c, pltpu.roll(turned, (c - taps) % LANES, 1), gains)
    gain_out[...] = gains[:, :own]


def local(hidden, cotangent, lengths, kernel, conv_gain, w_out):
    groups, frames, double = hidden.shape
    width = double // 2
    half = width // 2
    blocks = width // LANES
    taps = kernel.shape[1]
    seq_count = lax.axis_size("seq")
    devices = lax.axis_size("dp") * seq_count
    own = width // devices
    rows = groups * frames
    span = frames + 2 * HALF_PAD
    length = frames + 2 * PAD
    deep = own * half // LANES
    ends = seq_count - 1
    swap = [(i, i ^ 1) for i in range(seq_count)]
    place = lax.axis_index("seq")
    conv_flops = 2 * taps * rows * width

    spot = place.reshape(1)
    flat = cotangent.reshape(rows, width)
    inner_edge, outer_edge, weights = call(
        edges_kernel,
        [SMEM, HBM, HBM, HBM],
        [shape((groups, PAD + HALF_PAD, width), BF16)] * 2 + [shape((taps, width), F32)],
        [
            pltpu.VMEM((2, groups, PAD, double), BF16),
            pltpu.VMEM((2, groups, HALF_PAD, width), BF16),
            pltpu.SemaphoreType.DMA((2, 2, groups)),
            pltpu.SemaphoreType.DMA,
        ],
        1 << 20,
        4,
    )(spot, far_memory(hidden), far_memory(cotangent), far_memory(kernel.T))
    bridge = [(i, i + 1) for i in range(1, ends, 2)]
    across = lax.ppermute(outer_edge, "seq", bridge + [(j, i) for i, j in bridge])
    inside = lax.ppermute(inner_edge, "seq", swap)
    gain = conv_gain.reshape(1, width)
    slab_shape = shape((groups, blocks, length, LANES), F32)
    wide_shape = shape((groups * span, width), F32)
    gated, inner, swish, w_near = call(
        gate_kernel,
        [SMEM, SMEM] + [VMEM] * 3 + [HBM],
        [slab_shape, wide_shape, wide_shape, shape((width, width), BF16)],
        [
            pltpu.SemaphoreType.DMA((blocks // 2,)),
            pltpu.VMEM((groups, 3, 104, LANES), F32),
            pltpu.VMEM((groups, 88, LANES), F32),
            pltpu.VMEM((groups, 160, LANES), F32),
        ],
        conv_flops,
        4,
    )(lengths, spot, hidden, weights, flat, far_memory(w_out))
    slab, hat, grad_swish, inverse, message = call(
        forward_kernel,
        [SMEM, SMEM] + [VMEM] * 9,
        [
            slab_shape,
            wide_shape,
            wide_shape,
            shape((groups * span, LANES), F32),
            shape((width + half, rows), BF16),
        ],
        [pltpu.VMEM((groups * span, LANES), F32), pltpu.VMEM((2 * groups * HALF_PAD, width), BF16)],
        conv_flops,
        4,
        {2: 0, 3: 1, 4: 2},
    )(lengths, spot, gated, inner, swish, inside, across, weights, gain, flat, w_near)
    far = lax.ppermute(message, "seq", swap)
    grad, term_conv = call(
        backward_kernel,
        [SMEM, SMEM] + [VMEM] * 4,
        [shape((groups, blocks, span, LANES), F32), shape((1, width), F32)],
        [pltpu.VMEM((groups * span, width), F32), pltpu.VMEM((8, width), F32)],
        20 * rows * width,
        6,
    )(lengths, spot, grad_swish, hat, inverse, gain)
    packed = call(
        terms_kernel,
        [VMEM] * 3,
        shape((devices // 2, 2, 8, LANES), F32),
        [
            pltpu.VMEM((blocks, 32, LANES), F32),
            pltpu.VMEM((blocks // 4, LANES, LANES), F32),
            pltpu.VMEM((width // 4 + 8, LANES), F32),
            pltpu.VMEM((width // 4 + 16, LANES), F32),
            pltpu.VMEM((3, groups, frames // 2, LANES), F32),
            pltpu.VMEM((3, groups, frames // 2 + 16, LANES), F32),
            pltpu.VMEM((3, 128, LANES), F32),
        ],
        conv_flops,
        6,
    )(grad, slab, term_conv)
    pairs = 32
    steps = devices // (2 * pairs)
    pieces = call(
        product_kernel,
        [SMEM] + [VMEM] * 4,
        pltpu.HBM((devices // 2, 2, deep + 8, LANES), BF16),
        [
            pltpu.VMEM((pairs, 2, deep + 8, LANES), F32),
            pltpu.VMEM((steps, pairs, 2, deep + 8, LANES), BF16),
            pltpu.SemaphoreType.DMA((steps,)),
        ],
        4 * rows * width * half,
        10,
        out_specs=HBM,
    )(spot, message, flat, far, packed)
    got = lax.all_to_all(pieces.reshape(devices, deep + 8, LANES), AXES, 0, 0, tiled=True)
    grad_hidden = call(
        input_kernel,
        [SMEM, SMEM] + [VMEM] * 3,
        shape((groups, frames, double), BF16),
        [],
        conv_flops,
        4,
    )(lengths, spot, grad, hidden, weights)

    factor = 1.0 / math.sqrt(groups * lax.axis_size("dp") * frames * seq_count)
    slots = 4
    grad_w, grad_kernel, grad_gain = call(
        functools.partial(sum_kernel, factor),
        [HBM],
        [shape((own, width), F32), shape((own, taps), F32), shape((1, own), F32)],
        [
            pltpu.VMEM((2, deep + 8, LANES), F32),
            pltpu.VMEM((slots, devices // 2 // slots, 2, deep + 8, LANES), BF16),
            pltpu.SemaphoreType.DMA((slots,)),
        ],
        1 << 20,
        6,
    )(far_memory(got.reshape(devices // 2, 2, deep + 8, LANES)))
    return grad_hidden, grad_w, grad_kernel, grad_gain.reshape(own)


def solution(mesh):
    in_specs = (P("dp", "seq", None), P("dp", "seq", None), P("dp"), P(), P(), P())
    out_specs = (P("dp", "seq", None), P(AXES, None), P(AXES, None), P(AXES))
    return jax.shard_map(local, mesh=mesh, in_specs=in_specs, out_specs=out_specs, check_vma=False)
```

```python
import functools
import math

import jax
import jax.numpy as jnp
from jax import lax
from jax.experimental import pallas as pl
from jax.experimental.pallas import tpu as pltpu
from jax.sharding import PartitionSpec as P

EPSILON = 1e-05
AXES = ("dp", "seq")
LANES = 128
HALF_PAD = 16
PAD = 32
TILE = 16
F32, BF16 = jnp.float32, jnp.bfloat16
VMEM = pl.BlockSpec(memory_space=pltpu.VMEM)
SMEM = pl.BlockSpec(memory_space=pltpu.SMEM)
HBM = pl.BlockSpec(memory_space=pltpu.HBM)


def sigmoid(x):
    return 0.5 * jnp.tanh(0.5 * x) + 0.5


def left_of(lengths, place, u, frames):
    return lengths[u] - place[0] * frames


def lane(block):
    return pl.ds(pl.multiple_of(block * LANES, LANES), LANES)


def call(kernel, in_specs, out_shape, scratch, flops, limit, aliases=None, out_specs=None):
    return pl.pallas_call(
        kernel,
        in_specs=in_specs,
        out_specs=out_specs or jax.tree.map(lambda _: VMEM, out_shape),
        out_shape=out_shape,
        scratch_shapes=scratch,
        input_output_aliases=aliases or {},
        cost_estimate=pl.CostEstimate(flops=flops, bytes_accessed=8 << 20, transcendentals=0),
        compiler_params=pltpu.CompilerParams(vmem_limit_bytes=limit << 20),
    )


def shape(dims, dtype):
    return jax.ShapeDtypeStruct(dims, dtype)


def far_memory(array):
    return pltpu.with_memory_space_constraint(array, pltpu.HBM)


def depthwise(slab, weight, start, rows, order):
    total = None
    for j, row in enumerate(order):
        term = slab[pl.ds(start + 1 + j, rows), :] * weight[row]
        total = term if total is None else total + term
    return total


def edges_kernel(
    place, hidden, cotangent, source, inside, across, weights, cells, upstream, arrived, loaded
):
    groups, frames, double = hidden.shape
    width = double // 2
    core = place[0] & 1
    copies = []
    for side, last in enumerate((core, 1 - core)):
        start = pl.multiple_of(last * (frames - PAD), TILE)
        near = pl.multiple_of(last * (frames - HALF_PAD), TILE)
        for u in range(groups):
            copies.append(
                (
                    pltpu.make_async_copy(
                        hidden.at[u, pl.ds(start, PAD)], cells.at[side, u], arrived.at[0, side, u]
                    ),
                    pltpu.make_async_copy(
                        cotangent.at[u, pl.ds(near, HALF_PAD)],
                        upstream.at[side, u],
                        arrived.at[1, side, u],
                    ),
                )
            )
    for first, second in copies:
        first.start()
        second.start()
    taps = pltpu.make_async_copy(source, weights, loaded)
    taps.start()
    n = 0
    for side, out in enumerate((across, inside)):
        for u in range(groups):
            copies[n][0].wait()
            for cb in range(width // LANES):
                here = slice(cb * LANES, (cb + 1) * LANES)
                there = slice(width + cb * LANES, width + (cb + 1) * LANES)
                linear = cells[side, u, :, here].astype(F32)
                gate = sigmoid(cells[side, u, :, there].astype(F32))
                out[u, 0:PAD, here] = (linear * gate).astype(BF16)
            copies[n][1].wait()
            out[u, PAD:, :] = upstream[side, u]
            n += 1
    taps.wait()


CONTRACT_COLUMNS = (((1,), (1,)), ((), ()))


def inner_rows(block, weights, cb, cells, evens, mixed, some, taps):
    reach = cells.shape[1]
    here = block[pl.ds(PAD + 1, reach, stride=2), :]
    there = block[pl.ds(PAD + 2, reach, stride=2), :]
    after = block[pl.ds(PAD + 3, reach, stride=2), :]
    cells[0], cells[1], cells[2] = here, there, there + after
    weight = [weights[j : j + 1, lane(cb)] for j in range(taps)]
    paired = [weight[j] + weight[j + 1] for j in range(0, taps - 1, 2)] + [weight[taps - 1]]

    def run(kind, rows, chosen):
        total = None
        for i, factor in enumerate(chosen):
            part = cells[kind, pl.ds(i, rows), :] * factor
            total = part if total is None else total + part
        return total

    evens[...] = run(0, some + 8, weight[0::2])
    odd = run(1, some, weight[1::2])
    mixed[pl.ds(0, some, stride=2), :] = evens[0:some, :] + odd
    both = run(2, some, paired)
    mixed[pl.ds(1, some, stride=2), :] = both - evens[1 : some + 1, :] - odd


def gate_kernel(
    lengths, place, hidden, weights, cotangent, source, slab, hat, grad, w_out, arrived, cells, evens, mixed
):
    groups, frames, double = hidden.shape
    taps = weights.shape[0]
    width = double // 2
    blocks = width // LANES
    span = frames + 2 * HALF_PAD
    some = (span - 2 * PAD) // 2

    def copy(n):
        at = pl.ds(pl.multiple_of(n * 2 * LANES, 2 * LANES), 2 * LANES)
        return pltpu.make_async_copy(source.at[at], w_out.at[at], arrived.at[n])

    for n in range(blocks // 2):
        copy(n).start()

    def pair(n, _):
        at = pl.ds(pl.multiple_of(n * 2 * LANES, 2 * LANES), 2 * LANES)
        copy(n).wait()
        swish = lax.dot_general(
            cotangent[...], w_out[at, :], CONTRACT_COLUMNS, preferred_element_type=F32
        )
        for u in range(groups):
            limit = left_of(lengths, place, u, frames)
            base = u * span
            for cb in (2 * n, 2 * n + 1):
                row = lax.broadcasted_iota(jnp.int32, (frames, LANES), 0)
                linear = hidden[u, :, lane(cb)].astype(F32)
                gate = sigmoid(hidden[u, :, lane(blocks + cb)].astype(F32))
                glu = jnp.where(row < limit, linear * gate, 0.0)
                block = slab.at[u, cb]
                block[PAD : PAD + frames, :] = glu.astype(BF16).astype(F32)
                inner_rows(
                    block, weights, cb, cells.at[u], evens.at[u], mixed.at[u], some, taps
                )
                to = slice(base + PAD, base + span - PAD)
                hat[to, lane(cb)] = mixed[u]
        for u in range(groups):
            to = u * span + HALF_PAD
            grad[to : to + frames, at] = swish[u * frames : (u + 1) * frames]
        return 0

    lax.fori_loop(0, blocks // 2, pair, 0)


def row_mean(values, width):
    mean = jnp.sum(values, axis=-1, keepdims=True) * (1.0 / width)
    return jnp.broadcast_to(mean, values.shape)


def forward_kernel(
    lengths,
    place,
    gated,
    inner,
    swish,
    inside,
    across,
    weights,
    gain,
    cotangent,
    w_out,
    slab,
    hat,
    grad,
    inverse,
    message,
    mean,
    held,
):
    groups, blocks, length = slab.shape[:3]
    taps = weights.shape[0]
    width = blocks * LANES
    half = width // 2
    frames = length - 2 * PAD
    span = frames + 2 * HALF_PAD
    rows = groups * frames
    for side in range(half // rows):
        theirs = (1 - (place[0] & 1)) * half + side * rows
        part = cotangent[:, pl.ds(pl.multiple_of(theirs, LANES), rows)]
        message[width + side * rows : width + (side + 1) * rows, :] = part
    first = (place[0] & 1) == 0

    def sides(u, rows, lanes):
        one, two = inside[u, rows, lanes].astype(F32), across[u, rows, lanes].astype(F32)
        return jnp.where(first, two, one), jnp.where(first, one, two)

    for u in range(groups):
        left, right = sides(u, slice(PAD, PAD + HALF_PAD), slice(0, width))
        held[2 * u * HALF_PAD : (2 * u + 1) * HALF_PAD, :] = left.astype(BF16)
        held[(2 * u + 1) * HALF_PAD : (2 * u + 2) * HALF_PAD, :] = right.astype(BF16)

    def pair(n, _):
        at = pl.ds(pl.multiple_of(n * 2 * LANES, 2 * LANES), 2 * LANES)
        result = lax.dot_general(
            held[...], w_out[at, :], CONTRACT_COLUMNS, preferred_element_type=F32
        )
        row = lax.broadcasted_iota(jnp.int32, (PAD, LANES), 0)
        for u in range(groups):
            limit = left_of(lengths, place, u, frames)
            base = u * span
            for cb in (2 * n, 2 * n + 1):
                block = slab.at[u, cb]
                before, after = sides(u, slice(0, PAD), lane(cb))
                block[0:PAD, :] = jnp.where(row - PAD < limit, before, 0.0)
                block[PAD + frames :, :] = jnp.where(row + frames < limit, after, 0.0)
                weight = [weights[j : j + 1, lane(cb)] for j in range(taps)]
                for start in (0, span - PAD):
                    to = slice(base + start, base + start + PAD)
                    hat[to, lane(cb)] = depthwise(block, weight, start, PAD, range(taps))
        for u in range(groups):
            base = u * span
            near = 2 * u * HALF_PAD
            grad[base : base + HALF_PAD, at] = result[near : near + HALF_PAD]
            grad[base + span - HALF_PAD : base + span, at] = result[
                near + HALF_PAD : near + 2 * HALF_PAD
            ]
        return 0

    lax.fori_loop(0, blocks // 2, pair, 0)
    for u in range(groups):
        rows = slice(u * span, (u + 1) * span)
        total = hat[rows, 0:LANES]
        for cb in range(1, blocks):
            total = total + hat[rows, cb * LANES : (cb + 1) * LANES]
        mean[rows, :] = row_mean(total, width)
        total = None
        for cb in range(blocks):
            centered = hat[rows, cb * LANES : (cb + 1) * LANES] - mean[rows, :]
            total = centered * centered if total is None else total + centered * centered
        inverse[rows, :] = lax.rsqrt(row_mean(total, width) + EPSILON)

    def normalize(cb, _):
        outs = []
        for u in range(groups):
            limit = left_of(lengths, place, u, frames)
            rows = slice(u * span, (u + 1) * span)
            normed = (hat[rows, lane(cb)] - mean[rows, :]) * inverse[rows, :]
            hat[rows, lane(cb)] = normed
            pre = normed[HALF_PAD : HALF_PAD + frames] * (0.5 * gain[:, lane(cb)])
            out = pre * jnp.tanh(pre) + pre
            row = lax.broadcasted_iota(jnp.int32, (frames, LANES), 0)
            outs.append(jnp.where(row < limit, out, 0.0).astype(BF16))
        message[lane(cb), :] = jnp.concatenate(outs, axis=0).T
        return 0

    lax.fori_loop(0, blocks, normalize, 0)


def product_kernel(place, near, cotangent, far, packed, out, scratch, held, sent):
    rows, width = cotangent.shape
    half = width // 2
    pairs = scratch.shape[0]
    step = 24 * pairs
    wide = 2 * LANES
    first = lax.broadcasted_iota(jnp.int32, (pairs, 8, LANES), 1) < 4
    pick = lambda a, b: jnp.where(first, a, b)
    roll = lambda a: pltpu.roll(a, 4, 1)
    mine = pl.ds(pl.multiple_of((place[0] & 1) * half, LANES), half)

    def copy(s):
        return pltpu.make_async_copy(held.at[s], out.at[pl.ds(s * pairs, pairs)], sent.at[s])

    def chunk(s, _):
        at = pl.ds(pl.multiple_of(s * step, step), step)
        theirs = [far[width + n * rows : width + (n + 1) * rows, :] for n in range(half // rows)]
        left = jnp.concatenate([near[at, :], far[at, :]], axis=1)
        right = jnp.concatenate([cotangent[:, mine], jnp.concatenate(theirs, axis=1)], axis=0)
        small = packed[pl.ds(s * pairs, pairs)]
        before = small
        split = 12 * half // LANES
        for q in range(half // wide):
            result = jnp.dot(
                left, right[:, q * wide : (q + 1) * wide], preferred_element_type=F32
            )

            def parts(k):
                cut = result[:, k * LANES : (k + 1) * LANES].reshape(pairs, 3, 8, LANES)
                return cut[:, 0], cut[:, 1], cut[:, 2]

            a, b, c = parts(0)
            d, e, f = parts(1)
            rd, re, rf = roll(d), roll(e), roll(f)
            for i, tile in enumerate((a, pick(b, rd), pick(rd, re))):
                scratch[:, 24 * q + 8 * i : 24 * q + 8 * i + 8, :] = tile
            for i, tile in enumerate((pick(before, b), c, pick(re, rf))):
                spot = split + 24 * q + 8 * i
                scratch[:, spot : spot + 8, :] = tile
            before = rf
        scratch[:, 2 * split : 2 * split + 8, :] = pick(before, small)
        held[s] = scratch[...].astype(BF16)
        copy(s).start()
        return 0

    lax.fori_loop(0, width // step, chunk, 0)
    for s in range(width // step):
        copy(s).wait()


def backward_kernel(lengths, place, grad, hat, inverse, gain, slab, term, work, sums):
    groups, blocks, span = slab.shape[:3]
    width = blocks * LANES
    frames = span - 2 * HALF_PAD
    sums[...] = jnp.zeros_like(sums)
    part = span // 2

    def norm(n, _):
        u, start = n // 2, (n % 2) * part
        at = pl.ds(pl.multiple_of(n * part, TILE), part)
        limit = left_of(lengths, place, u, frames)
        row = start - HALF_PAD + lax.broadcasted_iota(jnp.int32, (part, LANES), 0)
        keep = row < limit
        inside = (row >= 0) & (row < frames)
        first = second = None
        for cb in range(blocks):
            here = slice(cb * LANES, (cb + 1) * LANES)
            normed = hat[at, here]
            halved = normed * (0.5 * gain[:, here])
            turn = jnp.tanh(halved)
            gate = 0.5 * turn + 0.5
            grad_pre = jnp.where(keep, grad[at, here], 0.0) * (gate * (1.0 + halved * (1.0 - turn)))
            term_part = jnp.where(inside, grad_pre * normed, 0.0)
            sums[:, here] += jnp.sum(term_part.reshape(part // 8, 8, LANES), axis=0)
            scaled = grad_pre * gain[:, here]
            work[at, here] = scaled
            first = scaled if first is None else first + scaled
            second = scaled * normed if second is None else second + scaled * normed
        mean = row_mean(first, width)
        slope = row_mean(second, width)
        inv = inverse[at, :]
        for cb in range(blocks):
            here = slice(cb * LANES, (cb + 1) * LANES)
            result = inv * (work[at, here] - mean - hat[at, here] * slope)
            to = pl.ds(pl.multiple_of(start, TILE), part)
            slab[u, cb, to, :] = result.astype(BF16).astype(F32)
        return 0

    lax.fori_loop(0, 2 * groups, norm, 0)
    term[...] = jnp.sum(sums[...], axis=0, keepdims=True)


def terms_kernel(
    grad, slab, term, packed, square, columns, rest, values, cells, taken
):
    groups, blocks, span = grad.shape[:3]
    frames = span - 2 * HALF_PAD
    taps = 31
    some = frames // 2
    reach = cells.shape[2]
    start = PAD - taps // 2
    taken[...] = jnp.zeros_like(taken)

    def channel(cb, _):
        for u in range(groups):
            even = grad[u, cb, pl.ds(HALF_PAD, some, stride=2), :]
            odd = grad[u, cb, pl.ds(HALF_PAD + 1, some, stride=2), :]
            values[0, u], values[1, u], values[2, u] = even, odd, even + odd
            here = slab[u, cb, pl.ds(start, reach, stride=2), :]
            there = slab[u, cb, pl.ds(start + 1, reach, stride=2), :]
            after = slab[u, cb, pl.ds(start + 2, reach, stride=2), :]
            cells[0, u], cells[1, u], cells[2, u] = here, there, there + after
        for kind, lags in enumerate((taps // 2 + 1, taps // 2 + 1, taps // 2)):
            for r in range(8):
                chosen = [i for i in range(r, lags, 8)]
                totals = [None] * len(chosen)
                for u in range(groups):
                    for m in range(0, some, 8):
                        value = values[kind, u, m : m + 8, :]
                        for n, i in enumerate(chosen):
                            part = value * cells[kind, u, pl.ds(m + i, 8), :]
                            totals[n] = part if totals[n] is None else totals[n] + part
                for n, i in enumerate(chosen):
                    taken[kind, 8 * i : 8 * i + 8, :] = totals[n]
        sums = []
        for kind in range(3):
            line = taken[kind, pl.ds(0, 16, stride=8), :]
            for k in range(1, 8):
                line = line + taken[kind, pl.ds(k, 16, stride=8), :]
            sums.append(line)
        evens = sums[0] + sums[1]
        odds = sums[2] - pltpu.roll(sums[0], 15, 0) - sums[1]
        square[cb, pl.ds(0, 16, stride=2), :] = evens
        square[cb, pl.ds(1, 16, stride=2), :] = odds
        square[cb, taps : taps + 1, :] = term[:, lane(cb)]
        return 0

    lax.fori_loop(0, blocks, channel, 0)
    quarter = blocks * LANES // 4
    spot = lax.broadcasted_iota(jnp.int32, (32, LANES), 1) // 32
    lines = []
    for g in range(blocks // 4):
        columns[g] = square[4 * g : 4 * g + 4].reshape(LANES, LANES).T
        for b in range(4):
            line = jnp.zeros((32, LANES), F32)
            for m in range(4):
                taken_rows = columns[g, pl.ds(m, 32, stride=4), :]
                line = jnp.where(spot == m, pltpu.roll(taken_rows, 32 * ((m - b) % 4), 1), line)
            lines.append(line)
    total = jnp.concatenate(lines, axis=0)
    rest[8 : 8 + quarter, :] = total
    row = lax.broadcasted_iota(jnp.int32, (8, LANES), 0)
    for p in range(packed.shape[0]):
        upper = rest[6 * p + 8 : 6 * p + 16, :]
        lower = rest[6 * p + 7 : 6 * p + 15, :]
        packed[p] = jnp.where(row < 3, upper, jnp.where((row > 3) & (row < 7), lower, 0.0))


def input_kernel(lengths, place, grad, hidden, weights, out):
    groups, frames, _ = hidden.shape
    blocks = grad.shape[1]
    taps = weights.shape[0]
    chunk = 64
    for u in range(groups):
        limit = left_of(lengths, place, u, frames)

        def channel(cb, _):
            block = grad.at[u, cb]
            weight = [weights[j : j + 1, lane(cb)] for j in range(taps)]
            for start in range(0, frames, chunk):
                at = slice(start, start + chunk)
                total = depthwise(block, weight, start, chunk, range(taps - 1, -1, -1))
                row = start + lax.broadcasted_iota(jnp.int32, (chunk, LANES), 0)
                total = jnp.where(row < limit, total, 0.0)
                linear = hidden[u, at, lane(cb)].astype(F32)
                gate = sigmoid(hidden[u, at, lane(blocks + cb)].astype(F32))
                opened = total * gate
                out[u, at, lane(cb)] = opened.astype(BF16)
                out[u, at, lane(blocks + cb)] = (opened * linear * (1.0 - gate)).astype(BF16)
            return 0

        lax.fori_loop(0, blocks, channel, 0)


def sum_kernel(factor, got, out, taps_out, gain_out, total, held, arrived):
    own = out.shape[0]
    slots, step = held.shape[:2]

    def copy(i):
        return pltpu.make_async_copy(got.at[pl.ds(i * step, step)], held.at[i], arrived.at[i])

    for i in range(slots):
        copy(i).start()
    total[...] = jnp.zeros_like(total)

    def add(i, _):
        copy(i).wait()
        for k in range(0, step, 4):
            total[...] += jnp.sum(held[i, k : k + 4].astype(F32), axis=0)
        return 0

    lax.fori_loop(0, slots, add, 0)
    tall = total.shape[0] // 2
    blocks = (tall - 4) // own
    for side in range(2):
        for k in range(blocks):
            at = (side * blocks + k) * LANES
            start = tall * side + own * k
            out[:, at : at + LANES] = total[start : start + own, :] * factor
    small = (total[tall - 4 : tall - 1, :] + total[2 * tall - 4 : 2 * tall - 1, :]) * factor
    taps = taps_out.shape[1]
    spot = lax.broadcasted_iota(jnp.int32, (1, LANES), 1)
    gains = jnp.zeros((1, LANES), F32)
    for r in range(3):
        for m in range(4):
            c = 4 * r + m
            turned = pltpu.roll(small[r : r + 1, :], (LANES - 32 * m) % LANES, 1)
            taps_out[c : c + 1, :] = turned[:, :taps]
            gains = jnp.where(spot == c, pltpu.roll(turned, (c - taps) % LANES, 1), gains)
    gain_out[...] = gains[:, :own]


def local(hidden, cotangent, lengths, kernel, conv_gain, w_out):
    groups, frames, double = hidden.shape
    width = double // 2
    half = width // 2
    blocks = width // LANES
    taps = kernel.shape[1]
    seq_count = lax.axis_size("seq")
    devices = lax.axis_size("dp") * seq_count
    own = width // devices
    rows = groups * frames
    span = frames + 2 * HALF_PAD
    length = frames + 2 * PAD
    tall = own * half // LANES + 4
    ends = seq_count - 1
    swap = [(i, i ^ 1) for i in range(seq_count)]
    place = lax.axis_index("seq")
    conv_flops = 2 * taps * rows * width

    spot = place.reshape(1)
    flat = cotangent.reshape(rows, width)
    inner_edge, outer_edge, weights = call(
        edges_kernel,
        [SMEM, HBM, HBM, HBM],
        [shape((groups, PAD + HALF_PAD, width), BF16)] * 2 + [shape((taps, width), F32)],
        [
            pltpu.VMEM((2, groups, PAD, double), BF16),
            pltpu.VMEM((2, groups, HALF_PAD, width), BF16),
            pltpu.SemaphoreType.DMA((2, 2, groups)),
            pltpu.SemaphoreType.DMA,
        ],
        1 << 20,
        4,
    )(spot, far_memory(hidden), far_memory(cotangent), far_memory(kernel.T))
    bridge = [(i, i + 1) for i in range(1, ends, 2)]
    across = lax.ppermute(outer_edge, "seq", bridge + [(j, i) for i, j in bridge])
    inside = lax.ppermute(inner_edge, "seq", swap)
    gain = conv_gain.reshape(1, width)
    slab_shape = shape((groups, blocks, length, LANES), F32)
    wide_shape = shape((groups * span, width), F32)
    gated, inner, swish, w_near = call(
        gate_kernel,
        [SMEM, SMEM] + [VMEM] * 3 + [HBM],
        [slab_shape, wide_shape, wide_shape, shape((width, width), BF16)],
        [
            pltpu.SemaphoreType.DMA((blocks // 2,)),
            pltpu.VMEM((groups, 3, 104, LANES), F32),
            pltpu.VMEM((groups, 88, LANES), F32),
            pltpu.VMEM((groups, 160, LANES), F32),
        ],
        conv_flops,
        4,
    )(lengths, spot, hidden, weights, flat, far_memory(w_out))
    slab, hat, grad_swish, inverse, message = call(
        forward_kernel,
        [SMEM, SMEM] + [VMEM] * 9,
        [
            slab_shape,
            wide_shape,
            wide_shape,
            shape((groups * span, LANES), F32),
            shape((width + half, rows), BF16),
        ],
        [pltpu.VMEM((groups * span, LANES), F32), pltpu.VMEM((2 * groups * HALF_PAD, width), BF16)],
        conv_flops,
        4,
        {2: 0, 3: 1, 4: 2},
    )(lengths, spot, gated, inner, swish, inside, across, weights, gain, flat, w_near)
    far = lax.ppermute(message, "seq", swap)
    grad, term_conv = call(
        backward_kernel,
        [SMEM, SMEM] + [VMEM] * 4,
        [shape((groups, blocks, span, LANES), F32), shape((1, width), F32)],
        [pltpu.VMEM((groups * span, width), F32), pltpu.VMEM((8, width), F32)],
        20 * rows * width,
        6,
    )(lengths, spot, grad_swish, hat, inverse, gain)
    packed = call(
        terms_kernel,
        [VMEM] * 3,
        shape((devices // 2, 8, LANES), F32),
        [
            pltpu.VMEM((blocks, 32, LANES), F32),
            pltpu.VMEM((blocks // 4, LANES, LANES), F32),
            pltpu.VMEM((width // 4 + 16, LANES), F32),
            pltpu.VMEM((3, groups, frames // 2, LANES), F32),
            pltpu.VMEM((3, groups, frames // 2 + 16, LANES), F32),
            pltpu.VMEM((3, 128, LANES), F32),
        ],
        conv_flops,
        6,
    )(grad, slab, term_conv)
    pairs = 32
    steps = devices // (2 * pairs)
    pieces = call(
        product_kernel,
        [SMEM] + [VMEM] * 4,
        pltpu.HBM((devices // 2, 2 * tall, LANES), BF16),
        [
            pltpu.VMEM((pairs, 2 * tall, LANES), F32),
            pltpu.VMEM((steps, pairs, 2 * tall, LANES), BF16),
            pltpu.SemaphoreType.DMA((steps,)),
        ],
        4 * rows * width * half,
        10,
        out_specs=HBM,
    )(spot, message, flat, far, packed)
    blocked = pieces.reshape(devices, tall // 4, 4, LANES)
    got = lax.all_to_all(blocked, AXES, 0, 0, tiled=True)
    grad_hidden = call(
        input_kernel,
        [SMEM, SMEM] + [VMEM] * 3,
        shape((groups, frames, double), BF16),
        [],
        conv_flops,
        4,
    )(lengths, spot, grad, hidden, weights)

    factor = 1.0 / math.sqrt(groups * lax.axis_size("dp") * frames * seq_count)
    slots = 4
    grad_w, grad_kernel, grad_gain = call(
        functools.partial(sum_kernel, factor),
        [HBM],
        [shape((own, width), F32), shape((own, taps), F32), shape((1, own), F32)],
        [
            pltpu.VMEM((2 * tall, LANES), F32),
            pltpu.VMEM((slots, devices // 2 // slots, 2 * tall, LANES), BF16),
            pltpu.SemaphoreType.DMA((slots,)),
        ],
        1 << 20,
        6,
    )(far_memory(got.reshape(devices // 2, 2 * tall, LANES)))
    return grad_hidden, grad_w, grad_kernel, grad_gain.reshape(own)


def solution(mesh):
    in_specs = (P("dp", "seq", None), P("dp", "seq", None), P("dp"), P(), P(), P())
    out_specs = (P("dp", "seq", None), P(AXES, None), P(AXES, None), P(AXES))
    return jax.shard_map(local, mesh=mesh, in_specs=in_specs, out_specs=out_specs, check_vma=False)
```

```python
import functools
import math

import jax
import jax.numpy as jnp
from jax import lax
from jax.experimental import pallas as pl
from jax.experimental.pallas import tpu as pltpu
from jax.sharding import PartitionSpec as P

EPSILON = 1e-05
AXES = ("dp", "seq")
LANES = 128
HALF_PAD = 16
PAD = 32
TILE = 16
F32, BF16 = jnp.float32, jnp.bfloat16
VMEM = pl.BlockSpec(memory_space=pltpu.VMEM)
SMEM = pl.BlockSpec(memory_space=pltpu.SMEM)
HBM = pl.BlockSpec(memory_space=pltpu.HBM)


def sigmoid(x):
    return 0.5 * jnp.tanh(0.5 * x) + 0.5


def left_of(lengths, place, u, frames):
    return lengths[u] - place[0] * frames


def lane(block):
    return pl.ds(pl.multiple_of(block * LANES, LANES), LANES)


def call(kernel, in_specs, out_shape, scratch, flops, limit, aliases=None, out_specs=None):
    return pl.pallas_call(
        kernel,
        in_specs=in_specs,
        out_specs=out_specs or jax.tree.map(lambda _: VMEM, out_shape),
        out_shape=out_shape,
        scratch_shapes=scratch,
        input_output_aliases=aliases or {},
        cost_estimate=pl.CostEstimate(flops=flops, bytes_accessed=8 << 20, transcendentals=0),
        compiler_params=pltpu.CompilerParams(vmem_limit_bytes=limit << 20),
    )


def shape(dims, dtype):
    return jax.ShapeDtypeStruct(dims, dtype)


def far_memory(array):
    return pltpu.with_memory_space_constraint(array, pltpu.HBM)


def depthwise(slab, weight, start, rows, order):
    total = None
    for j, row in enumerate(order):
        term = slab[pl.ds(start + 1 + j, rows), :] * weight[row]
        total = term if total is None else total + term
    return total


def edges_kernel(
    place, hidden, cotangent, source, inside, across, weights, cells, upstream, arrived, loaded
):
    groups, frames, double = hidden.shape
    width = double // 2
    core = place[0] & 1
    copies = []
    for side, last in enumerate((core, 1 - core)):
        start = pl.multiple_of(last * (frames - PAD), TILE)
        near = pl.multiple_of(last * (frames - HALF_PAD), TILE)
        for u in range(groups):
            copies.append(
                (
                    pltpu.make_async_copy(
                        hidden.at[u, pl.ds(start, PAD)], cells.at[side, u], arrived.at[0, side, u]
                    ),
                    pltpu.make_async_copy(
                        cotangent.at[u, pl.ds(near, HALF_PAD)],
                        upstream.at[side, u],
                        arrived.at[1, side, u],
                    ),
                )
            )
    for first, second in copies:
        first.start()
        second.start()
    taps = pltpu.make_async_copy(source, weights, loaded)
    taps.start()
    n = 0
    for side, out in enumerate((across, inside)):
        for u in range(groups):
            copies[n][0].wait()
            for cb in range(width // LANES):
                here = slice(cb * LANES, (cb + 1) * LANES)
                there = slice(width + cb * LANES, width + (cb + 1) * LANES)
                linear = cells[side, u, :, here].astype(F32)
                gate = sigmoid(cells[side, u, :, there].astype(F32))
                out[u, 0:PAD, here] = (linear * gate).astype(BF16)
            copies[n][1].wait()
            out[u, PAD:, :] = upstream[side, u]
            n += 1
    taps.wait()


CONTRACT_COLUMNS = (((1,), (1,)), ((), ()))


def inner_rows(block, weights, cb, cells, evens, mixed, some, taps):
    reach = cells.shape[1]
    here = block[pl.ds(PAD + 1, reach, stride=2), :]
    there = block[pl.ds(PAD + 2, reach, stride=2), :]
    after = block[pl.ds(PAD + 3, reach, stride=2), :]
    cells[0], cells[1], cells[2] = here, there, there + after
    weight = [weights[j : j + 1, lane(cb)] for j in range(taps)]
    paired = [weight[j] + weight[j + 1] for j in range(0, taps - 1, 2)] + [weight[taps - 1]]

    def run(kind, rows, chosen):
        total = None
        for i, factor in enumerate(chosen):
            part = cells[kind, pl.ds(i, rows), :] * factor
            total = part if total is None else total + part
        return total

    evens[...] = run(0, some + 8, weight[0::2])
    odd = run(1, some, weight[1::2])
    mixed[pl.ds(0, some, stride=2), :] = evens[0:some, :] + odd
    both = run(2, some, paired)
    mixed[pl.ds(1, some, stride=2), :] = both - evens[1 : some + 1, :] - odd


def gate_kernel(
    lengths, place, hidden, weights, cotangent, source, slab, hat, grad, w_out, arrived, cells, evens, mixed
):
    groups, frames, double = hidden.shape
    taps = weights.shape[0]
    width = double // 2
    blocks = width // LANES
    some = frames // 2 - HALF_PAD

    def copy(n):
        at = pl.ds(pl.multiple_of(n * 2 * LANES, 2 * LANES), 2 * LANES)
        return pltpu.make_async_copy(source.at[at], w_out.at[at], arrived.at[n])

    for n in range(blocks // 2):
        copy(n).start()

    def pair(n, _):
        at = pl.ds(pl.multiple_of(n * 2 * LANES, 2 * LANES), 2 * LANES)
        copy(n).wait()
        swish = lax.dot_general(
            cotangent[...], w_out[at, :], CONTRACT_COLUMNS, preferred_element_type=F32
        )
        for u in range(groups):
            limit = left_of(lengths, place, u, frames)
            base = u * frames
            for cb in (2 * n, 2 * n + 1):
                row = lax.broadcasted_iota(jnp.int32, (frames, LANES), 0)
                linear = hidden[u, :, lane(cb)].astype(F32)
                gate = sigmoid(hidden[u, :, lane(blocks + cb)].astype(F32))
                glu = jnp.where(row < limit, linear * gate, 0.0)
                block = slab.at[u, cb]
                block[PAD : PAD + frames, :] = glu.astype(BF16).astype(F32)
                inner_rows(
                    block, weights, cb, cells.at[u], evens.at[u], mixed.at[u], some, taps
                )
                to = slice(base + HALF_PAD, base + frames - HALF_PAD)
                hat[to, lane(cb)] = mixed[u]
        grad[:, at] = swish
        return 0

    lax.fori_loop(0, blocks // 2, pair, 0)


def row_mean(values, width):
    mean = jnp.sum(values, axis=-1, keepdims=True) * (1.0 / width)
    return jnp.broadcast_to(mean, values.shape)


def sides(place, inside, across, u, rows, lanes):
    first = (place[0] & 1) == 0
    one, two = inside[u, rows, lanes].astype(F32), across[u, rows, lanes].astype(F32)
    return jnp.where(first, two, one), jnp.where(first, one, two)


def forward_kernel(
    lengths,
    place,
    gated,
    inner,
    inside,
    across,
    weights,
    gain,
    cotangent,
    slab,
    hat,
    inverse,
    message,
    mean,
):
    groups, blocks, length = slab.shape[:3]
    taps = weights.shape[0]
    width = blocks * LANES
    half = width // 2
    frames = length - 2 * PAD
    rows = groups * frames
    for side in range(half // rows):
        theirs = (1 - (place[0] & 1)) * half + side * rows
        part = cotangent[:, pl.ds(pl.multiple_of(theirs, LANES), rows)]
        message[width + side * rows : width + (side + 1) * rows, :] = part

    def pair(n, _):
        row = lax.broadcasted_iota(jnp.int32, (PAD, LANES), 0)
        for cb in (2 * n, 2 * n + 1):
            weight = [weights[j : j + 1, lane(cb)] for j in range(taps)]
            for u in range(groups):
                limit = left_of(lengths, place, u, frames)
                base = u * frames
                block = slab.at[u, cb]
                before, after = sides(place, inside, across, u, slice(0, PAD), lane(cb))
                block[0:PAD, :] = jnp.where(row - PAD < limit, before, 0.0)
                block[PAD + frames :, :] = jnp.where(row + frames < limit, after, 0.0)
                for start in (0, frames - HALF_PAD):
                    to = slice(base + start, base + start + HALF_PAD)
                    hat[to, lane(cb)] = depthwise(
                        block, weight, HALF_PAD + start, HALF_PAD, range(taps)
                    )
        return 0

    lax.fori_loop(0, blocks // 2, pair, 0)
    for u in range(groups):
        rows = slice(u * frames, (u + 1) * frames)
        total = hat[rows, 0:LANES]
        for cb in range(1, blocks):
            total = total + hat[rows, cb * LANES : (cb + 1) * LANES]
        mean[rows, :] = row_mean(total, width)
        total = None
        for cb in range(blocks):
            centered = hat[rows, cb * LANES : (cb + 1) * LANES] - mean[rows, :]
            total = centered * centered if total is None else total + centered * centered
        inverse[rows, :] = lax.rsqrt(row_mean(total, width) + EPSILON)

    def normalize(cb, _):
        outs = []
        for u in range(groups):
            limit = left_of(lengths, place, u, frames)
            rows = slice(u * frames, (u + 1) * frames)
            normed = (hat[rows, lane(cb)] - mean[rows, :]) * inverse[rows, :]
            hat[rows, lane(cb)] = normed
            pre = normed * (0.5 * gain[:, lane(cb)])
            out = pre * jnp.tanh(pre) + pre
            row = lax.broadcasted_iota(jnp.int32, (frames, LANES), 0)
            outs.append(jnp.where(row < limit, out, 0.0).astype(BF16))
        message[lane(cb), :] = jnp.concatenate(outs, axis=0).T
        return 0

    lax.fori_loop(0, blocks, normalize, 0)


def fringe_kernel(
    lengths, place, grad, slab, inside, across, weights, gain, w_out, out, held, swish, hat
):
    groups, blocks, span = out.shape[:3]
    taps = weights.shape[0]
    width = blocks * LANES
    frames = span - 2 * HALF_PAD
    for u in range(groups):
        pieces = sides(place, inside, across, u, slice(PAD, PAD + HALF_PAD), slice(0, width))
        for n, piece in enumerate(pieces):
            at = (2 * u + n) * HALF_PAD
            held[at : at + HALF_PAD, :] = piece.astype(BF16)

    def pair(n, _):
        at = pl.ds(pl.multiple_of(n * 2 * LANES, 2 * LANES), 2 * LANES)
        swish[:, at] = lax.dot_general(
            held[...], w_out[at, :], CONTRACT_COLUMNS, preferred_element_type=F32
        )
        for cb in (2 * n, 2 * n + 1):
            weight = [weights[j : j + 1, lane(cb)] for j in range(taps)]
            for u in range(groups):
                for side, start in enumerate((0, span - HALF_PAD)):
                    to = (2 * u + side) * HALF_PAD
                    hat[to : to + HALF_PAD, lane(cb)] = depthwise(
                        slab.at[u, cb], weight, start, HALF_PAD, range(taps)
                    )
        return 0

    lax.fori_loop(0, blocks // 2, pair, 0)
    for u in range(groups):
        limit = left_of(lengths, place, u, frames)
        for side, start in enumerate((0, span - HALF_PAD)):
            at = slice((2 * u + side) * HALF_PAD, (2 * u + side + 1) * HALF_PAD)
            values = hat[at, :]
            centered = values - jnp.sum(values, axis=-1, keepdims=True) * (1.0 / width)
            spread = jnp.sum(centered * centered, axis=-1, keepdims=True) * (1.0 / width)
            inv = lax.rsqrt(spread + EPSILON)
            normed = centered * inv
            halved = normed * (0.5 * gain[...])
            turn = jnp.tanh(halved)
            gate = 0.5 * turn + 0.5
            row = start - HALF_PAD + lax.broadcasted_iota(jnp.int32, (HALF_PAD, width), 0)
            upstream = jnp.where(row < limit, swish[at, :], 0.0)
            scaled = upstream * (gate * (1.0 + halved * (1.0 - turn))) * gain[...]
            mean = jnp.sum(scaled, axis=-1, keepdims=True) * (1.0 / width)
            slope = jnp.sum(scaled * normed, axis=-1, keepdims=True) * (1.0 / width)
            result = (inv * (scaled - mean - normed * slope)).astype(BF16).astype(F32)
            for cb in range(blocks):
                out[u, cb, start : start + HALF_PAD, :] = result[:, cb * LANES : (cb + 1) * LANES]


def product_kernel(place, near, cotangent, far, packed, out, scratch, held, sent):
    rows, width = cotangent.shape
    half = width // 2
    pairs = scratch.shape[0]
    step = 24 * pairs
    wide = 2 * LANES
    first = lax.broadcasted_iota(jnp.int32, (pairs, 8, LANES), 1) < 4
    pick = lambda a, b: jnp.where(first, a, b)
    roll = lambda a: pltpu.roll(a, 4, 1)
    mine = pl.ds(pl.multiple_of((place[0] & 1) * half, LANES), half)

    def copy(s):
        return pltpu.make_async_copy(held.at[s], out.at[pl.ds(s * pairs, pairs)], sent.at[s])

    def chunk(s, _):
        at = pl.ds(pl.multiple_of(s * step, step), step)
        theirs = [far[width + n * rows : width + (n + 1) * rows, :] for n in range(half // rows)]
        left = jnp.concatenate([near[at, :], far[at, :]], axis=1)
        right = jnp.concatenate([cotangent[:, mine], jnp.concatenate(theirs, axis=1)], axis=0)
        small = packed[pl.ds(s * pairs, pairs)]
        before = small
        split = 12 * half // LANES
        for q in range(half // wide):
            result = jnp.dot(
                left, right[:, q * wide : (q + 1) * wide], preferred_element_type=F32
            )

            def parts(k):
                cut = result[:, k * LANES : (k + 1) * LANES].reshape(pairs, 3, 8, LANES)
                return cut[:, 0], cut[:, 1], cut[:, 2]

            a, b, c = parts(0)
            d, e, f = parts(1)
            rd, re, rf = roll(d), roll(e), roll(f)
            for i, tile in enumerate((a, pick(b, rd), pick(rd, re))):
                scratch[:, 24 * q + 8 * i : 24 * q + 8 * i + 8, :] = tile
            for i, tile in enumerate((pick(before, b), c, pick(re, rf))):
                spot = split + 24 * q + 8 * i
                scratch[:, spot : spot + 8, :] = tile
            before = rf
        scratch[:, 2 * split : 2 * split + 8, :] = pick(before, small)
        held[s] = scratch[...].astype(BF16)
        copy(s).start()
        return 0

    lax.fori_loop(0, width // step, chunk, 0)
    for s in range(width // step):
        copy(s).wait()


def backward_kernel(lengths, place, grad, hat, inverse, gain, slab, term, work, sums):
    groups, blocks, span = slab.shape[:3]
    width = blocks * LANES
    frames = span - 2 * HALF_PAD
    sums[...] = jnp.zeros_like(sums)
    part = frames // 2

    def norm(n, _):
        u, start = n // 2, (n % 2) * part
        at = pl.ds(pl.multiple_of(n * part, TILE), part)
        limit = left_of(lengths, place, u, frames)
        row = start + lax.broadcasted_iota(jnp.int32, (part, LANES), 0)
        keep = row < limit
        first = second = None
        for cb in range(blocks):
            here = slice(cb * LANES, (cb + 1) * LANES)
            normed = hat[at, here]
            halved = normed * (0.5 * gain[:, here])
            turn = jnp.tanh(halved)
            gate = 0.5 * turn + 0.5
            grad_pre = jnp.where(keep, grad[at, here], 0.0) * (gate * (1.0 + halved * (1.0 - turn)))
            term_part = grad_pre * normed
            sums[:, here] += jnp.sum(term_part.reshape(part // 8, 8, LANES), axis=0)
            scaled = grad_pre * gain[:, here]
            work[at, here] = scaled
            first = scaled if first is None else first + scaled
            second = scaled * normed if second is None else second + scaled * normed
        mean = row_mean(first, width)
        slope = row_mean(second, width)
        inv = inverse[at, :]
        for cb in range(blocks):
            here = slice(cb * LANES, (cb + 1) * LANES)
            result = inv * (work[at, here] - mean - hat[at, here] * slope)
            to = pl.ds(pl.multiple_of(HALF_PAD + start, TILE), part)
            slab[u, cb, to, :] = result.astype(BF16).astype(F32)
        return 0

    lax.fori_loop(0, 2 * groups, norm, 0)
    term[...] = jnp.sum(sums[...], axis=0, keepdims=True)


def terms_kernel(
    grad, slab, term, packed, square, columns, rest, values, cells, taken
):
    groups, blocks, span = grad.shape[:3]
    frames = span - 2 * HALF_PAD
    taps = 31
    some = frames // 2
    reach = cells.shape[2]
    start = PAD - taps // 2
    taken[...] = jnp.zeros_like(taken)

    def channel(cb, _):
        for u in range(groups):
            even = grad[u, cb, pl.ds(HALF_PAD, some, stride=2), :]
            odd = grad[u, cb, pl.ds(HALF_PAD + 1, some, stride=2), :]
            values[0, u], values[1, u], values[2, u] = even, odd, even + odd
            here = slab[u, cb, pl.ds(start, reach, stride=2), :]
            there = slab[u, cb, pl.ds(start + 1, reach, stride=2), :]
            after = slab[u, cb, pl.ds(start + 2, reach, stride=2), :]
            cells[0, u], cells[1, u], cells[2, u] = here, there, there + after
        for kind, lags in enumerate((taps // 2 + 1, taps // 2 + 1, taps // 2)):
            for r in range(8):
                chosen = [i for i in range(r, lags, 8)]
                totals = [None] * len(chosen)
                for u in range(groups):
                    for m in range(0, some, 8):
                        value = values[kind, u, m : m + 8, :]
                        for n, i in enumerate(chosen):
                            part = value * cells[kind, u, pl.ds(m + i, 8), :]
                            totals[n] = part if totals[n] is None else totals[n] + part
                for n, i in enumerate(chosen):
                    taken[kind, 8 * i : 8 * i + 8, :] = totals[n]
        sums = []
        for kind in range(3):
            line = taken[kind, pl.ds(0, 16, stride=8), :]
            for k in range(1, 8):
                line = line + taken[kind, pl.ds(k, 16, stride=8), :]
            sums.append(line)
        evens = sums[0] + sums[1]
        odds = sums[2] - pltpu.roll(sums[0], 15, 0) - sums[1]
        square[cb, pl.ds(0, 16, stride=2), :] = evens
        square[cb, pl.ds(1, 16, stride=2), :] = odds
        square[cb, taps : taps + 1, :] = term[:, lane(cb)]
        return 0

    lax.fori_loop(0, blocks, channel, 0)
    quarter = blocks * LANES // 4
    spot = lax.broadcasted_iota(jnp.int32, (32, LANES), 1) // 32
    lines = []
    for g in range(blocks // 4):
        columns[g] = square[4 * g : 4 * g + 4].reshape(LANES, LANES).T
        for b in range(4):
            line = jnp.zeros((32, LANES), F32)
            for m in range(4):
                taken_rows = columns[g, pl.ds(m, 32, stride=4), :]
                line = jnp.where(spot == m, pltpu.roll(taken_rows, 32 * ((m - b) % 4), 1), line)
            lines.append(line)
    total = jnp.concatenate(lines, axis=0)
    rest[8 : 8 + quarter, :] = total
    row = lax.broadcasted_iota(jnp.int32, (8, LANES), 0)
    for p in range(packed.shape[0]):
        upper = rest[6 * p + 8 : 6 * p + 16, :]
        lower = rest[6 * p + 7 : 6 * p + 15, :]
        packed[p] = jnp.where(row < 3, upper, jnp.where((row > 3) & (row < 7), lower, 0.0))


def input_kernel(lengths, place, grad, hidden, weights, out):
    groups, frames, _ = hidden.shape
    blocks = grad.shape[1]
    taps = weights.shape[0]
    chunk = 64
    for u in range(groups):
        limit = left_of(lengths, place, u, frames)

        def channel(cb, _):
            block = grad.at[u, cb]
            weight = [weights[j : j + 1, lane(cb)] for j in range(taps)]
            for start in range(0, frames, chunk):
                at = slice(start, start + chunk)
                total = depthwise(block, weight, start, chunk, range(taps - 1, -1, -1))
                row = start + lax.broadcasted_iota(jnp.int32, (chunk, LANES), 0)
                total = jnp.where(row < limit, total, 0.0)
                linear = hidden[u, at, lane(cb)].astype(F32)
                gate = sigmoid(hidden[u, at, lane(blocks + cb)].astype(F32))
                opened = total * gate
                out[u, at, lane(cb)] = opened.astype(BF16)
                out[u, at, lane(blocks + cb)] = (opened * linear * (1.0 - gate)).astype(BF16)
            return 0

        lax.fori_loop(0, blocks, channel, 0)


def sum_kernel(factor, got, out, taps_out, gain_out, total, held, arrived):
    own = out.shape[0]
    slots, step = held.shape[:2]

    def copy(i):
        return pltpu.make_async_copy(got.at[pl.ds(i * step, step)], held.at[i], arrived.at[i])

    for i in range(slots):
        copy(i).start()
    total[...] = jnp.zeros_like(total)

    def add(i, _):
        copy(i).wait()
        for k in range(0, step, 4):
            total[...] += jnp.sum(held[i, k : k + 4].astype(F32), axis=0)
        return 0

    lax.fori_loop(0, slots, add, 0)
    tall = total.shape[0] // 2
    blocks = (tall - 4) // own
    for side in range(2):
        for k in range(blocks):
            at = (side * blocks + k) * LANES
            start = tall * side + own * k
            out[:, at : at + LANES] = total[start : start + own, :] * factor
    small = (total[tall - 4 : tall - 1, :] + total[2 * tall - 4 : 2 * tall - 1, :]) * factor
    taps = taps_out.shape[1]
    spot = lax.broadcasted_iota(jnp.int32, (1, LANES), 1)
    gains = jnp.zeros((1, LANES), F32)
    for r in range(3):
        for m in range(4):
            c = 4 * r + m
            turned = pltpu.roll(small[r : r + 1, :], (LANES - 32 * m) % LANES, 1)
            taps_out[c : c + 1, :] = turned[:, :taps]
            gains = jnp.where(spot == c, pltpu.roll(turned, (c - taps) % LANES, 1), gains)
    gain_out[...] = gains[:, :own]


def local(hidden, cotangent, lengths, kernel, conv_gain, w_out):
    groups, frames, double = hidden.shape
    width = double // 2
    half = width // 2
    blocks = width // LANES
    taps = kernel.shape[1]
    seq_count = lax.axis_size("seq")
    devices = lax.axis_size("dp") * seq_count
    own = width // devices
    rows = groups * frames
    span = frames + 2 * HALF_PAD
    length = frames + 2 * PAD
    tall = own * half // LANES + 4
    ends = seq_count - 1
    swap = [(i, i ^ 1) for i in range(seq_count)]
    place = lax.axis_index("seq")
    conv_flops = 2 * taps * rows * width

    spot = place.reshape(1)
    flat = cotangent.reshape(rows, width)
    inner_edge, outer_edge, weights = call(
        edges_kernel,
        [SMEM, HBM, HBM, HBM],
        [shape((groups, PAD + HALF_PAD, width), BF16)] * 2 + [shape((taps, width), F32)],
        [
            pltpu.VMEM((2, groups, PAD, double), BF16),
            pltpu.VMEM((2, groups, HALF_PAD, width), BF16),
            pltpu.SemaphoreType.DMA((2, 2, groups)),
            pltpu.SemaphoreType.DMA,
        ],
        1 << 20,
        4,
    )(spot, far_memory(hidden), far_memory(cotangent), far_memory(kernel.T))
    bridge = [(i, i + 1) for i in range(1, ends, 2)]
    across = lax.ppermute(outer_edge, "seq", bridge + [(j, i) for i, j in bridge])
    inside = lax.ppermute(inner_edge, "seq", swap)
    gain = conv_gain.reshape(1, width)
    slab_shape = shape((groups, blocks, length, LANES), F32)
    wide_shape = shape((rows, width), F32)
    gated, inner, swish = call(
        gate_kernel,
        [SMEM, SMEM] + [VMEM] * 3 + [HBM],
        [slab_shape, wide_shape, wide_shape],
        [
            pltpu.VMEM((width, width), BF16),
            pltpu.SemaphoreType.DMA((blocks // 2,)),
            pltpu.VMEM((groups, 3, 104, LANES), F32),
            pltpu.VMEM((groups, 88, LANES), F32),
            pltpu.VMEM((groups, 160, LANES), F32),
        ],
        conv_flops,
        10,
    )(lengths, spot, hidden, weights, flat, far_memory(w_out))
    slab, hat, inverse, message = call(
        forward_kernel,
        [SMEM, SMEM] + [VMEM] * 7,
        [
            slab_shape,
            wide_shape,
            shape((rows, LANES), F32),
            shape((width + half, rows), BF16),
        ],
        [pltpu.VMEM((rows, LANES), F32)],
        conv_flops,
        4,
        {2: 0, 3: 1},
    )(lengths, spot, gated, inner, inside, across, weights, gain, flat)
    far = lax.ppermute(message, "seq", swap)
    grad, term_conv = call(
        backward_kernel,
        [SMEM, SMEM] + [VMEM] * 4,
        [shape((groups, blocks, span, LANES), F32), shape((1, width), F32)],
        [pltpu.VMEM((rows, width), F32), pltpu.VMEM((8, width), F32)],
        20 * rows * width,
        6,
    )(lengths, spot, swish, hat, inverse, gain)
    packed = call(
        terms_kernel,
        [VMEM] * 3,
        shape((devices // 2, 8, LANES), F32),
        [
            pltpu.VMEM((blocks, 32, LANES), F32),
            pltpu.VMEM((blocks // 4, LANES, LANES), F32),
            pltpu.VMEM((width // 4 + 16, LANES), F32),
            pltpu.VMEM((3, groups, frames // 2, LANES), F32),
            pltpu.VMEM((3, groups, frames // 2 + 16, LANES), F32),
            pltpu.VMEM((3, 128, LANES), F32),
        ],
        conv_flops,
        6,
    )(grad, slab, term_conv)
    pairs = 32
    steps = devices // (2 * pairs)
    pieces = call(
        product_kernel,
        [SMEM] + [VMEM] * 4,
        pltpu.HBM((devices // 2, 2 * tall, LANES), BF16),
        [
            pltpu.VMEM((pairs, 2 * tall, LANES), F32),
            pltpu.VMEM((steps, pairs, 2 * tall, LANES), BF16),
            pltpu.SemaphoreType.DMA((steps,)),
        ],
        4 * rows * width * half,
        10,
        out_specs=HBM,
    )(spot, message, flat, far, packed)
    blocked = pieces.reshape(devices, tall // 4, 4, LANES)
    got = lax.all_to_all(blocked, AXES, 0, 0, tiled=True)
    full = call(
        fringe_kernel,
        [SMEM, SMEM] + [VMEM] * 7,
        shape((groups, blocks, span, LANES), F32),
        [
            pltpu.VMEM((2 * groups * HALF_PAD, width), BF16),
            pltpu.VMEM((2 * groups * HALF_PAD, width), F32),
            pltpu.VMEM((2 * groups * HALF_PAD, width), F32),
        ],
        conv_flops // 6,
        6,
        {2: 0},
    )(lengths, spot, grad, slab, inside, across, weights, gain, w_out)
    grad_hidden = call(
        input_kernel,
        [SMEM, SMEM] + [VMEM] * 3,
        shape((groups, frames, double), BF16),
        [],
        conv_flops,
        4,
    )(lengths, spot, full, hidden, weights)

    factor = 1.0 / math.sqrt(groups * lax.axis_size("dp") * frames * seq_count)
    slots = 4
    grad_w, grad_kernel, grad_gain = call(
        functools.partial(sum_kernel, factor),
        [HBM],
        [shape((own, width), F32), shape((own, taps), F32), shape((1, own), F32)],
        [
            pltpu.VMEM((2 * tall, LANES), F32),
            pltpu.VMEM((slots, devices // 2 // slots, 2 * tall, LANES), BF16),
            pltpu.SemaphoreType.DMA((slots,)),
        ],
        1 << 20,
        6,
    )(far_memory(got.reshape(devices // 2, 2 * tall, LANES)))
    return grad_hidden, grad_w, grad_kernel, grad_gain.reshape(own)


def solution(mesh):
    in_specs = (P("dp", "seq", None), P("dp", "seq", None), P("dp"), P(), P(), P())
    out_specs = (P("dp", "seq", None), P(AXES, None), P(AXES, None), P(AXES))
    return jax.shard_map(local, mesh=mesh, in_specs=in_specs, out_specs=out_specs, check_vma=False)
```

```python
import functools
import math

import jax
import jax.numpy as jnp
from jax import lax
from jax.experimental import pallas as pl
from jax.experimental.pallas import tpu as pltpu
from jax.sharding import PartitionSpec as P

EPSILON = 1e-05
AXES = ("dp", "seq")
LANES = 128
HALF_PAD = 16
PAD = 32
TILE = 16
F32, BF16 = jnp.float32, jnp.bfloat16
VMEM = pl.BlockSpec(memory_space=pltpu.VMEM)
SMEM = pl.BlockSpec(memory_space=pltpu.SMEM)
HBM = pl.BlockSpec(memory_space=pltpu.HBM)


def sigmoid(x):
    return 0.5 * jnp.tanh(0.5 * x) + 0.5


def left_of(lengths, place, u, frames):
    return lengths[u] - place[0] * frames


def lane(block):
    return pl.ds(pl.multiple_of(block * LANES, LANES), LANES)


def call(kernel, in_specs, out_shape, scratch, flops, limit, aliases=None, out_specs=None):
    return pl.pallas_call(
        kernel,
        in_specs=in_specs,
        out_specs=out_specs or jax.tree.map(lambda _: VMEM, out_shape),
        out_shape=out_shape,
        scratch_shapes=scratch,
        input_output_aliases=aliases or {},
        cost_estimate=pl.CostEstimate(flops=flops, bytes_accessed=8 << 20, transcendentals=0),
        compiler_params=pltpu.CompilerParams(vmem_limit_bytes=limit << 20),
    )


def shape(dims, dtype):
    return jax.ShapeDtypeStruct(dims, dtype)


def far_memory(array):
    return pltpu.with_memory_space_constraint(array, pltpu.HBM)


def depthwise(slab, weight, start, rows, order):
    total = None
    for j, row in enumerate(order):
        term = slab[pl.ds(start + 1 + j, rows), :] * weight[row]
        total = term if total is None else total + term
    return total


def edges_kernel(
    place, hidden, cotangent, source, inside, across, weights, cells, upstream, arrived, loaded
):
    groups, frames, double = hidden.shape
    width = double // 2
    core = place[0] & 1
    copies = []
    for side, last in enumerate((core, 1 - core)):
        start = pl.multiple_of(last * (frames - PAD), TILE)
        near = pl.multiple_of(last * (frames - HALF_PAD), TILE)
        for u in range(groups):
            copies.append(
                (
                    pltpu.make_async_copy(
                        hidden.at[u, pl.ds(start, PAD)], cells.at[side, u], arrived.at[0, side, u]
                    ),
                    pltpu.make_async_copy(
                        cotangent.at[u, pl.ds(near, HALF_PAD)],
                        upstream.at[side, u],
                        arrived.at[1, side, u],
                    ),
                )
            )
    for first, second in copies:
        first.start()
        second.start()
    taps = pltpu.make_async_copy(source, weights, loaded)
    taps.start()
    n = 0
    for side, out in enumerate((across, inside)):
        for u in range(groups):
            copies[n][0].wait()
            for cb in range(width // LANES):
                here = slice(cb * LANES, (cb + 1) * LANES)
                there = slice(width + cb * LANES, width + (cb + 1) * LANES)
                linear = cells[side, u, :, here].astype(F32)
                gate = sigmoid(cells[side, u, :, there].astype(F32))
                out[u, 0:PAD, here] = (linear * gate).astype(BF16)
            copies[n][1].wait()
            out[u, PAD:, :] = upstream[side, u]
            n += 1
    taps.wait()


CONTRACT_COLUMNS = (((1,), (1,)), ((), ()))


def inner_rows(block, weights, cb, cells, evens, mixed, some, taps):
    reach = cells.shape[1]
    here = block[pl.ds(PAD + 1, reach, stride=2), :]
    there = block[pl.ds(PAD + 2, reach, stride=2), :]
    after = block[pl.ds(PAD + 3, reach, stride=2), :]
    cells[0], cells[1], cells[2] = here, there, there + after
    weight = [weights[j : j + 1, lane(cb)] for j in range(taps)]
    paired = [weight[j] + weight[j + 1] for j in range(0, taps - 1, 2)] + [weight[taps - 1]]

    def run(kind, rows, chosen):
        total = None
        for i, factor in enumerate(chosen):
            part = cells[kind, pl.ds(i, rows), :] * factor
            total = part if total is None else total + part
        return total

    evens[...] = run(0, some + 8, weight[0::2])
    odd = run(1, some, weight[1::2])
    mixed[pl.ds(0, some, stride=2), :] = evens[0:some, :] + odd
    both = run(2, some, paired)
    mixed[pl.ds(1, some, stride=2), :] = both - evens[1 : some + 1, :] - odd


def gate_kernel(
    lengths, place, hidden, weights, cotangent, source, slab, hat, grad, w_out, arrived, cells, evens, mixed
):
    groups, frames, double = hidden.shape
    taps = weights.shape[0]
    width = double // 2
    blocks = width // LANES
    some = frames // 2 - HALF_PAD

    def copy(n):
        at = pl.ds(pl.multiple_of(n * 2 * LANES, 2 * LANES), 2 * LANES)
        return pltpu.make_async_copy(source.at[at], w_out.at[at], arrived.at[n])

    for n in range(blocks // 2):
        copy(n).start()

    def pair(n, _):
        at = pl.ds(pl.multiple_of(n * 2 * LANES, 2 * LANES), 2 * LANES)
        copy(n).wait()
        swish = lax.dot_general(
            cotangent[...], w_out[at, :], CONTRACT_COLUMNS, preferred_element_type=F32
        )
        for u in range(groups):
            limit = left_of(lengths, place, u, frames)
            base = u * frames
            for cb in (2 * n, 2 * n + 1):
                row = lax.broadcasted_iota(jnp.int32, (frames, LANES), 0)
                linear = hidden[u, :, lane(cb)].astype(F32)
                gate = sigmoid(hidden[u, :, lane(blocks + cb)].astype(F32))
                glu = jnp.where(row < limit, linear * gate, 0.0)
                block = slab.at[u, cb]
                block[PAD : PAD + frames, :] = glu.astype(BF16).astype(F32)
                inner_rows(
                    block, weights, cb, cells.at[u], evens.at[u], mixed.at[u], some, taps
                )
                to = slice(base + HALF_PAD, base + frames - HALF_PAD)
                hat[to, lane(cb)] = mixed[u]
        grad[:, at] = swish
        return 0

    lax.fori_loop(0, blocks // 2, pair, 0)


def row_mean(values, width):
    mean = jnp.sum(values, axis=-1, keepdims=True) * (1.0 / width)
    return jnp.broadcast_to(mean, values.shape)


def sides(place, inside, across, u, rows, lanes):
    first = (place[0] & 1) == 0
    one, two = inside[u, rows, lanes].astype(F32), across[u, rows, lanes].astype(F32)
    return jnp.where(first, two, one), jnp.where(first, one, two)


def forward_kernel(
    lengths,
    place,
    gated,
    inner,
    inside,
    across,
    weights,
    gain,
    cotangent,
    slab,
    hat,
    inverse,
    message,
    mean,
):
    groups, blocks, length = slab.shape[:3]
    taps = weights.shape[0]
    width = blocks * LANES
    half = width // 2
    frames = length - 2 * PAD
    rows = groups * frames
    for side in range(half // rows):
        theirs = (1 - (place[0] & 1)) * half + side * rows
        part = cotangent[:, pl.ds(pl.multiple_of(theirs, LANES), rows)]
        message[width + side * rows : width + (side + 1) * rows, :] = part

    def pair(n, _):
        row = lax.broadcasted_iota(jnp.int32, (PAD, LANES), 0)
        for cb in (2 * n, 2 * n + 1):
            weight = [weights[j : j + 1, lane(cb)] for j in range(taps)]
            for u in range(groups):
                limit = left_of(lengths, place, u, frames)
                base = u * frames
                block = slab.at[u, cb]
                before, after = sides(place, inside, across, u, slice(0, PAD), lane(cb))
                block[0:PAD, :] = jnp.where(row - PAD < limit, before, 0.0)
                block[PAD + frames :, :] = jnp.where(row + frames < limit, after, 0.0)
                for start in (0, frames - HALF_PAD):
                    to = slice(base + start, base + start + HALF_PAD)
                    hat[to, lane(cb)] = depthwise(
                        block, weight, HALF_PAD + start, HALF_PAD, range(taps)
                    )
        return 0

    lax.fori_loop(0, blocks // 2, pair, 0)
    for u in range(groups):
        rows = slice(u * frames, (u + 1) * frames)
        total = hat[rows, 0:LANES]
        for cb in range(1, blocks):
            total = total + hat[rows, cb * LANES : (cb + 1) * LANES]
        mean[rows, :] = row_mean(total, width)
        total = None
        for cb in range(blocks):
            centered = hat[rows, cb * LANES : (cb + 1) * LANES] - mean[rows, :]
            total = centered * centered if total is None else total + centered * centered
        inverse[rows, :] = lax.rsqrt(row_mean(total, width) + EPSILON)

    def normalize(cb, _):
        outs = []
        for u in range(groups):
            limit = left_of(lengths, place, u, frames)
            rows = slice(u * frames, (u + 1) * frames)
            normed = (hat[rows, lane(cb)] - mean[rows, :]) * inverse[rows, :]
            hat[rows, lane(cb)] = normed
            pre = normed * (0.5 * gain[:, lane(cb)])
            out = pre * jnp.tanh(pre) + pre
            row = lax.broadcasted_iota(jnp.int32, (frames, LANES), 0)
            outs.append(jnp.where(row < limit, out, 0.0).astype(BF16))
        message[lane(cb), :] = jnp.concatenate(outs, axis=0).T
        return 0

    lax.fori_loop(0, blocks, normalize, 0)


def fringe_kernel(
    lengths, place, grad, slab, inside, across, weights, gain, w_out, out, held, swish, hat
):
    groups, blocks, span = out.shape[:3]
    taps = weights.shape[0]
    width = blocks * LANES
    frames = span - 2 * HALF_PAD
    for u in range(groups):
        pieces = sides(place, inside, across, u, slice(PAD, PAD + HALF_PAD), slice(0, width))
        for n, piece in enumerate(pieces):
            at = (2 * u + n) * HALF_PAD
            held[at : at + HALF_PAD, :] = piece.astype(BF16)

    def pair(n, _):
        at = pl.ds(pl.multiple_of(n * 2 * LANES, 2 * LANES), 2 * LANES)
        swish[:, at] = lax.dot_general(
            held[...], w_out[at, :], CONTRACT_COLUMNS, preferred_element_type=F32
        )
        for cb in (2 * n, 2 * n + 1):
            weight = [weights[j : j + 1, lane(cb)] for j in range(taps)]
            for u in range(groups):
                for side, start in enumerate((0, span - HALF_PAD)):
                    to = (2 * u + side) * HALF_PAD
                    hat[to : to + HALF_PAD, lane(cb)] = depthwise(
                        slab.at[u, cb], weight, start, HALF_PAD, range(taps)
                    )
        return 0

    lax.fori_loop(0, blocks // 2, pair, 0)
    for u in range(groups):
        limit = left_of(lengths, place, u, frames)
        for side, start in enumerate((0, span - HALF_PAD)):
            at = slice((2 * u + side) * HALF_PAD, (2 * u + side + 1) * HALF_PAD)
            values = hat[at, :]
            centered = values - jnp.sum(values, axis=-1, keepdims=True) * (1.0 / width)
            spread = jnp.sum(centered * centered, axis=-1, keepdims=True) * (1.0 / width)
            inv = lax.rsqrt(spread + EPSILON)
            normed = centered * inv
            halved = normed * (0.5 * gain[...])
            turn = jnp.tanh(halved)
            gate = 0.5 * turn + 0.5
            row = start - HALF_PAD + lax.broadcasted_iota(jnp.int32, (HALF_PAD, width), 0)
            upstream = jnp.where(row < limit, swish[at, :], 0.0)
            scaled = upstream * (gate * (1.0 + halved * (1.0 - turn))) * gain[...]
            mean = jnp.sum(scaled, axis=-1, keepdims=True) * (1.0 / width)
            slope = jnp.sum(scaled * normed, axis=-1, keepdims=True) * (1.0 / width)
            result = (inv * (scaled - mean - normed * slope)).astype(BF16).astype(F32)
            for cb in range(blocks):
                out[u, cb, start : start + HALF_PAD, :] = result[:, cb * LANES : (cb + 1) * LANES]


def product_kernel(place, near, cotangent, far, packed, out, scratch, held, sent):
    rows, width = cotangent.shape
    half = width // 2
    pairs = scratch.shape[0]
    step = 24 * pairs
    wide = 2 * LANES
    first = lax.broadcasted_iota(jnp.int32, (pairs, 8, LANES), 1) < 4
    pick = lambda a, b: jnp.where(first, a, b)
    roll = lambda a: pltpu.roll(a, 4, 1)
    mine = pl.ds(pl.multiple_of((place[0] & 1) * half, LANES), half)

    part = pairs // 4

    def copy(s, n):
        at = pl.ds(s * pairs + n * part, part)
        return pltpu.make_async_copy(held.at[s, pl.ds(n * part, part)], out.at[at], sent.at[s, n])

    def chunk(s, _):
        at = pl.ds(pl.multiple_of(s * step, step), step)
        theirs = [far[width + n * rows : width + (n + 1) * rows, :] for n in range(half // rows)]
        left = jnp.concatenate([near[at, :], far[at, :]], axis=1)
        right = jnp.concatenate([cotangent[:, mine], jnp.concatenate(theirs, axis=1)], axis=0)
        small = packed[pl.ds(s * pairs, pairs)]
        before = small
        split = 12 * half // LANES
        for q in range(half // wide):
            result = jnp.dot(
                left, right[:, q * wide : (q + 1) * wide], preferred_element_type=F32
            )

            def parts(k):
                cut = result[:, k * LANES : (k + 1) * LANES].reshape(pairs, 3, 8, LANES)
                return cut[:, 0], cut[:, 1], cut[:, 2]

            a, b, c = parts(0)
            d, e, f = parts(1)
            rd, re, rf = roll(d), roll(e), roll(f)
            for i, tile in enumerate((a, pick(b, rd), pick(rd, re))):
                scratch[:, 24 * q + 8 * i : 24 * q + 8 * i + 8, :] = tile
            for i, tile in enumerate((pick(before, b), c, pick(re, rf))):
                spot = split + 24 * q + 8 * i
                scratch[:, spot : spot + 8, :] = tile
            before = rf
        scratch[:, 2 * split : 2 * split + 8, :] = pick(before, small)
        for n in range(4):
            held[s, n * part : (n + 1) * part] = scratch[n * part : (n + 1) * part].astype(BF16)
            copy(s, n).start()
        return 0

    lax.fori_loop(0, width // step, chunk, 0)
    for s in range(width // step):
        for n in range(4):
            copy(s, n).wait()


def backward_kernel(lengths, place, grad, hat, inverse, gain, slab, term, work, sums):
    groups, blocks, span = slab.shape[:3]
    width = blocks * LANES
    frames = span - 2 * HALF_PAD
    sums[...] = jnp.zeros_like(sums)
    part = frames // 2

    def norm(n, _):
        u, start = n // 2, (n % 2) * part
        at = pl.ds(pl.multiple_of(n * part, TILE), part)
        limit = left_of(lengths, place, u, frames)
        row = start + lax.broadcasted_iota(jnp.int32, (part, LANES), 0)
        keep = row < limit
        first = second = None
        for cb in range(blocks):
            here = slice(cb * LANES, (cb + 1) * LANES)
            normed = hat[at, here]
            halved = normed * (0.5 * gain[:, here])
            turn = jnp.tanh(halved)
            gate = 0.5 * turn + 0.5
            grad_pre = jnp.where(keep, grad[at, here], 0.0) * (gate * (1.0 + halved * (1.0 - turn)))
            term_part = grad_pre * normed
            sums[:, here] += jnp.sum(term_part.reshape(part // 8, 8, LANES), axis=0)
            scaled = grad_pre * gain[:, here]
            work[at, here] = scaled
            first = scaled if first is None else first + scaled
            second = scaled * normed if second is None else second + scaled * normed
        mean = row_mean(first, width)
        slope = row_mean(second, width)
        inv = inverse[at, :]
        for cb in range(blocks):
            here = slice(cb * LANES, (cb + 1) * LANES)
            result = inv * (work[at, here] - mean - hat[at, here] * slope)
            to = pl.ds(pl.multiple_of(HALF_PAD + start, TILE), part)
            slab[u, cb, to, :] = result.astype(BF16).astype(F32)
        return 0

    lax.fori_loop(0, 2 * groups, norm, 0)
    term[...] = jnp.sum(sums[...], axis=0, keepdims=True)


def terms_kernel(
    grad, slab, term, packed, square, columns, rest, values, cells, taken
):
    groups, blocks, span = grad.shape[:3]
    frames = span - 2 * HALF_PAD
    taps = 31
    some = frames // 2
    reach = cells.shape[2]
    start = PAD - taps // 2
    taken[...] = jnp.zeros_like(taken)

    def channel(cb, _):
        for u in range(groups):
            even = grad[u, cb, pl.ds(HALF_PAD, some, stride=2), :]
            odd = grad[u, cb, pl.ds(HALF_PAD + 1, some, stride=2), :]
            values[0, u], values[1, u], values[2, u] = even, odd, even + odd
            here = slab[u, cb, pl.ds(start, reach, stride=2), :]
            there = slab[u, cb, pl.ds(start + 1, reach, stride=2), :]
            after = slab[u, cb, pl.ds(start + 2, reach, stride=2), :]
            cells[0, u], cells[1, u], cells[2, u] = here, there, there + after
        for kind, lags in enumerate((taps // 2 + 1, taps // 2 + 1, taps // 2)):
            for r in range(8):
                chosen = [i for i in range(r, lags, 8)]
                totals = [None] * len(chosen)
                for u in range(groups):
                    for m in range(0, some, 8):
                        value = values[kind, u, m : m + 8, :]
                        for n, i in enumerate(chosen):
                            part = value * cells[kind, u, pl.ds(m + i, 8), :]
                            totals[n] = part if totals[n] is None else totals[n] + part
                for n, i in enumerate(chosen):
                    taken[kind, 8 * i : 8 * i + 8, :] = totals[n]
        sums = []
        for kind in range(3):
            line = taken[kind, pl.ds(0, 16, stride=8), :]
            for k in range(1, 8):
                line = line + taken[kind, pl.ds(k, 16, stride=8), :]
            sums.append(line)
        evens = sums[0] + sums[1]
        odds = sums[2] - pltpu.roll(sums[0], 15, 0) - sums[1]
        square[cb, pl.ds(0, 16, stride=2), :] = evens
        square[cb, pl.ds(1, 16, stride=2), :] = odds
        square[cb, taps : taps + 1, :] = term[:, lane(cb)]
        return 0

    lax.fori_loop(0, blocks, channel, 0)
    quarter = blocks * LANES // 4
    spot = lax.broadcasted_iota(jnp.int32, (32, LANES), 1) // 32
    lines = []
    for g in range(blocks // 4):
        columns[g] = square[4 * g : 4 * g + 4].reshape(LANES, LANES).T
        for b in range(4):
            line = jnp.zeros((32, LANES), F32)
            for m in range(4):
                taken_rows = columns[g, pl.ds(m, 32, stride=4), :]
                line = jnp.where(spot == m, pltpu.roll(taken_rows, 32 * ((m - b) % 4), 1), line)
            lines.append(line)
    total = jnp.concatenate(lines, axis=0)
    rest[8 : 8 + quarter, :] = total
    row = lax.broadcasted_iota(jnp.int32, (8, LANES), 0)
    for p in range(packed.shape[0]):
        upper = rest[6 * p + 8 : 6 * p + 16, :]
        lower = rest[6 * p + 7 : 6 * p + 15, :]
        packed[p] = jnp.where(row < 3, upper, jnp.where((row > 3) & (row < 7), lower, 0.0))


def gradient_kernel(lengths, place, swish, hat, inverse, gain, slab, grad, packed, term, *scratch):
    work, sums, *rest = scratch
    backward_kernel(lengths, place, swish, hat, inverse, gain, grad, term, work, sums)
    terms_kernel(grad, slab, term, packed, *rest)


def input_kernel(lengths, place, grad, hidden, weights, out):
    groups, frames, _ = hidden.shape
    blocks = grad.shape[1]
    taps = weights.shape[0]
    chunk = 64
    for u in range(groups):
        limit = left_of(lengths, place, u, frames)

        def channel(cb, _):
            block = grad.at[u, cb]
            weight = [weights[j : j + 1, lane(cb)] for j in range(taps)]
            for start in range(0, frames, chunk):
                at = slice(start, start + chunk)
                total = depthwise(block, weight, start, chunk, range(taps - 1, -1, -1))
                row = start + lax.broadcasted_iota(jnp.int32, (chunk, LANES), 0)
                total = jnp.where(row < limit, total, 0.0)
                linear = hidden[u, at, lane(cb)].astype(F32)
                gate = sigmoid(hidden[u, at, lane(blocks + cb)].astype(F32))
                opened = total * gate
                out[u, at, lane(cb)] = opened.astype(BF16)
                out[u, at, lane(blocks + cb)] = (opened * linear * (1.0 - gate)).astype(BF16)
            return 0

        lax.fori_loop(0, blocks, channel, 0)


def sum_kernel(factor, got, out, taps_out, gain_out, total, held, arrived):
    own = out.shape[0]
    slots, step = held.shape[:2]

    def copy(i):
        return pltpu.make_async_copy(got.at[pl.ds(i * step, step)], held.at[i], arrived.at[i])

    for i in range(slots):
        copy(i).start()
    total[...] = jnp.zeros_like(total)

    def add(i, _):
        copy(i).wait()
        for k in range(0, step, 4):
            total[...] += jnp.sum(held[i, k : k + 4].astype(F32), axis=0)
        return 0

    lax.fori_loop(0, slots, add, 0)
    tall = total.shape[0] // 2
    blocks = (tall - 4) // own
    for side in range(2):
        for k in range(blocks):
            at = (side * blocks + k) * LANES
            start = tall * side + own * k
            out[:, at : at + LANES] = total[start : start + own, :] * factor
    small = (total[tall - 4 : tall - 1, :] + total[2 * tall - 4 : 2 * tall - 1, :]) * factor
    taps = taps_out.shape[1]
    spot = lax.broadcasted_iota(jnp.int32, (1, LANES), 1)
    gains = jnp.zeros((1, LANES), F32)
    for r in range(3):
        for m in range(4):
            c = 4 * r + m
            turned = pltpu.roll(small[r : r + 1, :], (LANES - 32 * m) % LANES, 1)
            taps_out[c : c + 1, :] = turned[:, :taps]
            gains = jnp.where(spot == c, pltpu.roll(turned, (c - taps) % LANES, 1), gains)
    gain_out[...] = gains[:, :own]


def local(hidden, cotangent, lengths, kernel, conv_gain, w_out):
    groups, frames, double = hidden.shape
    width = double // 2
    half = width // 2
    blocks = width // LANES
    taps = kernel.shape[1]
    seq_count = lax.axis_size("seq")
    devices = lax.axis_size("dp") * seq_count
    own = width // devices
    rows = groups * frames
    span = frames + 2 * HALF_PAD
    length = frames + 2 * PAD
    tall = own * half // LANES + 4
    ends = seq_count - 1
    swap = [(i, i ^ 1) for i in range(seq_count)]
    place = lax.axis_index("seq")
    conv_flops = 2 * taps * rows * width

    spot = place.reshape(1)
    flat = cotangent.reshape(rows, width)
    inner_edge, outer_edge, weights = call(
        edges_kernel,
        [SMEM, HBM, HBM, HBM],
        [shape((groups, PAD + HALF_PAD, width), BF16)] * 2 + [shape((taps, width), F32)],
        [
            pltpu.VMEM((2, groups, PAD, double), BF16),
            pltpu.VMEM((2, groups, HALF_PAD, width), BF16),
            pltpu.SemaphoreType.DMA((2, 2, groups)),
            pltpu.SemaphoreType.DMA,
        ],
        1 << 20,
        4,
    )(spot, far_memory(hidden), far_memory(cotangent), far_memory(kernel.T))
    bridge = [(i, i + 1) for i in range(1, ends, 2)]
    across = lax.ppermute(outer_edge, "seq", bridge + [(j, i) for i, j in bridge])
    inside = lax.ppermute(inner_edge, "seq", swap)
    gain = conv_gain.reshape(1, width)
    slab_shape = shape((groups, blocks, length, LANES), F32)
    wide_shape = shape((rows, width), F32)
    gated, inner, swish = call(
        gate_kernel,
        [SMEM, SMEM] + [VMEM] * 3 + [HBM],
        [slab_shape, wide_shape, wide_shape],
        [
            pltpu.VMEM((width, width), BF16),
            pltpu.SemaphoreType.DMA((blocks // 2,)),
            pltpu.VMEM((groups, 3, 104, LANES), F32),
            pltpu.VMEM((groups, 88, LANES), F32),
            pltpu.VMEM((groups, 160, LANES), F32),
        ],
        conv_flops,
        10,
    )(lengths, spot, hidden, weights, flat, far_memory(w_out))
    slab, hat, inverse, message = call(
        forward_kernel,
        [SMEM, SMEM] + [VMEM] * 7,
        [
            slab_shape,
            wide_shape,
            shape((rows, LANES), F32),
            shape((width + half, rows), BF16),
        ],
        [pltpu.VMEM((rows, LANES), F32)],
        conv_flops,
        4,
        {2: 0, 3: 1},
    )(lengths, spot, gated, inner, inside, across, weights, gain, flat)
    far = lax.ppermute(message, "seq", swap)
    grad, packed = call(
        gradient_kernel,
        [SMEM, SMEM] + [VMEM] * 5,
        [
            shape((groups, blocks, span, LANES), F32),
            shape((devices // 2, 8, LANES), F32),
        ],
        [
            pltpu.VMEM((1, width), F32),
            pltpu.VMEM((rows, width), F32),
            pltpu.VMEM((8, width), F32),
            pltpu.VMEM((blocks, 32, LANES), F32),
            pltpu.VMEM((blocks // 4, LANES, LANES), F32),
            pltpu.VMEM((width // 4 + 16, LANES), F32),
            pltpu.VMEM((3, groups, frames // 2, LANES), F32),
            pltpu.VMEM((3, groups, frames // 2 + 16, LANES), F32),
            pltpu.VMEM((3, 128, LANES), F32),
        ],
        conv_flops,
        10,
    )(lengths, spot, swish, hat, inverse, gain, slab)
    pairs = 32
    steps = devices // (2 * pairs)
    pieces = call(
        product_kernel,
        [SMEM] + [VMEM] * 4,
        pltpu.HBM((devices // 2, 2 * tall, LANES), BF16),
        [
            pltpu.VMEM((pairs, 2 * tall, LANES), F32),
            pltpu.VMEM((steps, pairs, 2 * tall, LANES), BF16),
            pltpu.SemaphoreType.DMA((steps, 4)),
        ],
        4 * rows * width * half,
        10,
        out_specs=HBM,
    )(spot, message, flat, far, packed)
    blocked = pieces.reshape(devices, tall // 4, 4, LANES)
    got = lax.all_to_all(blocked, AXES, 0, 0, tiled=True)
    full = call(
        fringe_kernel,
        [SMEM, SMEM] + [VMEM] * 7,
        shape((groups, blocks, span, LANES), F32),
        [
            pltpu.VMEM((2 * groups * HALF_PAD, width), BF16),
            pltpu.VMEM((2 * groups * HALF_PAD, width), F32),
            pltpu.VMEM((2 * groups * HALF_PAD, width), F32),
        ],
        conv_flops // 6,
        6,
        {2: 0},
    )(lengths, spot, grad, slab, inside, across, weights, gain, w_out)
    grad_hidden = call(
        input_kernel,
        [SMEM, SMEM] + [VMEM] * 3,
        shape((groups, frames, double), BF16),
        [],
        conv_flops,
        4,
    )(lengths, spot, full, hidden, weights)

    factor = 1.0 / math.sqrt(groups * lax.axis_size("dp") * frames * seq_count)
    slots = 8
    grad_w, grad_kernel, grad_gain = call(
        functools.partial(sum_kernel, factor),
        [HBM],
        [shape((own, width), F32), shape((own, taps), F32), shape((1, own), F32)],
        [
            pltpu.VMEM((2 * tall, LANES), F32),
            pltpu.VMEM((slots, devices // 2 // slots, 2 * tall, LANES), BF16),
            pltpu.SemaphoreType.DMA((slots,)),
        ],
        1 << 20,
        6,
    )(far_memory(got.reshape(devices // 2, 2 * tall, LANES)))
    return grad_hidden, grad_w, grad_kernel, grad_gain.reshape(own)


def solution(mesh):
    in_specs = (P("dp", "seq", None), P("dp", "seq", None), P("dp"), P(), P(), P())
    out_specs = (P("dp", "seq", None), P(AXES, None), P(AXES, None), P(AXES))
    return jax.shard_map(local, mesh=mesh, in_specs=in_specs, out_specs=out_specs, check_vma=False)
```

```python
import functools
import math

import jax
import jax.numpy as jnp
from jax import lax
from jax.experimental import pallas as pl
from jax.experimental.pallas import tpu as pltpu
from jax.sharding import PartitionSpec as P

EPSILON = 1e-05
AXES = ("dp", "seq")
LANES = 128
HALF_PAD = 16
PAD = 32
TILE = 16
F32, BF16 = jnp.float32, jnp.bfloat16
VMEM = pl.BlockSpec(memory_space=pltpu.VMEM)
SMEM = pl.BlockSpec(memory_space=pltpu.SMEM)
HBM = pl.BlockSpec(memory_space=pltpu.HBM)


def sigmoid(x):
    return 0.5 * jnp.tanh(0.5 * x) + 0.5


def left_of(lengths, place, u, frames):
    return lengths[u] - place[0] * frames


def lane(block):
    return pl.ds(pl.multiple_of(block * LANES, LANES), LANES)


def call(kernel, in_specs, out_shape, scratch, flops, limit, aliases=None, out_specs=None):
    return pl.pallas_call(
        kernel,
        in_specs=in_specs,
        out_specs=out_specs or jax.tree.map(lambda _: VMEM, out_shape),
        out_shape=out_shape,
        scratch_shapes=scratch,
        input_output_aliases=aliases or {},
        cost_estimate=pl.CostEstimate(flops=flops, bytes_accessed=8 << 20, transcendentals=0),
        compiler_params=pltpu.CompilerParams(vmem_limit_bytes=limit << 20),
    )


def shape(dims, dtype):
    return jax.ShapeDtypeStruct(dims, dtype)


def far_memory(array):
    return pltpu.with_memory_space_constraint(array, pltpu.HBM)


def depthwise(slab, weight, start, rows, order):
    total = None
    for j, row in enumerate(order):
        term = slab[pl.ds(start + 1 + j, rows), :] * weight[row]
        total = term if total is None else total + term
    return total


def edges_kernel(
    place, hidden, cotangent, source, inside, across, weights, cells, upstream, arrived, loaded
):
    groups, frames, double = hidden.shape
    width = double // 2
    core = place[0] & 1
    copies = []
    for side, last in enumerate((core, 1 - core)):
        start = pl.multiple_of(last * (frames - PAD), TILE)
        near = pl.multiple_of(last * (frames - HALF_PAD), TILE)
        for u in range(groups):
            copies.append(
                (
                    pltpu.make_async_copy(
                        hidden.at[u, pl.ds(start, PAD)], cells.at[side, u], arrived.at[0, side, u]
                    ),
                    pltpu.make_async_copy(
                        cotangent.at[u, pl.ds(near, HALF_PAD)],
                        upstream.at[side, u],
                        arrived.at[1, side, u],
                    ),
                )
            )
    for first, second in copies:
        first.start()
        second.start()
    taps = pltpu.make_async_copy(source, weights, loaded)
    taps.start()
    n = 0
    for side, out in enumerate((across, inside)):
        for u in range(groups):
            copies[n][0].wait()
            for cb in range(width // LANES):
                here = slice(cb * LANES, (cb + 1) * LANES)
                there = slice(width + cb * LANES, width + (cb + 1) * LANES)
                linear = cells[side, u, :, here].astype(F32)
                gate = sigmoid(cells[side, u, :, there].astype(F32))
                out[u, 0:PAD, here] = (linear * gate).astype(BF16)
            copies[n][1].wait()
            out[u, PAD:, :] = upstream[side, u]
            n += 1
    taps.wait()


CONTRACT_COLUMNS = (((1,), (1,)), ((), ()))


def inner_rows(block, weights, cb, cells, evens, mixed, some, taps):
    reach = cells.shape[1]
    here = block[pl.ds(PAD + 1, reach, stride=2), :]
    there = block[pl.ds(PAD + 2, reach, stride=2), :]
    after = block[pl.ds(PAD + 3, reach, stride=2), :]
    cells[0], cells[1], cells[2] = here, there, there + after
    weight = [weights[j : j + 1, lane(cb)] for j in range(taps)]
    paired = [weight[j] + weight[j + 1] for j in range(0, taps - 1, 2)] + [weight[taps - 1]]

    def run(kind, rows, chosen):
        total = None
        for i, factor in enumerate(chosen):
            part = cells[kind, pl.ds(i, rows), :] * factor
            total = part if total is None else total + part
        return total

    evens[...] = run(0, some + 8, weight[0::2])
    odd = run(1, some, weight[1::2])
    mixed[pl.ds(0, some, stride=2), :] = evens[0:some, :] + odd
    both = run(2, some, paired)
    mixed[pl.ds(1, some, stride=2), :] = both - evens[1 : some + 1, :] - odd


def gate_kernel(
    lengths, place, hidden, weights, cotangent, source, slab, hat, grad, w_out, arrived, cells, evens, mixed
):
    groups, frames, double = hidden.shape
    taps = weights.shape[0]
    width = double // 2
    blocks = width // LANES
    some = frames // 2 - HALF_PAD

    def copy(n):
        at = pl.ds(pl.multiple_of(n * 2 * LANES, 2 * LANES), 2 * LANES)
        return pltpu.make_async_copy(source.at[at], w_out.at[at], arrived.at[n])

    for n in range(blocks // 2):
        copy(n).start()

    def pair(n, _):
        at = pl.ds(pl.multiple_of(n * 2 * LANES, 2 * LANES), 2 * LANES)
        copy(n).wait()
        swish = lax.dot_general(
            cotangent[...], w_out[at, :], CONTRACT_COLUMNS, preferred_element_type=F32
        )
        for u in range(groups):
            limit = left_of(lengths, place, u, frames)
            base = u * frames
            for cb in (2 * n, 2 * n + 1):
                row = lax.broadcasted_iota(jnp.int32, (frames, LANES), 0)
                linear = hidden[u, :, lane(cb)].astype(F32)
                gate = sigmoid(hidden[u, :, lane(blocks + cb)].astype(F32))
                glu = jnp.where(row < limit, linear * gate, 0.0)
                block = slab.at[u, cb]
                block[PAD : PAD + frames, :] = glu.astype(BF16).astype(F32)
                inner_rows(
                    block, weights, cb, cells.at[u], evens.at[u], mixed.at[u], some, taps
                )
                to = slice(base + HALF_PAD, base + frames - HALF_PAD)
                hat[to, lane(cb)] = mixed[u]
        grad[:, at] = swish
        return 0

    lax.fori_loop(0, blocks // 2, pair, 0)


def row_mean(values, width):
    mean = jnp.sum(values, axis=-1, keepdims=True) * (1.0 / width)
    return jnp.broadcast_to(mean, values.shape)


def sides(place, inside, across, u, rows, lanes):
    first = (place[0] & 1) == 0
    one, two = inside[u, rows, lanes].astype(F32), across[u, rows, lanes].astype(F32)
    return jnp.where(first, two, one), jnp.where(first, one, two)


def forward_kernel(
    lengths,
    place,
    gated,
    inner,
    inside,
    across,
    weights,
    gain,
    cotangent,
    slab,
    hat,
    inverse,
    message,
    mean,
):
    groups, blocks, length = slab.shape[:3]
    taps = weights.shape[0]
    width = blocks * LANES
    half = width // 2
    frames = length - 2 * PAD
    rows = groups * frames
    for side in range(half // rows):
        theirs = (1 - (place[0] & 1)) * half + side * rows
        part = cotangent[:, pl.ds(pl.multiple_of(theirs, LANES), rows)]
        message[width + side * rows : width + (side + 1) * rows, :] = part

    def pair(n, _):
        row = lax.broadcasted_iota(jnp.int32, (PAD, LANES), 0)
        for cb in (2 * n, 2 * n + 1):
            weight = [weights[j : j + 1, lane(cb)] for j in range(taps)]
            for u in range(groups):
                limit = left_of(lengths, place, u, frames)
                base = u * frames
                block = slab.at[u, cb]
                before, after = sides(place, inside, across, u, slice(0, PAD), lane(cb))
                block[0:PAD, :] = jnp.where(row - PAD < limit, before, 0.0)
                block[PAD + frames :, :] = jnp.where(row + frames < limit, after, 0.0)
                for start in (0, frames - HALF_PAD):
                    to = slice(base + start, base + start + HALF_PAD)
                    hat[to, lane(cb)] = depthwise(
                        block, weight, HALF_PAD + start, HALF_PAD, range(taps)
                    )
        return 0

    lax.fori_loop(0, blocks // 2, pair, 0)
    for u in range(groups):
        rows = slice(u * frames, (u + 1) * frames)
        total = hat[rows, 0:LANES]
        for cb in range(1, blocks):
            total = total + hat[rows, cb * LANES : (cb + 1) * LANES]
        mean[rows, :] = row_mean(total, width)
        total = None
        for cb in range(blocks):
            centered = hat[rows, cb * LANES : (cb + 1) * LANES] - mean[rows, :]
            total = centered * centered if total is None else total + centered * centered
        inverse[rows, :] = lax.rsqrt(row_mean(total, width) + EPSILON)

    def normalize(cb, _):
        outs = []
        for u in range(groups):
            limit = left_of(lengths, place, u, frames)
            rows = slice(u * frames, (u + 1) * frames)
            normed = (hat[rows, lane(cb)] - mean[rows, :]) * inverse[rows, :]
            hat[rows, lane(cb)] = normed
            pre = normed * (0.5 * gain[:, lane(cb)])
            out = pre * jnp.tanh(pre) + pre
            row = lax.broadcasted_iota(jnp.int32, (frames, LANES), 0)
            outs.append(jnp.where(row < limit, out, 0.0).astype(BF16))
        message[lane(cb), :] = jnp.concatenate(outs, axis=0).T
        return 0

    lax.fori_loop(0, blocks, normalize, 0)


def fringe_kernel(
    lengths, place, grad, slab, inside, across, weights, gain, w_out, out, held, swish, hat
):
    groups, blocks, span = out.shape[:3]
    taps = weights.shape[0]
    width = blocks * LANES
    frames = span - 2 * HALF_PAD
    for u in range(groups):
        pieces = sides(place, inside, across, u, slice(PAD, PAD + HALF_PAD), slice(0, width))
        for n, piece in enumerate(pieces):
            at = (2 * u + n) * HALF_PAD
            held[at : at + HALF_PAD, :] = piece.astype(BF16)

    def pair(n, _):
        at = pl.ds(pl.multiple_of(n * 2 * LANES, 2 * LANES), 2 * LANES)
        swish[:, at] = lax.dot_general(
            held[...], w_out[at, :], CONTRACT_COLUMNS, preferred_element_type=F32
        )
        for cb in (2 * n, 2 * n + 1):
            weight = [weights[j : j + 1, lane(cb)] for j in range(taps)]
            for u in range(groups):
                for side, start in enumerate((0, span - HALF_PAD)):
                    to = (2 * u + side) * HALF_PAD
                    hat[to : to + HALF_PAD, lane(cb)] = depthwise(
                        slab.at[u, cb], weight, start, HALF_PAD, range(taps)
                    )
        return 0

    lax.fori_loop(0, blocks // 2, pair, 0)
    for u in range(groups):
        limit = left_of(lengths, place, u, frames)
        for side, start in enumerate((0, span - HALF_PAD)):
            at = slice((2 * u + side) * HALF_PAD, (2 * u + side + 1) * HALF_PAD)
            values = hat[at, :]
            centered = values - jnp.sum(values, axis=-1, keepdims=True) * (1.0 / width)
            spread = jnp.sum(centered * centered, axis=-1, keepdims=True) * (1.0 / width)
            inv = lax.rsqrt(spread + EPSILON)
            normed = centered * inv
            halved = normed * (0.5 * gain[...])
            turn = jnp.tanh(halved)
            gate = 0.5 * turn + 0.5
            row = start - HALF_PAD + lax.broadcasted_iota(jnp.int32, (HALF_PAD, width), 0)
            upstream = jnp.where(row < limit, swish[at, :], 0.0)
            scaled = upstream * (gate * (1.0 + halved * (1.0 - turn))) * gain[...]
            mean = jnp.sum(scaled, axis=-1, keepdims=True) * (1.0 / width)
            slope = jnp.sum(scaled * normed, axis=-1, keepdims=True) * (1.0 / width)
            result = (inv * (scaled - mean - normed * slope)).astype(BF16).astype(F32)
            for cb in range(blocks):
                out[u, cb, start : start + HALF_PAD, :] = result[:, cb * LANES : (cb + 1) * LANES]


def product_kernel(place, near, cotangent, far, packed, out, scratch, held, sent):
    rows, width = cotangent.shape
    half = width // 2
    pairs = scratch.shape[0]
    step = 24 * pairs
    wide = 2 * LANES
    first = lax.broadcasted_iota(jnp.int32, (pairs, 8, LANES), 1) < 4
    pick = lambda a, b: jnp.where(first, a, b)
    roll = lambda a: pltpu.roll(a, 4, 1)
    mine = pl.ds(pl.multiple_of((place[0] & 1) * half, LANES), half)

    part = pairs // 4

    def copy(s, n):
        at = pl.ds(s * pairs + n * part, part)
        return pltpu.make_async_copy(held.at[s, pl.ds(n * part, part)], out.at[at], sent.at[s, n])

    def chunk(s, _):
        at = pl.ds(pl.multiple_of(s * step, step), step)
        theirs = [far[width + n * rows : width + (n + 1) * rows, :] for n in range(half // rows)]
        left = jnp.concatenate([near[at, :], far[at, :]], axis=1)
        right = jnp.concatenate([cotangent[:, mine], jnp.concatenate(theirs, axis=1)], axis=0)
        small = packed[pl.ds(s * pairs, pairs)]
        before = small
        split = 12 * half // LANES
        for q in range(half // wide):
            result = jnp.dot(
                left, right[:, q * wide : (q + 1) * wide], preferred_element_type=F32
            )

            def parts(k):
                cut = result[:, k * LANES : (k + 1) * LANES].reshape(pairs, 3, 8, LANES)
                return cut[:, 0], cut[:, 1], cut[:, 2]

            a, b, c = parts(0)
            d, e, f = parts(1)
            rd, re, rf = roll(d), roll(e), roll(f)
            for i, tile in enumerate((a, pick(b, rd), pick(rd, re))):
                scratch[:, 24 * q + 8 * i : 24 * q + 8 * i + 8, :] = tile
            for i, tile in enumerate((pick(before, b), c, pick(re, rf))):
                spot = split + 24 * q + 8 * i
                scratch[:, spot : spot + 8, :] = tile
            before = rf
        scratch[:, 2 * split : 2 * split + 8, :] = pick(before, small)
        for n in range(4):
            held[s, n * part : (n + 1) * part] = scratch[n * part : (n + 1) * part].astype(BF16)
            copy(s, n).start()
        return 0

    lax.fori_loop(0, width // step, chunk, 0)
    for s in range(width // step):
        for n in range(4):
            copy(s, n).wait()


def backward_kernel(lengths, place, grad, hat, inverse, gain, slab, term, work, sums):
    groups, blocks, span = slab.shape[:3]
    width = blocks * LANES
    frames = span - 2 * HALF_PAD
    sums[...] = jnp.zeros_like(sums)
    part = frames // 4

    def norm(n, _):
        u, start = n // 4, (n % 4) * part
        at = pl.ds(pl.multiple_of(n * part, TILE), part)
        limit = left_of(lengths, place, u, frames)
        row = start + lax.broadcasted_iota(jnp.int32, (part, LANES), 0)
        keep = row < limit
        first = second = None
        for cb in range(blocks):
            here = slice(cb * LANES, (cb + 1) * LANES)
            normed = hat[at, here]
            halved = normed * (0.5 * gain[:, here])
            turn = jnp.tanh(halved)
            gate = 0.5 * turn + 0.5
            grad_pre = jnp.where(keep, grad[at, here], 0.0) * (gate * (1.0 + halved * (1.0 - turn)))
            term_part = grad_pre * normed
            sums[:, here] += jnp.sum(term_part.reshape(part // 8, 8, LANES), axis=0)
            scaled = grad_pre * gain[:, here]
            work[at, here] = scaled
            first = scaled if first is None else first + scaled
            second = scaled * normed if second is None else second + scaled * normed
        mean = row_mean(first, width)
        slope = row_mean(second, width)
        inv = inverse[at, :]
        for cb in range(blocks):
            here = slice(cb * LANES, (cb + 1) * LANES)
            result = inv * (work[at, here] - mean - hat[at, here] * slope)
            to = pl.ds(pl.multiple_of(HALF_PAD + start, TILE), part)
            slab[u, cb, to, :] = result.astype(BF16).astype(F32)
        return 0

    lax.fori_loop(0, 4 * groups, norm, 0)
    term[...] = jnp.sum(sums[...], axis=0, keepdims=True)


def terms_kernel(
    grad, slab, term, packed, square, columns, rest, values, cells, taken
):
    groups, blocks, span = grad.shape[:3]
    frames = span - 2 * HALF_PAD
    taps = 31
    some = frames // 2
    reach = cells.shape[2]
    start = PAD - taps // 2
    taken[...] = jnp.zeros_like(taken)

    def channel(cb, _):
        for u in range(groups):
            even = grad[u, cb, pl.ds(HALF_PAD, some, stride=2), :]
            odd = grad[u, cb, pl.ds(HALF_PAD + 1, some, stride=2), :]
            values[0, u], values[1, u], values[2, u] = even, odd, even + odd
            here = slab[u, cb, pl.ds(start, reach, stride=2), :]
            there = slab[u, cb, pl.ds(start + 1, reach, stride=2), :]
            after = slab[u, cb, pl.ds(start + 2, reach, stride=2), :]
            cells[0, u], cells[1, u], cells[2, u] = here, there, there + after
        for kind, lags in enumerate((taps // 2 + 1, taps // 2 + 1, taps // 2)):
            for r in range(8):
                chosen = [i for i in range(r, lags, 8)]
                totals = [None] * len(chosen)
                for u in range(groups):
                    for m in range(0, some, 8):
                        value = values[kind, u, m : m + 8, :]
                        for n, i in enumerate(chosen):
                            part = value * cells[kind, u, pl.ds(m + i, 8), :]
                            totals[n] = part if totals[n] is None else totals[n] + part
                for n, i in enumerate(chosen):
                    taken[kind, 8 * i : 8 * i + 8, :] = totals[n]
        sums = []
        for kind in range(3):
            line = taken[kind, pl.ds(0, 16, stride=8), :]
            for k in range(1, 8):
                line = line + taken[kind, pl.ds(k, 16, stride=8), :]
            sums.append(line)
        evens = sums[0] + sums[1]
        odds = sums[2] - pltpu.roll(sums[0], 15, 0) - sums[1]
        square[cb, pl.ds(0, 16, stride=2), :] = evens
        square[cb, pl.ds(1, 16, stride=2), :] = odds
        square[cb, taps : taps + 1, :] = term[:, lane(cb)]
        return 0

    lax.fori_loop(0, blocks, channel, 0)
    quarter = blocks * LANES // 4
    spot = lax.broadcasted_iota(jnp.int32, (32, LANES), 1) // 32
    lines = []
    for g in range(blocks // 4):
        columns[g] = square[4 * g : 4 * g + 4].reshape(LANES, LANES).T
        for b in range(4):
            line = jnp.zeros((32, LANES), F32)
            for m in range(4):
                taken_rows = columns[g, pl.ds(m, 32, stride=4), :]
                line = jnp.where(spot == m, pltpu.roll(taken_rows, 32 * ((m - b) % 4), 1), line)
            lines.append(line)
    total = jnp.concatenate(lines, axis=0)
    rest[8 : 8 + quarter, :] = total
    row = lax.broadcasted_iota(jnp.int32, (8, LANES), 0)
    for p in range(packed.shape[0]):
        upper = rest[6 * p + 8 : 6 * p + 16, :]
        lower = rest[6 * p + 7 : 6 * p + 15, :]
        packed[p] = jnp.where(row < 3, upper, jnp.where((row > 3) & (row < 7), lower, 0.0))


def gradient_kernel(lengths, place, swish, hat, inverse, gain, slab, grad, packed, term, *scratch):
    work, sums, *rest = scratch
    backward_kernel(lengths, place, swish, hat, inverse, gain, grad, term, work, sums)
    terms_kernel(grad, slab, term, packed, *rest)


def input_kernel(lengths, place, grad, hidden, weights, out):
    groups, frames, _ = hidden.shape
    blocks = grad.shape[1]
    taps = weights.shape[0]
    chunk = 64
    for u in range(groups):
        limit = left_of(lengths, place, u, frames)

        def channel(cb, _):
            block = grad.at[u, cb]
            weight = [weights[j : j + 1, lane(cb)] for j in range(taps)]
            for start in range(0, frames, chunk):
                at = slice(start, start + chunk)
                total = depthwise(block, weight, start, chunk, range(taps - 1, -1, -1))
                row = start + lax.broadcasted_iota(jnp.int32, (chunk, LANES), 0)
                total = jnp.where(row < limit, total, 0.0)
                linear = hidden[u, at, lane(cb)].astype(F32)
                gate = sigmoid(hidden[u, at, lane(blocks + cb)].astype(F32))
                opened = total * gate
                out[u, at, lane(cb)] = opened.astype(BF16)
                out[u, at, lane(blocks + cb)] = (opened * linear * (1.0 - gate)).astype(BF16)
            return 0

        lax.fori_loop(0, blocks, channel, 0)


def sum_kernel(factor, got, out, taps_out, gain_out, total, held, arrived):
    own = out.shape[0]
    slots, step = held.shape[:2]

    def copy(i):
        return pltpu.make_async_copy(got.at[pl.ds(i * step, step)], held.at[i], arrived.at[i])

    for i in range(slots):
        copy(i).start()
    total[...] = jnp.zeros_like(total)

    def add(i, _):
        copy(i).wait()
        for k in range(0, step, 4):
            total[...] += jnp.sum(held[i, k : k + 4].astype(F32), axis=0)
        return 0

    lax.fori_loop(0, slots, add, 0)
    tall = total.shape[0] // 2
    blocks = (tall - 4) // own
    for side in range(2):
        for k in range(blocks):
            at = (side * blocks + k) * LANES
            start = tall * side + own * k
            out[:, at : at + LANES] = total[start : start + own, :] * factor
    small = (total[tall - 4 : tall - 1, :] + total[2 * tall - 4 : 2 * tall - 1, :]) * factor
    taps = taps_out.shape[1]
    spot = lax.broadcasted_iota(jnp.int32, (1, LANES), 1)
    gains = jnp.zeros((1, LANES), F32)
    for r in range(3):
        for m in range(4):
            c = 4 * r + m
            turned = pltpu.roll(small[r : r + 1, :], (LANES - 32 * m) % LANES, 1)
            taps_out[c : c + 1, :] = turned[:, :taps]
            gains = jnp.where(spot == c, pltpu.roll(turned, (c - taps) % LANES, 1), gains)
    gain_out[...] = gains[:, :own]


def local(hidden, cotangent, lengths, kernel, conv_gain, w_out):
    groups, frames, double = hidden.shape
    width = double // 2
    half = width // 2
    blocks = width // LANES
    taps = kernel.shape[1]
    seq_count = lax.axis_size("seq")
    devices = lax.axis_size("dp") * seq_count
    own = width // devices
    rows = groups * frames
    span = frames + 2 * HALF_PAD
    length = frames + 2 * PAD
    tall = own * half // LANES + 4
    ends = seq_count - 1
    swap = [(i, i ^ 1) for i in range(seq_count)]
    place = lax.axis_index("seq")
    conv_flops = 2 * taps * rows * width

    spot = place.reshape(1)
    flat = cotangent.reshape(rows, width)
    inner_edge, outer_edge, weights = call(
        edges_kernel,
        [SMEM, HBM, HBM, HBM],
        [shape((groups, PAD + HALF_PAD, width), BF16)] * 2 + [shape((taps, width), F32)],
        [
            pltpu.VMEM((2, groups, PAD, double), BF16),
            pltpu.VMEM((2, groups, HALF_PAD, width), BF16),
            pltpu.SemaphoreType.DMA((2, 2, groups)),
            pltpu.SemaphoreType.DMA,
        ],
        1 << 20,
        4,
    )(spot, far_memory(hidden), far_memory(cotangent), far_memory(kernel.T))
    bridge = [(i, i + 1) for i in range(1, ends, 2)]
    across = lax.ppermute(outer_edge, "seq", bridge + [(j, i) for i, j in bridge])
    inside = lax.ppermute(inner_edge, "seq", swap)
    gain = conv_gain.reshape(1, width)
    slab_shape = shape((groups, blocks, length, LANES), F32)
    wide_shape = shape((rows, width), F32)
    gated, inner, swish = call(
        gate_kernel,
        [SMEM, SMEM] + [VMEM] * 3 + [HBM],
        [slab_shape, wide_shape, wide_shape],
        [
            pltpu.VMEM((width, width), BF16),
            pltpu.SemaphoreType.DMA((blocks // 2,)),
            pltpu.VMEM((groups, 3, 104, LANES), F32),
            pltpu.VMEM((groups, 88, LANES), F32),
            pltpu.VMEM((groups, 160, LANES), F32),
        ],
        conv_flops,
        10,
    )(lengths, spot, hidden, weights, flat, far_memory(w_out))
    slab, hat, inverse, message = call(
        forward_kernel,
        [SMEM, SMEM] + [VMEM] * 7,
        [
            slab_shape,
            wide_shape,
            shape((rows, LANES), F32),
            shape((width + half, rows), BF16),
        ],
        [pltpu.VMEM((rows, LANES), F32)],
        conv_flops,
        4,
        {2: 0, 3: 1},
    )(lengths, spot, gated, inner, inside, across, weights, gain, flat)
    far = lax.ppermute(message, "seq", swap)
    grad, packed = call(
        gradient_kernel,
        [SMEM, SMEM] + [VMEM] * 5,
        [
            shape((groups, blocks, span, LANES), F32),
            shape((devices // 2, 8, LANES), F32),
        ],
        [
            pltpu.VMEM((1, width), F32),
            pltpu.VMEM((rows, width), F32),
            pltpu.VMEM((8, width), F32),
            pltpu.VMEM((blocks, 32, LANES), F32),
            pltpu.VMEM((blocks // 4, LANES, LANES), F32),
            pltpu.VMEM((width // 4 + 16, LANES), F32),
            pltpu.VMEM((3, groups, frames // 2, LANES), F32),
            pltpu.VMEM((3, groups, frames // 2 + 16, LANES), F32),
            pltpu.VMEM((3, 128, LANES), F32),
        ],
        conv_flops,
        10,
    )(lengths, spot, swish, hat, inverse, gain, slab)
    pairs = 32
    steps = devices // (2 * pairs)
    pieces = call(
        product_kernel,
        [SMEM] + [VMEM] * 4,
        pltpu.HBM((devices // 2, 2 * tall, LANES), BF16),
        [
            pltpu.VMEM((pairs, 2 * tall, LANES), F32),
            pltpu.VMEM((steps, pairs, 2 * tall, LANES), BF16),
            pltpu.SemaphoreType.DMA((steps, 4)),
        ],
        4 * rows * width * half,
        10,
        out_specs=HBM,
    )(spot, message, flat, far, packed)
    blocked = pieces.reshape(devices, tall // 4, 4, LANES)
    got = lax.all_to_all(blocked, AXES, 0, 0, tiled=True)
    full = call(
        fringe_kernel,
        [SMEM, SMEM] + [VMEM] * 7,
        shape((groups, blocks, span, LANES), F32),
        [
            pltpu.VMEM((2 * groups * HALF_PAD, width), BF16),
            pltpu.VMEM((2 * groups * HALF_PAD, width), F32),
            pltpu.VMEM((2 * groups * HALF_PAD, width), F32),
        ],
        conv_flops // 6,
        6,
        {2: 0},
    )(lengths, spot, grad, slab, inside, across, weights, gain, w_out)
    grad_hidden = call(
        input_kernel,
        [SMEM, SMEM] + [VMEM] * 3,
        shape((groups, frames, double), BF16),
        [],
        conv_flops,
        4,
    )(lengths, spot, full, hidden, weights)

    factor = 1.0 / math.sqrt(groups * lax.axis_size("dp") * frames * seq_count)
    slots = 8
    grad_w, grad_kernel, grad_gain = call(
        functools.partial(sum_kernel, factor),
        [HBM],
        [shape((own, width), F32), shape((own, taps), F32), shape((1, own), F32)],
        [
            pltpu.VMEM((2 * tall, LANES), F32),
            pltpu.VMEM((slots, devices // 2 // slots, 2 * tall, LANES), BF16),
            pltpu.SemaphoreType.DMA((slots,)),
        ],
        1 << 20,
        6,
    )(far_memory(got.reshape(devices // 2, 2 * tall, LANES)))
    return grad_hidden, grad_w, grad_kernel, grad_gain.reshape(own)


def solution(mesh):
    in_specs = (P("dp", "seq", None), P("dp", "seq", None), P("dp"), P(), P(), P())
    out_specs = (P("dp", "seq", None), P(AXES, None), P(AXES, None), P(AXES))
    return jax.shard_map(local, mesh=mesh, in_specs=in_specs, out_specs=out_specs, check_vma=False)
```
